256 devices in a mesh: chan: 16 (over y, x_hi, core), win: 16 (over z, x_lo).
Axes of the slice: x: 4 (x_hi: 2, x_lo: 2; x = x_hi * 2 + x_lo), y: 4, z: 8, core: 2. Of those that a mesh axis runs over, the one named last changes fastest.
Arguments:
- spectra: bfloat16 [64, 512, 4096], P('win', 'chan'), may hold values from -80 to 80
- quality: int32 [512], P('chan'), may hold values 0 or 1
- source_block: int32 [2], replicated, may hold values from 0 to 63
Outputs:
- correlations: bfloat16 [2, 512, 8, 512], P(None, ('chan', 'win'))
The draws below stay inside these ranges and needn't reach their ends.
All inputs are finite; a program needn't handle non-finite values. No bound on the sum of `quality` on one device may be relied on, other than what follows from the above.
Results may differ from the reference program's by a relative error of at most 0.0045.
Values may be sent and summed in bfloat16 or wider, within the bound.
A program may use at most 192 MiB of HBM per device.

```python
import math
import jax
import jax.numpy as jnp
from jax import lax

F = 2048
L = 512
SRC = 8
STEPS = 2
CHANNELS = 512
WINDOWS = 64


def draw_spectra(key, part):
    first = jax.random.fold_in(key, 0)
    second = jax.random.fold_in(key, 1)
    fourth = jax.random.fold_in(key, 3)
    shape = (WINDOWS, CHANNELS, 2 * F)
    base = jnp.clip(jax.random.normal(first, shape, jnp.float32), -6.0, 6.0)
    scales = jnp.exp(jax.random.uniform(second, (WINDOWS, CHANNELS, 1), jnp.float32, 0.0, math.log(10.0)))
    shaping = jnp.exp(jax.random.uniform(fourth, (1, 1, 2 * F), jnp.float32, -0.5, 0.5))
    return (base * scales * shaping).astype(jnp.bfloat16)


def plant(result, own_key, least, largest):
    index_at = [jax.random.randint(jax.random.fold_in(own_key, axis), (), 0, length) for axis, length in enumerate(result.shape)]
    widest = result.shape.index(max(result.shape))
    beside = index_at[:widest] + [(index_at[widest] + 1) % result.shape[widest]] + index_at[widest + 1:]
    return result.at[tuple(index_at)].set(least).at[tuple(beside)].set(largest)


def setup_inputs(seed: int = 0) -> dict:
    key_of = jax.random.split(jax.random.key(seed), 4)
    return {
        "spectra": draw_spectra(jax.random.fold_in(key_of[3], 71), 0),
        "quality": plant((jax.random.randint(key_of[1], (CHANNELS,), 0, 8) < 7).astype(jnp.int32), jax.random.fold_in(key_of[1], 1), 0, 1),
        "source_block": jax.random.randint(key_of[2], (STEPS,), 0, CHANNELS // SRC).astype(jnp.int32),
    }


def lag_table(bins, lags, factor):
    bin_index = lax.iota(jnp.int32, bins)[:, None]
    shifts = lax.iota(jnp.int32, lags)[None, :] - lags // 2
    residue = jnp.mod(bin_index * shifts, 2 * bins)
    phase_angle = residue.astype(jnp.float32) * (2.0 * math.pi / (2 * bins))
    return jnp.concatenate([jnp.cos(phase_angle), -jnp.sin(phase_angle)], axis=0) * factor

def whiten(block, quality):
    values = block.astype(jnp.float32)
    bins = values.shape[-1] // 2
    energy = lax.optimization_barrier(jnp.sum(values * values, axis=-1)) / bins
    weights = quality.astype(jnp.float32)[None, :] / jnp.sqrt(energy + 1e-06)
    return (values * weights[:, :, None]).astype(jnp.bfloat16)

def cross_spectra(sources, receivers):
    bins = sources.shape[-1] // 2
    src_real = sources[:, :, :bins].astype(jnp.float32)
    src_imag = sources[:, :, bins:].astype(jnp.float32)
    rec_real = receivers[:, :, :bins].astype(jnp.float32)
    rec_imag = receivers[:, :, bins:].astype(jnp.float32)
    real_part = jnp.einsum('wsf,wrf->rsf', src_real, rec_real) + jnp.einsum('wsf,wrf->rsf', src_imag, rec_imag)
    imag_part = jnp.einsum('wsf,wrf->rsf', src_real, rec_imag) - jnp.einsum('wsf,wrf->rsf', src_imag, rec_real)
    return jnp.concatenate([real_part, imag_part], axis=-1)

def reference(spectra, quality, source_block):
    window_count, channel_count, row_width = spectra.shape
    bins = row_width // 2
    transform = lag_table(bins, L, 1.0 / math.sqrt(row_width * window_count))

    def one_window(carry, index):
        block = lax.dynamic_slice_in_dim(spectra, index, 1, 0)
        whitened = whiten(block, quality)
        terms = []
        for step in range(STEPS):
            start = (source_block[step] * SRC).astype(jnp.int32)
            sources = lax.dynamic_slice_in_dim(whitened, start, SRC, 1)
            terms.append(cross_spectra(sources, whitened))
        return (carry + jnp.stack(terms), None)
    empty = jnp.zeros((STEPS, channel_count, SRC, row_width), jnp.float32)
    cross, _ = lax.scan(one_window, empty, jnp.arange(window_count, dtype=jnp.int32))
    lagged = jnp.dot(cross.reshape(-1, row_width), transform, precision=lax.Precision.HIGHEST, preferred_element_type=jnp.float32)
    return lagged.reshape(STEPS, channel_count, SRC, L).astype(jnp.bfloat16)
```

```python
import math

import jax
import jax.numpy as jnp
from jax import lax
from jax.experimental import pallas as pl
from jax.sharding import PartitionSpec as P

L = 512
SRC = 8
STEPS = 2


def from_root(value, axis, source):
    kept = jnp.where(lax.axis_index(axis) == source, value, 0).astype(value.dtype)
    return lax.psum(kept, axis)


def lag_table(bins, lags, factor):
    inner = 64
    period = 2 * bins
    shifts = lax.iota(jnp.int32, lags)[None, :] - lags // 2
    hi = lax.iota(jnp.int32, bins // inner)[:, None] * inner
    lo = lax.iota(jnp.int32, inner)[:, None]
    scale = 2.0 * math.pi / period
    angle_hi = jnp.mod(hi * shifts, period).astype(jnp.float32) * scale
    angle_lo = jnp.mod(lo * shifts, period).astype(jnp.float32) * scale
    cos_hi, sin_hi = jnp.cos(angle_hi)[:, None, :], jnp.sin(angle_hi)[:, None, :]
    cos_lo, sin_lo = jnp.cos(angle_lo)[None, :, :], jnp.sin(angle_lo)[None, :, :]
    cos_t = (cos_hi * cos_lo - sin_hi * sin_lo).reshape(bins, lags)
    sin_t = (sin_hi * cos_lo + cos_hi * sin_lo).reshape(bins, lags)
    return cos_t * factor, -sin_t * factor


def whiten(block, quality):
    values = block.astype(jnp.float32)
    bins = values.shape[-1] // 2
    energy = jnp.sum(values * values, axis=-1) / bins
    weights = quality.astype(jnp.float32)[None, :] / jnp.sqrt(energy + 1e-06)
    return (values * weights[:, :, None]).astype(jnp.bfloat16)


def cross_spectra(sources, receivers):
    bins = sources.shape[-1] // 2
    sr = sources[:, None, :, :bins].astype(jnp.float32)
    si = sources[:, None, :, bins:].astype(jnp.float32)
    rr = receivers[:, :, None, :bins].astype(jnp.float32)
    ri = receivers[:, :, None, bins:].astype(jnp.float32)
    real_part = jnp.sum(sr * rr + si * ri, axis=0)
    imag_part = jnp.sum(sr * ri - si * rr, axis=0)
    return real_part, imag_part


def cast_kernel(x_ref, o_ref):
    o_ref[...] = x_ref[...].astype(o_ref.dtype)


def to_bf16(x):
    return pl.pallas_call(
        cast_kernel, out_shape=jax.ShapeDtypeStruct(x.shape, jnp.bfloat16)
    )(x)


def body(spectra, quality, source_block):
    window_count, channel_count, row_width = spectra.shape
    bins = row_width // 2
    total_windows = window_count * lax.axis_size("win")
    cos_t, sin_t = lag_table(bins, L, 1.0 / math.sqrt(row_width * total_windows))
    whitened = whiten(spectra, quality)
    per_group = channel_count // SRC
    own = []
    roots = []
    for step in range(STEPS):
        block_index = source_block[step]
        offset = block_index % per_group * SRC
        own.append(lax.dynamic_slice_in_dim(whitened, offset, SRC, 1))
        roots.append(block_index // per_group)
    me = lax.axis_index("chan")
    kept = jnp.stack(
        [jnp.where(me == roots[k], own[k], jnp.zeros_like(own[k])) for k in range(STEPS)]
    )
    sources = lax.psum(kept, "chan")
    win_size = lax.axis_size("win")
    per_dest = channel_count // win_size
    reals, imags = [], []
    for step in range(STEPS):
        real_part, imag_part = cross_spectra(sources[step], whitened)
        reals.append(real_part.reshape(win_size, per_dest, SRC, bins))
        imags.append(imag_part.reshape(win_size, per_dest, SRC, bins))
    rows = channel_count * SRC * STEPS
    real_rows = jnp.stack(reals, axis=1).reshape(rows, bins)
    imag_rows = jnp.stack(imags, axis=1).reshape(rows, bins)
    out = jnp.dot(
        real_rows, cos_t, precision=lax.Precision.HIGHEST, preferred_element_type=jnp.float32
    )
    out = out + jnp.dot(
        imag_rows, sin_t, precision=lax.Precision.HIGHEST, preferred_element_type=jnp.float32
    )
    out = out.reshape(win_size, STEPS * per_dest * SRC * L)
    stacked = lax.psum_scatter(out, "win", scatter_dimension=0, tiled=True)
    return to_bf16(stacked.reshape(STEPS * per_dest * SRC, L)).reshape(STEPS, per_dest, SRC, L)


def solution(mesh):
    return jax.shard_map(
        body,
        mesh=mesh,
        in_specs=(P("win", "chan", None), P("chan"), P()),
        out_specs=P(None, ("chan", "win"), None, None),
        check_vma=False,
    )
```

```python
import math

import jax
import jax.numpy as jnp
from jax import lax
from jax.experimental import pallas as pl
from jax.sharding import PartitionSpec as P

L = 512
SRC = 8
STEPS = 2


def from_root(value, axis, source):
    kept = jnp.where(lax.axis_index(axis) == source, value, 0).astype(value.dtype)
    return lax.psum(kept, axis)


def lag_table(bins, lags, factor):
    inner = 64
    period = 2 * bins
    shifts = lax.iota(jnp.int32, lags)[None, :] - lags // 2
    hi = lax.iota(jnp.int32, bins // inner)[:, None] * inner
    lo = lax.iota(jnp.int32, inner)[:, None]
    scale = 2.0 * math.pi / period
    angle_hi = jnp.mod(hi * shifts, period).astype(jnp.float32) * scale
    angle_lo = jnp.mod(lo * shifts, period).astype(jnp.float32) * scale
    cos_hi, sin_hi = jnp.cos(angle_hi)[:, None, :], jnp.sin(angle_hi)[:, None, :]
    cos_lo, sin_lo = jnp.cos(angle_lo)[None, :, :], jnp.sin(angle_lo)[None, :, :]
    cos_t = (cos_hi * cos_lo - sin_hi * sin_lo).reshape(bins, lags)
    sin_t = (sin_hi * cos_lo + cos_hi * sin_lo).reshape(bins, lags)
    return cos_t * factor, -sin_t * factor


def whiten(block, quality):
    values = block.astype(jnp.float32)
    bins = values.shape[-1] // 2
    energy = jnp.sum(values * values, axis=-1) / bins
    weights = quality.astype(jnp.float32)[None, :] / jnp.sqrt(energy + 1e-06)
    return (values * weights[:, :, None]).astype(jnp.bfloat16)


def cross_spectra(sources, receivers):
    bins = sources.shape[-1] // 2
    sr = sources[:, None, :, :bins].astype(jnp.float32)
    si = sources[:, None, :, bins:].astype(jnp.float32)
    rr = receivers[:, :, None, :bins].astype(jnp.float32)
    ri = receivers[:, :, None, bins:].astype(jnp.float32)
    real_part = jnp.sum(sr * rr + si * ri, axis=0)
    imag_part = jnp.sum(sr * ri - si * rr, axis=0)
    return real_part, imag_part


def scatter_sum(rows, axis):
    n = rows.shape[0]
    me = lax.axis_index(axis)
    total = lax.dynamic_index_in_dim(rows, me, 0, keepdims=False).astype(jnp.float32)
    for shift in range(1, n):
        piece = lax.dynamic_index_in_dim(rows, (me + shift) % n, 0, keepdims=False)
        got = lax.ppermute(piece, axis, [(i, (i + shift) % n) for i in range(n)])
        total = total + got.astype(jnp.float32)
    return total.astype(rows.dtype)


def gather_rows(row, axis):
    n = lax.axis_size(axis)
    me = lax.axis_index(axis)
    held = [row]
    for shift in range(1, n):
        held.append(lax.ppermute(row, axis, [(i, (i + shift) % n) for i in range(n)]))
    held = jnp.stack(held)
    order = (me - lax.iota(jnp.int32, n)) % n
    return jnp.take(held, order, axis=0)


def broadcast_sum(value, axis):
    n = lax.axis_size(axis)
    rows = value.reshape(n, -1)
    return gather_rows(scatter_sum(rows, axis), axis).reshape(value.shape)


def cast_kernel(x_ref, o_ref):
    o_ref[...] = x_ref[...].astype(o_ref.dtype)


def to_bf16(x):
    return pl.pallas_call(
        cast_kernel, out_shape=jax.ShapeDtypeStruct(x.shape, jnp.bfloat16)
    )(x)


def body(spectra, quality, source_block):
    window_count, channel_count, row_width = spectra.shape
    bins = row_width // 2
    total_windows = window_count * lax.axis_size("win")
    cos_t, sin_t = lag_table(bins, L, 1.0 / math.sqrt(row_width * total_windows))
    whitened = whiten(spectra, quality)
    per_group = channel_count // SRC
    own = []
    roots = []
    for step in range(STEPS):
        block_index = source_block[step]
        offset = block_index % per_group * SRC
        own.append(lax.dynamic_slice_in_dim(whitened, offset, SRC, 1))
        roots.append(block_index // per_group)
    me = lax.axis_index("chan")
    kept = jnp.stack(
        [jnp.where(me == roots[k], own[k], jnp.zeros_like(own[k])) for k in range(STEPS)]
    )
    sources = broadcast_sum(kept, "chan")
    win_size = lax.axis_size("win")
    per_dest = channel_count // win_size
    reals, imags = [], []
    for step in range(STEPS):
        real_part, imag_part = cross_spectra(sources[step], whitened)
        reals.append(real_part.reshape(win_size, per_dest, SRC, bins))
        imags.append(imag_part.reshape(win_size, per_dest, SRC, bins))
    rows = channel_count * SRC * STEPS
    real_rows = jnp.stack(reals, axis=1).reshape(rows, bins)
    imag_rows = jnp.stack(imags, axis=1).reshape(rows, bins)
    out = jnp.dot(
        real_rows, cos_t, precision=lax.Precision.HIGHEST, preferred_element_type=jnp.float32
    )
    out = out + jnp.dot(
        imag_rows, sin_t, precision=lax.Precision.HIGHEST, preferred_element_type=jnp.float32
    )
    out = out.reshape(win_size, STEPS * per_dest * SRC * L)
    stacked = scatter_sum(out, "win")
    return to_bf16(stacked.reshape(STEPS * per_dest * SRC, L)).reshape(STEPS, per_dest, SRC, L)


def solution(mesh):
    return jax.shard_map(
        body,
        mesh=mesh,
        in_specs=(P("win", "chan", None), P("chan"), P()),
        out_specs=P(None, ("chan", "win"), None, None),
        check_vma=False,
    )
```

```python
import functools
import math

import jax
import jax.numpy as jnp
from jax import lax
from jax.experimental import pallas as pl
from jax.experimental.pallas import tpu as pltpu
from jax.sharding import PartitionSpec as P

L = 512
SRC = 8
STEPS = 2


def from_root(value, axis, source):
    kept = jnp.where(lax.axis_index(axis) == source, value, 0).astype(value.dtype)
    return lax.psum(kept, axis)


def lag_table(bins, lags, factor):
    inner = 64
    period = 2 * bins
    shifts = lax.iota(jnp.int32, lags)[None, :] - lags // 2
    hi = lax.iota(jnp.int32, bins // inner)[:, None] * inner
    lo = lax.iota(jnp.int32, inner)[:, None]
    scale = 2.0 * math.pi / period
    angle_hi = jnp.mod(hi * shifts, period).astype(jnp.float32) * scale
    angle_lo = jnp.mod(lo * shifts, period).astype(jnp.float32) * scale
    cos_hi, sin_hi = jnp.cos(angle_hi)[:, None, :], jnp.sin(angle_hi)[:, None, :]
    cos_lo, sin_lo = jnp.cos(angle_lo)[None, :, :], jnp.sin(angle_lo)[None, :, :]
    cos_t = (cos_hi * cos_lo - sin_hi * sin_lo).reshape(bins, lags)
    sin_t = (sin_hi * cos_lo + cos_hi * sin_lo).reshape(bins, lags)
    return cos_t * factor, -sin_t * factor


def whiten(block, quality):
    values = block.astype(jnp.float32)
    bins = values.shape[-1] // 2
    energy = jnp.sum(values * values, axis=-1) / bins
    weights = quality.astype(jnp.float32)[None, :] / jnp.sqrt(energy + 1e-06)
    return (values * weights[:, :, None]).astype(jnp.bfloat16)


def cross_spectra(sources, receivers):
    bins = sources.shape[-1] // 2
    sr = sources[:, None, :, :bins].astype(jnp.float32)
    si = sources[:, None, :, bins:].astype(jnp.float32)
    rr = receivers[:, :, None, :bins].astype(jnp.float32)
    ri = receivers[:, :, None, bins:].astype(jnp.float32)
    real_part = jnp.sum(sr * rr + si * ri, axis=0)
    imag_part = jnp.sum(sr * ri - si * rr, axis=0)
    return real_part, imag_part


def exchange_kernel(axis, n, single, x_ref, o_ref, buf, send_sem, recv_sem):
    me = lax.axis_index(axis)
    own = x_ref.at[0] if single else x_ref.at[me]
    buf[me] = own[...]
    barrier = pltpu.get_barrier_semaphore()
    for k in range(1, n):
        pl.semaphore_signal(barrier, inc=1, device_id={axis: (me + k) % n},
                            device_id_type=pl.DeviceIdType.MESH)
    pl.semaphore_wait(barrier, n - 1)
    copies = []
    for k in range(1, n):
        peer = (me + k) % n
        src = x_ref.at[0] if single else x_ref.at[peer]
        copy = pltpu.make_async_remote_copy(
            src_ref=src, dst_ref=buf.at[me], send_sem=send_sem.at[k],
            recv_sem=recv_sem.at[me], device_id={axis: peer},
            device_id_type=pl.DeviceIdType.MESH)
        copy.start()
        copies.append(copy)
    for copy in copies:
        copy.wait_send()
    for k in range(1, n):
        source = (me + n - k) % n
        pltpu.make_async_remote_copy(
            src_ref=buf.at[source], dst_ref=buf.at[source], send_sem=send_sem.at[k],
            recv_sem=recv_sem.at[source], device_id={axis: source},
            device_id_type=pl.DeviceIdType.MESH).wait_recv()
    o_ref[...] = buf[...]


def exchange(x, axis, n, cid):
    single = x.shape[0] == 1
    shape = (n,) + x.shape[1:]
    return pl.pallas_call(
        functools.partial(exchange_kernel, axis, n, single),
        out_shape=jax.ShapeDtypeStruct(shape, x.dtype),
        in_specs=[pl.BlockSpec(memory_space=pltpu.VMEM)],
        out_specs=pl.BlockSpec(memory_space=pltpu.VMEM),
        scratch_shapes=[pltpu.VMEM(shape, x.dtype), pltpu.SemaphoreType.DMA((n,)),
                        pltpu.SemaphoreType.DMA((n,))],
        compiler_params=pltpu.CompilerParams(collective_id=cid, has_side_effects=True),
    )(x)


def chunks(value, n):
    return value.reshape(n, 16, -1)


def broadcast_sum(value, axis):
    n = lax.axis_size(axis)
    mine = jnp.sum(exchange(chunks(value, n), axis, n, 0), axis=0, dtype=jnp.float32)
    gathered = exchange(mine.astype(value.dtype)[None], axis, n, 1)
    return gathered.reshape(value.shape)


def scatter_sum(rows, axis):
    n = rows.shape[0]
    got = exchange(chunks(rows, n), axis, n, 2)
    return jnp.sum(got, axis=0).reshape(rows.shape[1:])


def cast_kernel(x_ref, o_ref):
    o_ref[...] = x_ref[...].astype(o_ref.dtype)


def to_bf16(x):
    return pl.pallas_call(
        cast_kernel, out_shape=jax.ShapeDtypeStruct(x.shape, jnp.bfloat16)
    )(x)


def body(spectra, quality, source_block):
    window_count, channel_count, row_width = spectra.shape
    bins = row_width // 2
    total_windows = window_count * lax.axis_size("win")
    cos_t, sin_t = lag_table(bins, L, 1.0 / math.sqrt(row_width * total_windows))
    whitened = whiten(spectra, quality)
    per_group = channel_count // SRC
    own = []
    roots = []
    for step in range(STEPS):
        block_index = source_block[step]
        offset = block_index % per_group * SRC
        own.append(lax.dynamic_slice_in_dim(whitened, offset, SRC, 1))
        roots.append(block_index // per_group)
    me = lax.axis_index("chan")
    kept = jnp.stack(
        [jnp.where(me == roots[k], own[k], jnp.zeros_like(own[k])) for k in range(STEPS)]
    )
    sources = broadcast_sum(kept, "chan")
    win_size = lax.axis_size("win")
    per_dest = channel_count // win_size
    reals, imags = [], []
    for step in range(STEPS):
        real_part, imag_part = cross_spectra(sources[step], whitened)
        reals.append(real_part.reshape(win_size, per_dest, SRC, bins))
        imags.append(imag_part.reshape(win_size, per_dest, SRC, bins))
    rows = channel_count * SRC * STEPS
    real_rows = jnp.stack(reals, axis=1).reshape(rows, bins)
    imag_rows = jnp.stack(imags, axis=1).reshape(rows, bins)
    out = jnp.dot(
        real_rows, cos_t, precision=lax.Precision.HIGHEST, preferred_element_type=jnp.float32
    )
    out = out + jnp.dot(
        imag_rows, sin_t, precision=lax.Precision.HIGHEST, preferred_element_type=jnp.float32
    )
    out = out.reshape(win_size, STEPS * per_dest * SRC * L)
    stacked = scatter_sum(out, "win")
    return to_bf16(stacked.reshape(STEPS * per_dest * SRC, L)).reshape(STEPS, per_dest, SRC, L)


def solution(mesh):
    return jax.shard_map(
        body,
        mesh=mesh,
        in_specs=(P("win", "chan", None), P("chan"), P()),
        out_specs=P(None, ("chan", "win"), None, None),
        check_vma=False,
    )
```

```python
import functools
import math

import jax
import jax.numpy as jnp
from jax import lax
from jax.experimental import pallas as pl
from jax.experimental.pallas import tpu as pltpu
from jax.sharding import PartitionSpec as P

L = 512
SRC = 8
STEPS = 2


def from_root(value, axis, source):
    kept = jnp.where(lax.axis_index(axis) == source, value, 0).astype(value.dtype)
    return lax.psum(kept, axis)


def lag_table(bins, lags, factor):
    inner = 64
    period = 2 * bins
    shifts = lax.iota(jnp.int32, lags)[None, :] - lags // 2
    hi = lax.iota(jnp.int32, bins // inner)[:, None] * inner
    lo = lax.iota(jnp.int32, inner)[:, None]
    scale = 2.0 * math.pi / period
    angle_hi = jnp.mod(hi * shifts, period).astype(jnp.float32) * scale
    angle_lo = jnp.mod(lo * shifts, period).astype(jnp.float32) * scale
    cos_hi, sin_hi = jnp.cos(angle_hi)[:, None, :], jnp.sin(angle_hi)[:, None, :]
    cos_lo, sin_lo = jnp.cos(angle_lo)[None, :, :], jnp.sin(angle_lo)[None, :, :]
    cos_t = (cos_hi * cos_lo - sin_hi * sin_lo).reshape(bins, lags)
    sin_t = (sin_hi * cos_lo + cos_hi * sin_lo).reshape(bins, lags)
    return cos_t * factor, -sin_t * factor


def whiten(block, quality):
    values = block.astype(jnp.float32)
    bins = values.shape[-1] // 2
    energy = jnp.sum(values * values, axis=-1) / bins
    weights = quality.astype(jnp.float32)[None, :] / jnp.sqrt(energy + 1e-06)
    return (values * weights[:, :, None]).astype(jnp.bfloat16)


def cross_spectra(sources, receivers):
    bins = sources.shape[-1] // 2
    sr = sources[:, None, :, :bins].astype(jnp.float32)
    si = sources[:, None, :, bins:].astype(jnp.float32)
    rr = receivers[:, :, None, :bins].astype(jnp.float32)
    ri = receivers[:, :, None, bins:].astype(jnp.float32)
    real_part = jnp.sum(sr * rr + si * ri, axis=0)
    imag_part = jnp.sum(sr * ri - si * rr, axis=0)
    return real_part, imag_part


def exchange_kernel(axis, n, single, x_ref, o_ref, buf, send_sem, recv_sem):
    me = lax.axis_index(axis)
    own = x_ref.at[0] if single else x_ref.at[me]
    buf[me] = own[...]
    barrier = pltpu.get_barrier_semaphore()
    for k in range(1, n):
        pl.semaphore_signal(barrier, inc=1, device_id={axis: (me + k) % n},
                            device_id_type=pl.DeviceIdType.MESH)
    pl.semaphore_wait(barrier, n - 1)
    copies = []
    for k in range(1, n):
        peer = (me + k) % n
        src = x_ref.at[0] if single else x_ref.at[peer]
        copy = pltpu.make_async_remote_copy(
            src_ref=src, dst_ref=buf.at[me], send_sem=send_sem.at[k],
            recv_sem=recv_sem.at[me], device_id={axis: peer},
            device_id_type=pl.DeviceIdType.MESH)
        copy.start()
        copies.append(copy)
    for copy in copies:
        copy.wait_send()
    for k in range(1, n):
        source = (me + n - k) % n
        pltpu.make_async_remote_copy(
            src_ref=buf.at[source], dst_ref=buf.at[source], send_sem=send_sem.at[k],
            recv_sem=recv_sem.at[source], device_id={axis: source},
            device_id_type=pl.DeviceIdType.MESH).wait_recv()
    o_ref[...] = buf[...]


def exchange(x, axis, n, cid):
    single = x.shape[0] == 1
    shape = (n,) + x.shape[1:]
    return pl.pallas_call(
        functools.partial(exchange_kernel, axis, n, single),
        out_shape=jax.ShapeDtypeStruct(shape, x.dtype),
        in_specs=[pl.BlockSpec(memory_space=pltpu.VMEM)],
        out_specs=pl.BlockSpec(memory_space=pltpu.VMEM),
        scratch_shapes=[pltpu.VMEM(shape, x.dtype), pltpu.SemaphoreType.DMA((n,)),
                        pltpu.SemaphoreType.DMA((n,))],
        compiler_params=pltpu.CompilerParams(collective_id=cid, has_side_effects=True),
    )(x)


def chunks(value, n):
    return value.reshape(n, 16, -1)


def broadcast_sum(value, axis):
    n = lax.axis_size(axis)
    mine = jnp.sum(exchange(chunks(value, n), axis, n, 0), axis=0, dtype=jnp.float32)
    gathered = exchange(mine.astype(value.dtype)[None], axis, n, 1)
    return gathered.reshape(value.shape)


def scatter_sum(rows, axis):
    n = rows.shape[0]
    got = exchange(chunks(rows, n), axis, n, 2)
    return jnp.sum(got, axis=0).reshape(rows.shape[1:])


def cast_kernel(x_ref, o_ref):
    o_ref[...] = x_ref[...].astype(o_ref.dtype)


def to_bf16(x):
    return pl.pallas_call(
        cast_kernel, out_shape=jax.ShapeDtypeStruct(x.shape, jnp.bfloat16)
    )(x)


def body(spectra, quality, source_block):
    window_count, channel_count, row_width = spectra.shape
    bins = row_width // 2
    total_windows = window_count * lax.axis_size("win")
    cos_t, sin_t = lag_table(bins, L, 1.0 / math.sqrt(row_width * total_windows))
    whitened = whiten(spectra, quality)
    per_group = channel_count // SRC
    own = []
    roots = []
    for step in range(STEPS):
        block_index = source_block[step]
        offset = block_index % per_group * SRC
        own.append(lax.dynamic_slice_in_dim(whitened, offset, SRC, 1))
        roots.append(block_index // per_group)
    me = lax.axis_index("chan")
    kept = jnp.stack(
        [jnp.where(me == roots[k], own[k], jnp.zeros_like(own[k])) for k in range(STEPS)]
    )
    sources = broadcast_sum(kept, "chan")
    win_size = lax.axis_size("win")
    per_dest = channel_count // win_size
    reals, imags = [], []
    for step in range(STEPS):
        real_part, imag_part = cross_spectra(sources[step], whitened)
        reals.append(real_part.reshape(win_size, per_dest, SRC, bins))
        imags.append(imag_part.reshape(win_size, per_dest, SRC, bins))
    rows = channel_count * SRC * STEPS
    real_rows = jnp.stack(reals, axis=1).reshape(rows, bins)
    imag_rows = jnp.stack(imags, axis=1).reshape(rows, bins)
    out = jnp.dot(
        real_rows, cos_t, precision=lax.Precision.HIGH, preferred_element_type=jnp.float32
    )
    out = out + jnp.dot(
        imag_rows, sin_t, precision=lax.Precision.HIGH, preferred_element_type=jnp.float32
    )
    out = out.reshape(win_size, STEPS * per_dest * SRC * L)
    stacked = scatter_sum(out, "win")
    return to_bf16(stacked.reshape(STEPS * per_dest * SRC, L)).reshape(STEPS, per_dest, SRC, L)


def solution(mesh):
    return jax.shard_map(
        body,
        mesh=mesh,
        in_specs=(P("win", "chan", None), P("chan"), P()),
        out_specs=P(None, ("chan", "win"), None, None),
        check_vma=False,
    )
```

```python
import functools
import math

import jax
import jax.numpy as jnp
from jax import lax
from jax.experimental import pallas as pl
from jax.experimental.pallas import tpu as pltpu
from jax.sharding import PartitionSpec as P

L = 512
SRC = 8
STEPS = 2


def from_root(value, axis, source):
    kept = jnp.where(lax.axis_index(axis) == source, value, 0).astype(value.dtype)
    return lax.psum(kept, axis)


def lag_table(bins, lags, factor):
    inner = 64
    period = 2 * bins
    shifts = lax.iota(jnp.int32, lags)[None, :] - lags // 2
    hi = lax.iota(jnp.int32, bins // inner)[:, None] * inner
    lo = lax.iota(jnp.int32, inner)[:, None]
    scale = 2.0 * math.pi / period
    angle_hi = jnp.mod(hi * shifts, period).astype(jnp.float32) * scale
    angle_lo = jnp.mod(lo * shifts, period).astype(jnp.float32) * scale
    cos_hi, sin_hi = jnp.cos(angle_hi)[:, None, :], jnp.sin(angle_hi)[:, None, :]
    cos_lo, sin_lo = jnp.cos(angle_lo)[None, :, :], jnp.sin(angle_lo)[None, :, :]
    cos_t = (cos_hi * cos_lo - sin_hi * sin_lo).reshape(bins, lags)
    sin_t = (sin_hi * cos_lo + cos_hi * sin_lo).reshape(bins, lags)
    return cos_t * factor, -sin_t * factor


def whiten(block, quality):
    values = block.astype(jnp.float32)
    bins = values.shape[-1] // 2
    energy = jnp.sum(values * values, axis=-1) / bins
    weights = quality.astype(jnp.float32)[None, :] / jnp.sqrt(energy + 1e-06)
    return (values * weights[:, :, None]).astype(jnp.bfloat16)


def cross_spectra(sources, receivers):
    bins = sources.shape[-1] // 2
    sr = sources[:, None, :, :bins].astype(jnp.float32)
    si = sources[:, None, :, bins:].astype(jnp.float32)
    rr = receivers[:, :, None, :bins].astype(jnp.float32)
    ri = receivers[:, :, None, bins:].astype(jnp.float32)
    real_part = jnp.sum(sr * rr + si * ri, axis=0)
    imag_part = jnp.sum(sr * ri - si * rr, axis=0)
    return real_part, imag_part


def greet(axis, n, me):
    barrier = pltpu.get_barrier_semaphore()
    for k in range(1, n):
        pl.semaphore_signal(barrier, inc=1, device_id={axis: (me + k) % n},
                            device_id_type=pl.DeviceIdType.MESH)
    pl.semaphore_wait(barrier, n - 1)


def all_to_all(axis, n, me, rows_of, landing, send_sem, recv_sem):
    copies = []
    for k in range(1, n):
        peer = (me + k) % n
        copy = pltpu.make_async_remote_copy(
            src_ref=rows_of(peer), dst_ref=landing.at[me], send_sem=send_sem.at[k],
            recv_sem=recv_sem.at[me], device_id={axis: peer},
            device_id_type=pl.DeviceIdType.MESH)
        copy.start()
        copies.append(copy)
    for copy in copies:
        copy.wait_send()
    for k in range(1, n):
        source = (me + n - k) % n
        pltpu.make_async_remote_copy(
            src_ref=landing.at[source], dst_ref=landing.at[source], send_sem=send_sem.at[k],
            recv_sem=recv_sem.at[source], device_id={axis: source},
            device_id_type=pl.DeviceIdType.MESH).wait_recv()


def broadcast_kernel(axis, n, x_ref, o_ref, parts, mine, gathered, sems):
    me = lax.axis_index(axis)
    parts[me] = x_ref[me]
    greet(axis, n, me)
    all_to_all(axis, n, me, lambda peer: x_ref.at[peer], parts, sems.at[0], sems.at[1])
    mine[...] = jnp.sum(parts[...].astype(jnp.float32), axis=0).astype(mine.dtype)
    gathered[me] = mine[...]
    all_to_all(axis, n, me, lambda peer: mine, gathered, sems.at[2], sems.at[3])
    o_ref[...] = gathered[...]


def reduce_kernel(axis, n, x_ref, o_ref, parts, sems):
    me = lax.axis_index(axis)
    parts[me] = x_ref[me]
    greet(axis, n, me)
    all_to_all(axis, n, me, lambda peer: x_ref.at[peer], parts, sems.at[0], sems.at[1])
    o_ref[...] = jnp.sum(parts[...], axis=0).astype(o_ref.dtype)


def chunks(value, n):
    return value.reshape(n, 16, -1)


def broadcast_sum(value, axis):
    n = lax.axis_size(axis)
    x = chunks(value, n)
    out = pl.pallas_call(
        functools.partial(broadcast_kernel, axis, n),
        out_shape=jax.ShapeDtypeStruct(x.shape, x.dtype),
        in_specs=[pl.BlockSpec(memory_space=pltpu.VMEM)],
        out_specs=pl.BlockSpec(memory_space=pltpu.VMEM),
        scratch_shapes=[pltpu.VMEM(x.shape, x.dtype), pltpu.VMEM(x.shape[1:], x.dtype),
                        pltpu.VMEM(x.shape, x.dtype), pltpu.SemaphoreType.DMA((4, n))],
        compiler_params=pltpu.CompilerParams(collective_id=0, has_side_effects=True),
    )(x)
    return out.reshape(value.shape)


def scatter_sum(rows, axis, dtype):
    n = rows.shape[0]
    x = chunks(rows, n)
    out = pl.pallas_call(
        functools.partial(reduce_kernel, axis, n),
        out_shape=jax.ShapeDtypeStruct(x.shape[1:], dtype),
        in_specs=[pl.BlockSpec(memory_space=pltpu.VMEM)],
        out_specs=pl.BlockSpec(memory_space=pltpu.VMEM),
        scratch_shapes=[pltpu.VMEM(x.shape, x.dtype), pltpu.SemaphoreType.DMA((2, n))],
        compiler_params=pltpu.CompilerParams(collective_id=1, has_side_effects=True),
    )(x)
    return out.reshape(rows.shape[1:])


def body(spectra, quality, source_block):
    window_count, channel_count, row_width = spectra.shape
    bins = row_width // 2
    total_windows = window_count * lax.axis_size("win")
    cos_t, sin_t = lag_table(bins, L, 1.0 / math.sqrt(row_width * total_windows))
    whitened = whiten(spectra, quality)
    per_group = channel_count // SRC
    own = []
    roots = []
    for step in range(STEPS):
        block_index = source_block[step]
        offset = block_index % per_group * SRC
        own.append(lax.dynamic_slice_in_dim(whitened, offset, SRC, 1))
        roots.append(block_index // per_group)
    me = lax.axis_index("chan")
    kept = jnp.stack(
        [jnp.where(me == roots[k], own[k], jnp.zeros_like(own[k])) for k in range(STEPS)]
    )
    sources = broadcast_sum(kept, "chan")
    win_size = lax.axis_size("win")
    per_dest = channel_count // win_size
    reals, imags = [], []
    for step in range(STEPS):
        real_part, imag_part = cross_spectra(sources[step], whitened)
        reals.append(real_part.reshape(win_size, per_dest, SRC, bins))
        imags.append(imag_part.reshape(win_size, per_dest, SRC, bins))
    rows = channel_count * SRC * STEPS
    real_rows = jnp.stack(reals, axis=1).reshape(rows, bins)
    imag_rows = jnp.stack(imags, axis=1).reshape(rows, bins)
    out = jnp.dot(
        real_rows, cos_t, precision=lax.Precision.HIGH, preferred_element_type=jnp.float32
    )
    out = out + jnp.dot(
        imag_rows, sin_t, precision=lax.Precision.HIGH, preferred_element_type=jnp.float32
    )
    out = out.reshape(win_size, STEPS * per_dest * SRC * L)
    stacked = scatter_sum(out, "win", jnp.bfloat16)
    return stacked.reshape(STEPS, per_dest, SRC, L)


def solution(mesh):
    return jax.shard_map(
        body,
        mesh=mesh,
        in_specs=(P("win", "chan", None), P("chan"), P()),
        out_specs=P(None, ("chan", "win"), None, None),
        check_vma=False,
    )
```

```python
import functools
import math

import jax
import jax.numpy as jnp
from jax import lax
from jax.experimental import pallas as pl
from jax.experimental.pallas import tpu as pltpu
from jax.sharding import PartitionSpec as P

L = 512
SRC = 8
STEPS = 2


def from_root(value, axis, source):
    kept = jnp.where(lax.axis_index(axis) == source, value, 0).astype(value.dtype)
    return lax.psum(kept, axis)


def lag_table(bins, lags, factor):
    inner = 64
    period = 2 * bins
    shifts = lax.iota(jnp.int32, lags)[None, :] - lags // 2
    hi = lax.iota(jnp.int32, bins // inner)[:, None] * inner
    lo = lax.iota(jnp.int32, inner)[:, None]
    scale = 2.0 * math.pi / period
    angle_hi = jnp.mod(hi * shifts, period).astype(jnp.float32) * scale
    angle_lo = jnp.mod(lo * shifts, period).astype(jnp.float32) * scale
    cos_hi, sin_hi = jnp.cos(angle_hi)[:, None, :], jnp.sin(angle_hi)[:, None, :]
    cos_lo, sin_lo = jnp.cos(angle_lo)[None, :, :], jnp.sin(angle_lo)[None, :, :]
    cos_t = (cos_hi * cos_lo - sin_hi * sin_lo).reshape(bins, lags)
    sin_t = (sin_hi * cos_lo + cos_hi * sin_lo).reshape(bins, lags)
    return cos_t * factor, -sin_t * factor


def whiten(block, quality):
    values = block.astype(jnp.float32)
    bins = values.shape[-1] // 2
    energy = jnp.sum(values * values, axis=-1) / bins
    weights = quality.astype(jnp.float32)[None, :] / jnp.sqrt(energy + 1e-06)
    return (values * weights[:, :, None]).astype(jnp.bfloat16)


def cross_spectra(sources, receivers):
    bins = sources.shape[-1] // 2
    sr = sources[:, None, :, :bins].astype(jnp.float32)
    si = sources[:, None, :, bins:].astype(jnp.float32)
    rr = receivers[:, :, None, :bins].astype(jnp.float32)
    ri = receivers[:, :, None, bins:].astype(jnp.float32)
    real_part = jnp.sum(sr * rr + si * ri, axis=0)
    imag_part = jnp.sum(sr * ri - si * rr, axis=0)
    return real_part, imag_part


def greet(axis, n, me):
    barrier = pltpu.get_barrier_semaphore()
    for k in range(1, n):
        pl.semaphore_signal(barrier, inc=1, device_id={axis: (me + k) % n},
                            device_id_type=pl.DeviceIdType.MESH)
    pl.semaphore_wait(barrier, n - 1)


def all_to_all(axis, n, me, rows_of, landing, send_sem, recv_sem):
    copies = []
    for k in range(1, n):
        peer = (me + k) % n
        copy = pltpu.make_async_remote_copy(
            src_ref=rows_of(peer), dst_ref=landing.at[me], send_sem=send_sem.at[k],
            recv_sem=recv_sem.at[me], device_id={axis: peer},
            device_id_type=pl.DeviceIdType.MESH)
        copy.start()
        copies.append(copy)
    for copy in copies:
        copy.wait_send()
    for k in range(1, n):
        source = (me + n - k) % n
        pltpu.make_async_remote_copy(
            src_ref=landing.at[source], dst_ref=landing.at[source], send_sem=send_sem.at[k],
            recv_sem=recv_sem.at[source], device_id={axis: source},
            device_id_type=pl.DeviceIdType.MESH).wait_recv()


def broadcast_kernel(axis, n, x_ref, o_ref, parts, mine, gathered, sems):
    me = lax.axis_index(axis)
    parts[me] = x_ref[me]
    greet(axis, n, me)
    all_to_all(axis, n, me, lambda peer: x_ref.at[peer], parts, sems.at[0], sems.at[1])
    mine[...] = jnp.sum(parts[...].astype(jnp.float32), axis=0).astype(mine.dtype)
    gathered[me] = mine[...]
    all_to_all(axis, n, me, lambda peer: mine, gathered, sems.at[2], sems.at[3])
    o_ref[...] = gathered[...]


def reduce_kernel(axis, n, x_ref, o_ref, parts, sems):
    me = lax.axis_index(axis)
    parts[me] = x_ref[me]
    greet(axis, n, me)
    all_to_all(axis, n, me, lambda peer: x_ref.at[peer], parts, sems.at[0], sems.at[1])
    o_ref[...] = jnp.sum(parts[...], axis=0).astype(o_ref.dtype)


def chunks(value, n):
    return value.reshape(n, 16, -1)


def broadcast_sum(value, axis):
    n = lax.axis_size(axis)
    x = chunks(value, n)
    out = pl.pallas_call(
        functools.partial(broadcast_kernel, axis, n),
        out_shape=jax.ShapeDtypeStruct(x.shape, x.dtype),
        in_specs=[pl.BlockSpec(memory_space=pltpu.VMEM)],
        out_specs=pl.BlockSpec(memory_space=pltpu.VMEM),
        scratch_shapes=[pltpu.VMEM(x.shape, x.dtype), pltpu.VMEM(x.shape[1:], x.dtype),
                        pltpu.VMEM(x.shape, x.dtype), pltpu.SemaphoreType.DMA((4, n))],
        compiler_params=pltpu.CompilerParams(collective_id=0, has_side_effects=True),
    )(x)
    return out.reshape(value.shape)


def scatter_sum(rows, axis, dtype):
    n = rows.shape[0]
    x = chunks(rows, n)
    out = pl.pallas_call(
        functools.partial(reduce_kernel, axis, n),
        out_shape=jax.ShapeDtypeStruct(x.shape[1:], dtype),
        in_specs=[pl.BlockSpec(memory_space=pltpu.VMEM)],
        out_specs=pl.BlockSpec(memory_space=pltpu.VMEM),
        scratch_shapes=[pltpu.VMEM(x.shape, x.dtype), pltpu.SemaphoreType.DMA((2, n))],
        compiler_params=pltpu.CompilerParams(collective_id=1, has_side_effects=True),
    )(x)
    return out.reshape(rows.shape[1:])


def body(spectra, quality, source_block):
    window_count, channel_count, row_width = spectra.shape
    bins = row_width // 2
    total_windows = window_count * lax.axis_size("win")
    cos_t, sin_t = lag_table(bins, L, 1.0 / math.sqrt(row_width * total_windows))
    whitened = whiten(spectra, quality)
    per_group = channel_count // SRC
    me = lax.axis_index("chan")
    block_ids = me * per_group + lax.iota(jnp.int32, per_group)
    chosen = block_ids[None, :] == source_block[:, None]
    blocks = whitened.reshape(window_count, per_group, SRC, row_width)
    kept = jnp.sum(
        jnp.where(chosen[:, None, :, None, None], blocks[None], jnp.zeros((), blocks.dtype)),
        axis=2, dtype=jnp.float32,
    ).astype(jnp.bfloat16)
    sources = broadcast_sum(kept, "chan")
    win_size = lax.axis_size("win")
    per_dest = channel_count // win_size
    reals, imags = [], []
    for step in range(STEPS):
        real_part, imag_part = cross_spectra(sources[step], whitened)
        reals.append(real_part.reshape(win_size, per_dest, SRC, bins))
        imags.append(imag_part.reshape(win_size, per_dest, SRC, bins))
    rows = channel_count * SRC * STEPS
    real_rows = jnp.stack(reals, axis=1).reshape(rows, bins)
    imag_rows = jnp.stack(imags, axis=1).reshape(rows, bins)
    out = jnp.dot(
        real_rows, cos_t, precision=lax.Precision.HIGH, preferred_element_type=jnp.float32
    )
    out = out + jnp.dot(
        imag_rows, sin_t, precision=lax.Precision.HIGH, preferred_element_type=jnp.float32
    )
    out = out.reshape(win_size, STEPS * per_dest * SRC * L)
    stacked = scatter_sum(out, "win", jnp.bfloat16)
    return stacked.reshape(STEPS, per_dest, SRC, L)


def solution(mesh):
    return jax.shard_map(
        body,
        mesh=mesh,
        in_specs=(P("win", "chan", None), P("chan"), P()),
        out_specs=P(None, ("chan", "win"), None, None),
        check_vma=False,
    )
```

```python
import functools
import math

import jax
import jax.numpy as jnp
from jax import lax
from jax.experimental import pallas as pl
from jax.experimental.pallas import tpu as pltpu
from jax.sharding import PartitionSpec as P

L = 512
SRC = 8
STEPS = 2


def from_root(value, axis, source):
    kept = jnp.where(lax.axis_index(axis) == source, value, 0).astype(value.dtype)
    return lax.psum(kept, axis)


def lag_table(bins, lags, factor):
    inner = 64
    period = 2 * bins
    shifts = lax.iota(jnp.int32, lags)[None, :] - lags // 2
    hi = lax.iota(jnp.int32, bins // inner)[:, None] * inner
    lo = lax.iota(jnp.int32, inner)[:, None]
    scale = 2.0 * math.pi / period
    angle_hi = jnp.mod(hi * shifts, period).astype(jnp.float32) * scale
    angle_lo = jnp.mod(lo * shifts, period).astype(jnp.float32) * scale
    cos_hi, sin_hi = jnp.cos(angle_hi)[:, None, :], jnp.sin(angle_hi)[:, None, :]
    cos_lo, sin_lo = jnp.cos(angle_lo)[None, :, :], jnp.sin(angle_lo)[None, :, :]
    cos_t = (cos_hi * cos_lo - sin_hi * sin_lo).reshape(bins, lags)
    sin_t = (sin_hi * cos_lo + cos_hi * sin_lo).reshape(bins, lags)
    return cos_t * factor, -sin_t * factor


def whiten(block, quality):
    values = block.astype(jnp.float32)
    bins = values.shape[-1] // 2
    energy = jnp.sum(values * values, axis=-1) / bins
    weights = quality.astype(jnp.float32)[None, :] / jnp.sqrt(energy + 1e-06)
    return (values * weights[:, :, None]).astype(jnp.bfloat16)


def cross_spectra(sources, receivers):
    bins = sources.shape[-1] // 2
    sr = sources[:, None, :, :bins].astype(jnp.float32)
    si = sources[:, None, :, bins:].astype(jnp.float32)
    rr = receivers[:, :, None, :bins].astype(jnp.float32)
    ri = receivers[:, :, None, bins:].astype(jnp.float32)
    real_part = jnp.sum(sr * rr + si * ri, axis=0)
    imag_part = jnp.sum(sr * ri - si * rr, axis=0)
    return real_part, imag_part


def greet(axis, n, me):
    barrier = pltpu.get_barrier_semaphore()
    for k in range(1, n):
        pl.semaphore_signal(barrier, inc=1, device_id={axis: (me + k) % n},
                            device_id_type=pl.DeviceIdType.MESH)
    pl.semaphore_wait(barrier, n - 1)


def all_to_all(axis, n, me, rows_of, landing, send_sem, recv_sem):
    copies = []
    for k in range(1, n):
        peer = (me + k) % n
        copy = pltpu.make_async_remote_copy(
            src_ref=rows_of(peer), dst_ref=landing.at[me], send_sem=send_sem.at[k],
            recv_sem=recv_sem.at[me], device_id={axis: peer},
            device_id_type=pl.DeviceIdType.MESH)
        copy.start()
        copies.append(copy)
    for copy in copies:
        copy.wait_send()
    for k in range(1, n):
        source = (me + n - k) % n
        pltpu.make_async_remote_copy(
            src_ref=landing.at[source], dst_ref=landing.at[source], send_sem=send_sem.at[k],
            recv_sem=recv_sem.at[source], device_id={axis: source},
            device_id_type=pl.DeviceIdType.MESH).wait_recv()


def broadcast_kernel(axis, n, x_ref, o_ref, parts, mine, gathered, sems):
    me = lax.axis_index(axis)
    width = x_ref.shape[1] // n

    def columns(peer):
        return x_ref.at[:, pl.ds(pl.multiple_of(peer * width, width), width)]

    parts[me] = columns(me)[...]
    greet(axis, n, me)
    all_to_all(axis, n, me, columns, parts, sems.at[0], sems.at[1])
    mine[...] = jnp.sum(parts[...].astype(jnp.float32), axis=0).astype(mine.dtype)
    gathered[me] = mine[...]
    all_to_all(axis, n, me, lambda peer: mine, gathered, sems.at[2], sems.at[3])
    for peer in range(n):
        o_ref[:, peer * width:(peer + 1) * width] = gathered[peer]


def reduce_kernel(axis, n, x_ref, o_ref, parts, sems):
    me = lax.axis_index(axis)
    height = x_ref.shape[0] // n

    def rows(peer):
        return x_ref.at[pl.ds(pl.multiple_of(peer * height, height), height)]

    parts[me] = rows(me)[...]
    greet(axis, n, me)
    all_to_all(axis, n, me, rows, parts, sems.at[0], sems.at[1])
    total = jnp.sum(parts[...], axis=0).reshape(o_ref.shape)
    o_ref[...] = total.astype(o_ref.dtype)


def broadcast_sum(value, axis):
    n = lax.axis_size(axis)
    chunk = (value.shape[0], value.shape[1] // n)
    return pl.pallas_call(
        functools.partial(broadcast_kernel, axis, n),
        out_shape=jax.ShapeDtypeStruct(value.shape, value.dtype),
        in_specs=[pl.BlockSpec(memory_space=pltpu.VMEM)],
        out_specs=pl.BlockSpec(memory_space=pltpu.VMEM),
        scratch_shapes=[pltpu.VMEM((n,) + chunk, value.dtype), pltpu.VMEM(chunk, value.dtype),
                        pltpu.VMEM((n,) + chunk, value.dtype), pltpu.SemaphoreType.DMA((4, n))],
        compiler_params=pltpu.CompilerParams(collective_id=0, has_side_effects=True),
    )(value)


def scatter_sum(rows, axis, shape, dtype):
    n = lax.axis_size(axis)
    chunk = (rows.shape[0] // n, rows.shape[1])
    return pl.pallas_call(
        functools.partial(reduce_kernel, axis, n),
        out_shape=jax.ShapeDtypeStruct(shape, dtype),
        in_specs=[pl.BlockSpec(memory_space=pltpu.VMEM)],
        out_specs=pl.BlockSpec(memory_space=pltpu.VMEM),
        scratch_shapes=[pltpu.VMEM((n,) + chunk, rows.dtype), pltpu.SemaphoreType.DMA((2, n))],
        compiler_params=pltpu.CompilerParams(collective_id=1, has_side_effects=True),
    )(rows)


def body(spectra, quality, source_block):
    window_count, channel_count, row_width = spectra.shape
    bins = row_width // 2
    total_windows = window_count * lax.axis_size("win")
    cos_t, sin_t = lag_table(bins, L, 1.0 / math.sqrt(row_width * total_windows))
    whitened = whiten(spectra, quality)
    per_group = channel_count // SRC
    me = lax.axis_index("chan")
    block_ids = me * per_group + lax.iota(jnp.int32, per_group)
    chosen = block_ids[None, :] == source_block[:, None]
    blocks = whitened.reshape(window_count, per_group, SRC, row_width)
    kept = jnp.sum(
        jnp.where(chosen[:, None, :, None, None], blocks[None], jnp.zeros((), blocks.dtype)),
        axis=2, dtype=jnp.float32,
    ).astype(jnp.bfloat16)
    sources = broadcast_sum(
        kept.reshape(STEPS * window_count * SRC, row_width), "chan"
    ).reshape(STEPS, window_count, SRC, row_width)
    win_size = lax.axis_size("win")
    per_dest = channel_count // win_size
    reals, imags = [], []
    for step in range(STEPS):
        real_part, imag_part = cross_spectra(sources[step], whitened)
        reals.append(real_part.reshape(win_size, per_dest, SRC, bins))
        imags.append(imag_part.reshape(win_size, per_dest, SRC, bins))
    rows = channel_count * SRC * STEPS
    real_rows = jnp.stack(reals, axis=1).reshape(rows, bins)
    imag_rows = jnp.stack(imags, axis=1).reshape(rows, bins)
    out = jnp.dot(
        real_rows, cos_t, precision=lax.Precision.HIGH, preferred_element_type=jnp.float32
    )
    out = out + jnp.dot(
        imag_rows, sin_t, precision=lax.Precision.HIGH, preferred_element_type=jnp.float32
    )
    return scatter_sum(out, "win", (STEPS, per_dest, SRC, L), jnp.bfloat16)


def solution(mesh):
    return jax.shard_map(
        body,
        mesh=mesh,
        in_specs=(P("win", "chan", None), P("chan"), P()),
        out_specs=P(None, ("chan", "win"), None, None),
        check_vma=False,
    )
```

```python
import functools
import math

import jax
import jax.numpy as jnp
from jax import lax
from jax.experimental import pallas as pl
from jax.experimental.pallas import tpu as pltpu
from jax.sharding import PartitionSpec as P

L = 512
SRC = 8
STEPS = 2


def from_root(value, axis, source):
    kept = jnp.where(lax.axis_index(axis) == source, value, 0).astype(value.dtype)
    return lax.psum(kept, axis)


def lag_table(bins, lags, factor):
    inner = 64
    period = 2 * bins
    shifts = lax.iota(jnp.int32, lags)[None, :] - lags // 2
    hi = lax.iota(jnp.int32, bins // inner)[:, None] * inner
    lo = lax.iota(jnp.int32, inner)[:, None]
    scale = 2.0 * math.pi / period
    angle_hi = jnp.mod(hi * shifts, period).astype(jnp.float32) * scale
    angle_lo = jnp.mod(lo * shifts, period).astype(jnp.float32) * scale
    cos_hi, sin_hi = jnp.cos(angle_hi)[:, None, :], jnp.sin(angle_hi)[:, None, :]
    cos_lo, sin_lo = jnp.cos(angle_lo)[None, :, :], jnp.sin(angle_lo)[None, :, :]
    cos_t = (cos_hi * cos_lo - sin_hi * sin_lo).reshape(bins, lags)
    sin_t = (sin_hi * cos_lo + cos_hi * sin_lo).reshape(bins, lags)
    return cos_t * factor, -sin_t * factor


def whiten(block, quality):
    values = block.astype(jnp.float32)
    bins = values.shape[-1] // 2
    energy = jnp.sum(values * values, axis=-1) / bins
    weights = quality.astype(jnp.float32)[None, :] / jnp.sqrt(energy + 1e-06)
    return (values * weights[:, :, None]).astype(jnp.bfloat16)


def cross_spectra(sources, receivers):
    bins = sources.shape[-1] // 2
    sr = sources[:, None, :, :bins].astype(jnp.float32)
    si = sources[:, None, :, bins:].astype(jnp.float32)
    rr = receivers[:, :, None, :bins].astype(jnp.float32)
    ri = receivers[:, :, None, bins:].astype(jnp.float32)
    real_part = jnp.sum(sr * rr + si * ri, axis=0)
    imag_part = jnp.sum(sr * ri - si * rr, axis=0)
    return real_part, imag_part


def greet(groups):
    barrier = pltpu.get_barrier_semaphore()
    count = 0
    for axis, n in groups:
        me = lax.axis_index(axis)
        for k in range(1, n):
            pl.semaphore_signal(barrier, inc=1, device_id={axis: (me + k) % n},
                                device_id_type=pl.DeviceIdType.MESH)
        count += n - 1
    pl.semaphore_wait(barrier, count)


def start_all_to_all(axis, n, rows_of, landing, send_sem, recv_sem):
    me = lax.axis_index(axis)
    copies = []
    for k in range(1, n):
        peer = (me + k) % n
        copy = pltpu.make_async_remote_copy(
            src_ref=rows_of(peer), dst_ref=landing.at[me], send_sem=send_sem.at[k],
            recv_sem=recv_sem.at[me], device_id={axis: peer},
            device_id_type=pl.DeviceIdType.MESH)
        copy.start()
        copies.append(copy)

    def wait():
        for copy in copies:
            copy.wait_send()
        for k in range(1, n):
            source = (me + n - k) % n
            pltpu.make_async_remote_copy(
                src_ref=landing.at[source], dst_ref=landing.at[source], send_sem=send_sem.at[k],
                recv_sem=recv_sem.at[source], device_id={axis: source},
                device_id_type=pl.DeviceIdType.MESH).wait_recv()

    return wait


def columns_of(ref, n):
    width = ref.shape[1] // n
    return lambda peer: ref.at[:, pl.ds(pl.multiple_of(peer * width, width), width)]


def rows_of(ref, n):
    height = ref.shape[0] // n
    return lambda peer: ref.at[pl.ds(pl.multiple_of(peer * height, height), height)]


def broadcast_phases(axis, n, x_ref, o_ref, parts, mine, gathered, sems):
    me = lax.axis_index(axis)
    columns = columns_of(x_ref, n)
    parts[me] = columns(me)[...]
    wait = start_all_to_all(axis, n, columns, parts, sems.at[0], sems.at[1])
    yield
    wait()
    mine[...] = jnp.sum(parts[...].astype(jnp.float32), axis=0).astype(mine.dtype)
    gathered[me] = mine[...]
    wait = start_all_to_all(axis, n, lambda peer: mine, gathered, sems.at[2], sems.at[3])
    yield
    wait()
    width = mine.shape[1]
    for peer in range(n):
        o_ref[:, peer * width:(peer + 1) * width] = gathered[peer]


def reduce_phases(axis, n, x_ref, o_ref, parts, sems):
    me = lax.axis_index(axis)
    rows = rows_of(x_ref, n)
    parts[me] = rows(me)[...]
    wait = start_all_to_all(axis, n, rows, parts, sems.at[0], sems.at[1])
    yield
    wait()
    total = jnp.sum(parts[...], axis=0).reshape(o_ref.shape)
    o_ref[...] = total.astype(o_ref.dtype)


def run(*phase_lists):
    for phases in phase_lists:
        next(phases)
    for phases in phase_lists:
        for _ in phases:
            pass


def broadcast_kernel(axis, n, x_ref, o_ref, parts, mine, gathered, sems):
    greet([(axis, n)])
    run(broadcast_phases(axis, n, x_ref, o_ref, parts, mine, gathered, sems))


def reduce_kernel(axis, n, x_ref, o_ref, parts, sems):
    greet([(axis, n)])
    run(reduce_phases(axis, n, x_ref, o_ref, parts, sems))


def both_kernel(red_axis, rn, bc_axis, bn, rx_ref, bx_ref, ro_ref, bo_ref, rparts, rsems,
                bparts, bmine, bgathered, bsems):
    greet([(red_axis, rn), (bc_axis, bn)])
    run(reduce_phases(red_axis, rn, rx_ref, ro_ref, rparts, rsems),
        broadcast_phases(bc_axis, bn, bx_ref, bo_ref, bparts, bmine, bgathered, bsems))


def broadcast_scratch(value, n):
    chunk = (value.shape[0], value.shape[1] // n)
    return [pltpu.VMEM((n,) + chunk, value.dtype), pltpu.VMEM(chunk, value.dtype),
            pltpu.VMEM((n,) + chunk, value.dtype), pltpu.SemaphoreType.DMA((4, n))]


def reduce_scratch(rows, n):
    chunk = (rows.shape[0] // n, rows.shape[1])
    return [pltpu.VMEM((n,) + chunk, rows.dtype), pltpu.SemaphoreType.DMA((2, n))]


def vmem_call(kernel, out_shape, scratch, cid, *args):
    return pl.pallas_call(
        kernel,
        out_shape=out_shape,
        in_specs=[pl.BlockSpec(memory_space=pltpu.VMEM)] * len(args),
        out_specs=jax.tree.map(lambda _: pl.BlockSpec(memory_space=pltpu.VMEM), out_shape),
        scratch_shapes=scratch,
        compiler_params=pltpu.CompilerParams(collective_id=cid, has_side_effects=True),
    )(*args)


def body(spectra, quality, source_block):
    window_count, channel_count, row_width = spectra.shape
    bins = row_width // 2
    total_windows = window_count * lax.axis_size("win")
    cos_t, sin_t = lag_table(bins, L, 1.0 / math.sqrt(row_width * total_windows))
    whitened = whiten(spectra, quality)
    per_group = channel_count // SRC
    me = lax.axis_index("chan")
    block_ids = me * per_group + lax.iota(jnp.int32, per_group)
    chosen = block_ids[None, :] == source_block[:, None]
    blocks = whitened.reshape(window_count, per_group, SRC, row_width)
    kept = jnp.sum(
        jnp.where(chosen[:, None, :, None, None], blocks[None], jnp.zeros((), blocks.dtype)),
        axis=2, dtype=jnp.float32,
    ).astype(jnp.bfloat16)
    n = lax.axis_size("chan")
    win_size = lax.axis_size("win")
    per_dest = channel_count // win_size
    flat = kept.reshape(STEPS, window_count * SRC, row_width)
    src_shape = jax.ShapeDtypeStruct(flat.shape[1:], flat.dtype)
    out_shape = jax.ShapeDtypeStruct((per_dest, SRC, L), jnp.bfloat16)

    def lagged(sources):
        real_part, imag_part = cross_spectra(sources.reshape(window_count, SRC, row_width), whitened)
        rows = channel_count * SRC
        out = jnp.dot(real_part.reshape(rows, bins), cos_t,
                      precision=lax.Precision.HIGH, preferred_element_type=jnp.float32)
        return out + jnp.dot(imag_part.reshape(rows, bins), sin_t,
                             precision=lax.Precision.HIGH, preferred_element_type=jnp.float32)

    first = vmem_call(functools.partial(broadcast_kernel, "chan", n), src_shape,
                      broadcast_scratch(flat[0], n), 0, flat[0])
    rows0 = lagged(first)
    red0, second = vmem_call(
        functools.partial(both_kernel, "win", win_size, "chan", n), (out_shape, src_shape),
        reduce_scratch(rows0, win_size) + broadcast_scratch(flat[1], n), 1, rows0, flat[1])
    rows1 = lagged(second)
    red1 = vmem_call(functools.partial(reduce_kernel, "win", win_size), out_shape,
                     reduce_scratch(rows1, win_size), 2, rows1)
    return jnp.stack([red0, red1])


def solution(mesh):
    return jax.shard_map(
        body,
        mesh=mesh,
        in_specs=(P("win", "chan", None), P("chan"), P()),
        out_specs=P(None, ("chan", "win"), None, None),
        check_vma=False,
    )
```

```python
import functools
import math

import jax
import jax.numpy as jnp
from jax import lax
from jax.experimental import pallas as pl
from jax.experimental.pallas import tpu as pltpu
from jax.sharding import PartitionSpec as P

L = 512
SRC = 8
STEPS = 2


def from_root(value, axis, source):
    kept = jnp.where(lax.axis_index(axis) == source, value, 0).astype(value.dtype)
    return lax.psum(kept, axis)


def lag_table(bins, lags, factor):
    inner = 64
    period = 2 * bins
    shifts = lax.iota(jnp.int32, lags)[None, :] - lags // 2
    hi = lax.iota(jnp.int32, bins // inner)[:, None] * inner
    lo = lax.iota(jnp.int32, inner)[:, None]
    scale = 2.0 * math.pi / period
    angle_hi = jnp.mod(hi * shifts, period).astype(jnp.float32) * scale
    angle_lo = jnp.mod(lo * shifts, period).astype(jnp.float32) * scale
    cos_hi, sin_hi = jnp.cos(angle_hi)[:, None, :], jnp.sin(angle_hi)[:, None, :]
    cos_lo, sin_lo = jnp.cos(angle_lo)[None, :, :], jnp.sin(angle_lo)[None, :, :]
    cos_t = (cos_hi * cos_lo - sin_hi * sin_lo).reshape(bins, lags)
    sin_t = (sin_hi * cos_lo + cos_hi * sin_lo).reshape(bins, lags)
    return cos_t * factor, -sin_t * factor


def whiten(block, quality):
    values = block.astype(jnp.float32)
    bins = values.shape[-1] // 2
    energy = jnp.sum(values * values, axis=-1) / bins
    weights = quality.astype(jnp.float32)[None, :] / jnp.sqrt(energy + 1e-06)
    return (values * weights[:, :, None]).astype(jnp.bfloat16)


def cross_spectra(sources, receivers):
    bins = sources.shape[-1] // 2
    sr = sources[:, None, :, :bins].astype(jnp.float32)
    si = sources[:, None, :, bins:].astype(jnp.float32)
    rr = receivers[:, :, None, :bins].astype(jnp.float32)
    ri = receivers[:, :, None, bins:].astype(jnp.float32)
    real_part = jnp.sum(sr * rr + si * ri, axis=0)
    imag_part = jnp.sum(sr * ri - si * rr, axis=0)
    return real_part, imag_part


def greet(axis, n, me):
    barrier = pltpu.get_barrier_semaphore()
    for k in range(1, n):
        pl.semaphore_signal(barrier, inc=1, device_id={axis: (me + k) % n},
                            device_id_type=pl.DeviceIdType.MESH)
    pl.semaphore_wait(barrier, n - 1)


def all_to_all(axis, n, me, rows_of, landing, send_sem, recv_sem):
    copies = []
    for k in range(1, n):
        peer = (me + k) % n
        copy = pltpu.make_async_remote_copy(
            src_ref=rows_of(peer), dst_ref=landing.at[me], send_sem=send_sem.at[k],
            recv_sem=recv_sem.at[me], device_id={axis: peer},
            device_id_type=pl.DeviceIdType.MESH)
        copy.start()
        copies.append(copy)
    for copy in copies:
        copy.wait_send()
    for k in range(1, n):
        source = (me + n - k) % n
        pltpu.make_async_remote_copy(
            src_ref=landing.at[source], dst_ref=landing.at[source], send_sem=send_sem.at[k],
            recv_sem=recv_sem.at[source], device_id={axis: source},
            device_id_type=pl.DeviceIdType.MESH).wait_recv()


def broadcast_kernel(axis, n, x_ref, o_ref, parts, mine, gathered, sems):
    me = lax.axis_index(axis)
    width = x_ref.shape[1] // n

    def columns(peer):
        return x_ref.at[:, pl.ds(pl.multiple_of(peer * width, width), width)]

    parts[me] = columns(me)[...]
    greet(axis, n, me)
    all_to_all(axis, n, me, columns, parts, sems.at[0], sems.at[1])
    mine[...] = jnp.sum(parts[...].astype(jnp.float32), axis=0).astype(mine.dtype)
    gathered[me] = mine[...]
    all_to_all(axis, n, me, lambda peer: mine, gathered, sems.at[2], sems.at[3])
    for peer in range(n):
        o_ref[:, peer * width:(peer + 1) * width] = gathered[peer]


def reduce_kernel(axis, n, x_ref, o_ref, parts, sems):
    me = lax.axis_index(axis)
    height = x_ref.shape[0] // n

    def rows(peer):
        return x_ref.at[pl.ds(pl.multiple_of(peer * height, height), height)]

    parts[me] = rows(me)[...]
    greet(axis, n, me)
    all_to_all(axis, n, me, rows, parts, sems.at[0], sems.at[1])
    total = jnp.sum(parts[...], axis=0).reshape(o_ref.shape)
    o_ref[...] = total.astype(o_ref.dtype)


def broadcast_sum(value, axis):
    n = lax.axis_size(axis)
    chunk = (value.shape[0], value.shape[1] // n)
    return pl.pallas_call(
        functools.partial(broadcast_kernel, axis, n),
        out_shape=jax.ShapeDtypeStruct(value.shape, value.dtype),
        in_specs=[pl.BlockSpec(memory_space=pltpu.VMEM)],
        out_specs=pl.BlockSpec(memory_space=pltpu.VMEM),
        scratch_shapes=[pltpu.VMEM((n,) + chunk, value.dtype), pltpu.VMEM(chunk, value.dtype),
                        pltpu.VMEM((n,) + chunk, value.dtype), pltpu.SemaphoreType.DMA((4, n))],
        compiler_params=pltpu.CompilerParams(collective_id=0, has_side_effects=True),
    )(value)


def start_all_to_all(axis, n, rows_of, landing, send_sem, recv_sem):
    me = lax.axis_index(axis)
    copies = []
    for k in range(1, n):
        peer = (me + k) % n
        copy = pltpu.make_async_remote_copy(
            src_ref=rows_of(peer), dst_ref=landing.at[me], send_sem=send_sem.at[k],
            recv_sem=recv_sem.at[me], device_id={axis: peer},
            device_id_type=pl.DeviceIdType.MESH)
        copy.start()
        copies.append(copy)

    def wait():
        for copy in copies:
            copy.wait_send()
        for k in range(1, n):
            source = (me + n - k) % n
            pltpu.make_async_remote_copy(
                src_ref=landing.at[source], dst_ref=landing.at[source], send_sem=send_sem.at[k],
                recv_sem=recv_sem.at[source], device_id={axis: source},
                device_id_type=pl.DeviceIdType.MESH).wait_recv()

    return wait


def columns_of(ref, n):
    width = ref.shape[1] // n
    return lambda peer: ref.at[:, pl.ds(pl.multiple_of(peer * width, width), width)]


def whiten_broadcast_kernel(axis, n, per_group, spec_ref, q_ref, sb_ref, o_ref, w_ref,
                            send, parts, mine, gathered, sems):
    me = lax.axis_index(axis)
    windows, channels, width = spec_ref.shape
    bins = width // 2
    steps = sb_ref.shape[0]

    def weighted(w):
        values = spec_ref[w].astype(jnp.float32)
        energy = jnp.sum(values * values, axis=-1, keepdims=True) / bins
        return values * (q_ref[...] / jnp.sqrt(energy + 1e-06))

    for w in range(windows):
        block = weighted(w)
        for k in range(steps):
            kept = jnp.zeros((SRC, width), jnp.float32)
            for b in range(per_group):
                hit = me * per_group + b == sb_ref[k]
                kept = kept + jnp.where(hit, block[b * SRC:(b + 1) * SRC], 0.0)
            row = (k * windows + w) * SRC
            send[row:row + SRC, :] = kept.astype(send.dtype)
    greet(axis, n, me)
    columns = columns_of(send, n)
    parts[me] = columns(me)[...]
    wait = start_all_to_all(axis, n, columns, parts, sems.at[0], sems.at[1])
    for w in range(windows):
        w_ref[w] = weighted(w).astype(w_ref.dtype)
    wait()
    mine[...] = jnp.sum(parts[...].astype(jnp.float32), axis=0).astype(mine.dtype)
    gathered[me] = mine[...]
    wait = start_all_to_all(axis, n, lambda peer: mine, gathered, sems.at[2], sems.at[3])
    wait()
    piece = mine.shape[1]
    for peer in range(n):
        o_ref[:, peer * piece:(peer + 1) * piece] = gathered[peer]


def whiten_broadcast(spectra, quality, source_block, axis):
    n = lax.axis_size(axis)
    windows, channels, width = spectra.shape
    rows = source_block.shape[0] * windows * SRC
    chunk = (rows, width // n)
    vmem = pl.BlockSpec(memory_space=pltpu.VMEM)
    return pl.pallas_call(
        functools.partial(whiten_broadcast_kernel, axis, n, channels // SRC),
        out_shape=(jax.ShapeDtypeStruct((rows, width), jnp.bfloat16),
                   jax.ShapeDtypeStruct(spectra.shape, jnp.bfloat16)),
        in_specs=[vmem, vmem, pl.BlockSpec(memory_space=pltpu.SMEM)],
        out_specs=(vmem, vmem),
        scratch_shapes=[pltpu.VMEM((rows, width), jnp.bfloat16),
                        pltpu.VMEM((n,) + chunk, jnp.bfloat16), pltpu.VMEM(chunk, jnp.bfloat16),
                        pltpu.VMEM((n,) + chunk, jnp.bfloat16), pltpu.SemaphoreType.DMA((4, n))],
        compiler_params=pltpu.CompilerParams(collective_id=0, has_side_effects=True),
    )(spectra, quality.astype(jnp.float32).reshape(channels, 1), source_block)


def scatter_sum(rows, axis, shape, dtype):
    n = lax.axis_size(axis)
    chunk = (rows.shape[0] // n, rows.shape[1])
    return pl.pallas_call(
        functools.partial(reduce_kernel, axis, n),
        out_shape=jax.ShapeDtypeStruct(shape, dtype),
        in_specs=[pl.BlockSpec(memory_space=pltpu.VMEM)],
        out_specs=pl.BlockSpec(memory_space=pltpu.VMEM),
        scratch_shapes=[pltpu.VMEM((n,) + chunk, rows.dtype), pltpu.SemaphoreType.DMA((2, n))],
        compiler_params=pltpu.CompilerParams(collective_id=1, has_side_effects=True),
    )(rows)


def body(spectra, quality, source_block):
    window_count, channel_count, row_width = spectra.shape
    bins = row_width // 2
    total_windows = window_count * lax.axis_size("win")
    cos_t, sin_t = lag_table(bins, L, 1.0 / math.sqrt(row_width * total_windows))
    sources, whitened = whiten_broadcast(spectra, quality, source_block, "chan")
    sources = sources.reshape(STEPS, window_count, SRC, row_width)
    win_size = lax.axis_size("win")
    per_dest = channel_count // win_size
    reals, imags = [], []
    for step in range(STEPS):
        real_part, imag_part = cross_spectra(sources[step], whitened)
        reals.append(real_part.reshape(win_size, per_dest, SRC, bins))
        imags.append(imag_part.reshape(win_size, per_dest, SRC, bins))
    rows = channel_count * SRC * STEPS
    real_rows = jnp.stack(reals, axis=1).reshape(rows, bins)
    imag_rows = jnp.stack(imags, axis=1).reshape(rows, bins)
    out = jnp.dot(
        real_rows, cos_t, precision=lax.Precision.HIGH, preferred_element_type=jnp.float32
    )
    out = out + jnp.dot(
        imag_rows, sin_t, precision=lax.Precision.HIGH, preferred_element_type=jnp.float32
    )
    return scatter_sum(out, "win", (STEPS, per_dest, SRC, L), jnp.bfloat16)


def solution(mesh):
    return jax.shard_map(
        body,
        mesh=mesh,
        in_specs=(P("win", "chan", None), P("chan"), P()),
        out_specs=P(None, ("chan", "win"), None, None),
        check_vma=False,
    )
```

```python
import functools
import math

import jax
import jax.numpy as jnp
from jax import lax
from jax.experimental import pallas as pl
from jax.experimental.pallas import tpu as pltpu
from jax.sharding import PartitionSpec as P

L = 512
SRC = 8
STEPS = 2


def from_root(value, axis, source):
    kept = jnp.where(lax.axis_index(axis) == source, value, 0).astype(value.dtype)
    return lax.psum(kept, axis)


def lag_table(bins, lags, factor):
    inner = 64
    period = 2 * bins
    shifts = lax.iota(jnp.int32, lags)[None, :] - lags // 2
    hi = lax.iota(jnp.int32, bins // inner)[:, None] * inner
    lo = lax.iota(jnp.int32, inner)[:, None]
    scale = 2.0 * math.pi / period
    angle_hi = jnp.mod(hi * shifts, period).astype(jnp.float32) * scale
    angle_lo = jnp.mod(lo * shifts, period).astype(jnp.float32) * scale
    cos_hi, sin_hi = jnp.cos(angle_hi)[:, None, :], jnp.sin(angle_hi)[:, None, :]
    cos_lo, sin_lo = jnp.cos(angle_lo)[None, :, :], jnp.sin(angle_lo)[None, :, :]
    cos_t = (cos_hi * cos_lo - sin_hi * sin_lo).reshape(bins, lags)
    sin_t = (sin_hi * cos_lo + cos_hi * sin_lo).reshape(bins, lags)
    return cos_t * factor, -sin_t * factor


def whiten(block, quality):
    values = block.astype(jnp.float32)
    bins = values.shape[-1] // 2
    energy = jnp.sum(values * values, axis=-1) / bins
    weights = quality.astype(jnp.float32)[None, :] / jnp.sqrt(energy + 1e-06)
    return (values * weights[:, :, None]).astype(jnp.bfloat16)


def cross_spectra(sources, receivers):
    bins = sources.shape[-1] // 2
    sr = sources[:, None, :, :bins].astype(jnp.float32)
    si = sources[:, None, :, bins:].astype(jnp.float32)
    rr = receivers[:, :, None, :bins].astype(jnp.float32)
    ri = receivers[:, :, None, bins:].astype(jnp.float32)
    real_part = jnp.sum(sr * rr + si * ri, axis=0)
    imag_part = jnp.sum(sr * ri - si * rr, axis=0)
    return real_part, imag_part


def greet(axis, n, me):
    barrier = pltpu.get_barrier_semaphore()
    for k in range(1, n):
        pl.semaphore_signal(barrier, inc=1, device_id={axis: (me + k) % n},
                            device_id_type=pl.DeviceIdType.MESH)
    pl.semaphore_wait(barrier, n - 1)


def all_to_all(axis, n, me, rows_of, landing, send_sem, recv_sem):
    copies = []
    for k in range(1, n):
        peer = (me + k) % n
        copy = pltpu.make_async_remote_copy(
            src_ref=rows_of(peer), dst_ref=landing.at[me], send_sem=send_sem.at[k],
            recv_sem=recv_sem.at[me], device_id={axis: peer},
            device_id_type=pl.DeviceIdType.MESH)
        copy.start()
        copies.append(copy)
    for copy in copies:
        copy.wait_send()
    for k in range(1, n):
        source = (me + n - k) % n
        pltpu.make_async_remote_copy(
            src_ref=landing.at[source], dst_ref=landing.at[source], send_sem=send_sem.at[k],
            recv_sem=recv_sem.at[source], device_id={axis: source},
            device_id_type=pl.DeviceIdType.MESH).wait_recv()


def broadcast_kernel(axis, n, x_ref, o_ref, parts, mine, gathered, sems):
    me = lax.axis_index(axis)
    width = x_ref.shape[1] // n

    def columns(peer):
        return x_ref.at[:, pl.ds(pl.multiple_of(peer * width, width), width)]

    parts[me] = columns(me)[...]
    greet(axis, n, me)
    all_to_all(axis, n, me, columns, parts, sems.at[0], sems.at[1])
    mine[...] = jnp.sum(parts[...].astype(jnp.float32), axis=0).astype(mine.dtype)
    gathered[me] = mine[...]
    all_to_all(axis, n, me, lambda peer: mine, gathered, sems.at[2], sems.at[3])
    for peer in range(n):
        o_ref[:, peer * width:(peer + 1) * width] = gathered[peer]


def reduce_kernel(axis, n, x_ref, o_ref, parts, sems):
    me = lax.axis_index(axis)
    height = x_ref.shape[0] // n

    def rows(peer):
        return x_ref.at[pl.ds(pl.multiple_of(peer * height, height), height)]

    parts[me] = rows(me)[...]
    greet(axis, n, me)
    all_to_all(axis, n, me, rows, parts, sems.at[0], sems.at[1])
    total = jnp.sum(parts[...], axis=0).reshape(o_ref.shape)
    o_ref[...] = total.astype(o_ref.dtype)


def broadcast_sum(value, axis):
    n = lax.axis_size(axis)
    chunk = (value.shape[0], value.shape[1] // n)
    return pl.pallas_call(
        functools.partial(broadcast_kernel, axis, n),
        out_shape=jax.ShapeDtypeStruct(value.shape, value.dtype),
        in_specs=[pl.BlockSpec(memory_space=pltpu.VMEM)],
        out_specs=pl.BlockSpec(memory_space=pltpu.VMEM),
        scratch_shapes=[pltpu.VMEM((n,) + chunk, value.dtype), pltpu.VMEM(chunk, value.dtype),
                        pltpu.VMEM((n,) + chunk, value.dtype), pltpu.SemaphoreType.DMA((4, n))],
        compiler_params=pltpu.CompilerParams(collective_id=0, has_side_effects=True),
    )(value)


def start_all_to_all(axis, n, rows_of, landing, send_sem, recv_sem):
    me = lax.axis_index(axis)
    copies = []
    for k in range(1, n):
        peer = (me + k) % n
        copy = pltpu.make_async_remote_copy(
            src_ref=rows_of(peer), dst_ref=landing.at[me], send_sem=send_sem.at[k],
            recv_sem=recv_sem.at[me], device_id={axis: peer},
            device_id_type=pl.DeviceIdType.MESH)
        copy.start()
        copies.append(copy)

    def wait():
        for copy in copies:
            copy.wait_send()
        for k in range(1, n):
            source = (me + n - k) % n
            pltpu.make_async_remote_copy(
                src_ref=landing.at[source], dst_ref=landing.at[source], send_sem=send_sem.at[k],
                recv_sem=recv_sem.at[source], device_id={axis: source},
                device_id_type=pl.DeviceIdType.MESH).wait_recv()

    return wait


def columns_of(ref, n):
    width = ref.shape[1] // n
    return lambda peer: ref.at[:, pl.ds(pl.multiple_of(peer * width, width), width)]


def whiten_broadcast_kernel(axis, n, per_group, spec_ref, q_ref, sb_ref, sr_ref, si_ref,
                            rr_ref, ri_ref, send, parts, mine, gathered, sems):
    me = lax.axis_index(axis)
    windows, channels, width = spec_ref.shape
    bins = width // 2
    steps = sb_ref.shape[0]

    def weighted(w):
        values = spec_ref[w].astype(jnp.float32)
        energy = jnp.sum(values * values, axis=-1, keepdims=True) / bins
        return values * (q_ref[...] / jnp.sqrt(energy + 1e-06))

    for w in range(windows):
        block = weighted(w)
        for k in range(steps):
            kept = jnp.zeros((SRC, width), jnp.float32)
            for b in range(per_group):
                hit = me * per_group + b == sb_ref[k]
                kept = kept + jnp.where(hit, block[b * SRC:(b + 1) * SRC], 0.0)
            row = (k * windows + w) * SRC
            send[row:row + SRC, :] = kept.astype(send.dtype)
    greet(axis, n, me)
    columns = columns_of(send, n)
    parts[me] = columns(me)[...]
    wait = start_all_to_all(axis, n, columns, parts, sems.at[0], sems.at[1])
    for w in range(windows):
        rounded = weighted(w).astype(jnp.bfloat16).astype(jnp.float32)
        rr_ref[w] = rounded[:, :bins]
        ri_ref[w] = rounded[:, bins:]
    wait()
    mine[...] = jnp.sum(parts[...].astype(jnp.float32), axis=0).astype(mine.dtype)
    gathered[me] = mine[...]
    wait = start_all_to_all(axis, n, lambda peer: mine, gathered, sems.at[2], sems.at[3])
    wait()
    piece = mine.shape[1]
    for peer in range(n):
        start = peer * piece
        if start < bins:
            sr_ref[:, start:start + piece] = gathered[peer].astype(jnp.float32)
        else:
            si_ref[:, start - bins:start - bins + piece] = gathered[peer].astype(jnp.float32)


def whiten_broadcast(spectra, quality, source_block, axis):
    n = lax.axis_size(axis)
    windows, channels, width = spectra.shape
    rows = source_block.shape[0] * windows * SRC
    chunk = (rows, width // n)
    vmem = pl.BlockSpec(memory_space=pltpu.VMEM)
    return pl.pallas_call(
        functools.partial(whiten_broadcast_kernel, axis, n, channels // SRC),
        out_shape=(jax.ShapeDtypeStruct((rows, width // 2), jnp.float32),) * 2
        + (jax.ShapeDtypeStruct((windows, channels, width // 2), jnp.float32),) * 2,
        in_specs=[vmem, vmem, pl.BlockSpec(memory_space=pltpu.SMEM)],
        out_specs=(vmem,) * 4,
        scratch_shapes=[pltpu.VMEM((rows, width), jnp.bfloat16),
                        pltpu.VMEM((n,) + chunk, jnp.bfloat16), pltpu.VMEM(chunk, jnp.bfloat16),
                        pltpu.VMEM((n,) + chunk, jnp.bfloat16), pltpu.SemaphoreType.DMA((4, n))],
        compiler_params=pltpu.CompilerParams(collective_id=0, has_side_effects=True),
    )(spectra, quality.astype(jnp.float32).reshape(channels, 1), source_block)


def scatter_sum(rows, axis, shape, dtype):
    n = lax.axis_size(axis)
    chunk = (rows.shape[0] // n, rows.shape[1])
    return pl.pallas_call(
        functools.partial(reduce_kernel, axis, n),
        out_shape=jax.ShapeDtypeStruct(shape, dtype),
        in_specs=[pl.BlockSpec(memory_space=pltpu.VMEM)],
        out_specs=pl.BlockSpec(memory_space=pltpu.VMEM),
        scratch_shapes=[pltpu.VMEM((n,) + chunk, rows.dtype), pltpu.SemaphoreType.DMA((2, n))],
        compiler_params=pltpu.CompilerParams(collective_id=1, has_side_effects=True),
    )(rows)


def cross_parts(src_re, src_im, rec_re, rec_im):
    sr, si = src_re[:, None], src_im[:, None]
    rr, ri = rec_re[:, :, None], rec_im[:, :, None]
    real_part = jnp.sum(sr * rr + si * ri, axis=0)
    imag_part = jnp.sum(sr * ri - si * rr, axis=0)
    return real_part, imag_part


def body(spectra, quality, source_block):
    window_count, channel_count, row_width = spectra.shape
    bins = row_width // 2
    total_windows = window_count * lax.axis_size("win")
    cos_t, sin_t = lag_table(bins, L, 1.0 / math.sqrt(row_width * total_windows))
    src_re, src_im, rec_re, rec_im = whiten_broadcast(spectra, quality, source_block, "chan")
    src_re = src_re.reshape(STEPS, window_count, SRC, bins)
    src_im = src_im.reshape(STEPS, window_count, SRC, bins)
    win_size = lax.axis_size("win")
    per_dest = channel_count // win_size
    reals, imags = [], []
    for step in range(STEPS):
        real_part, imag_part = cross_parts(src_re[step], src_im[step], rec_re, rec_im)
        reals.append(real_part.reshape(win_size, per_dest, SRC, bins))
        imags.append(imag_part.reshape(win_size, per_dest, SRC, bins))
    rows = channel_count * SRC * STEPS
    real_rows = jnp.stack(reals, axis=1).reshape(rows, bins)
    imag_rows = jnp.stack(imags, axis=1).reshape(rows, bins)
    out = jnp.dot(
        real_rows, cos_t, precision=lax.Precision.HIGH, preferred_element_type=jnp.float32
    )
    out = out + jnp.dot(
        imag_rows, sin_t, precision=lax.Precision.HIGH, preferred_element_type=jnp.float32
    )
    return scatter_sum(out, "win", (STEPS, per_dest, SRC, L), jnp.bfloat16)


def solution(mesh):
    return jax.shard_map(
        body,
        mesh=mesh,
        in_specs=(P("win", "chan", None), P("chan"), P()),
        out_specs=P(None, ("chan", "win"), None, None),
        check_vma=False,
    )
```

```python
import functools
import math

import jax
import jax.numpy as jnp
from jax import lax
from jax.experimental import pallas as pl
from jax.experimental.pallas import tpu as pltpu
from jax.sharding import PartitionSpec as P

L = 512
SRC = 8
STEPS = 2


def from_root(value, axis, source):
    kept = jnp.where(lax.axis_index(axis) == source, value, 0).astype(value.dtype)
    return lax.psum(kept, axis)


def lag_table(bins, lags, factor):
    inner = 64
    period = 2 * bins
    shifts = lax.iota(jnp.int32, lags)[None, :] - lags // 2
    hi = lax.iota(jnp.int32, bins // inner)[:, None] * inner
    lo = lax.iota(jnp.int32, inner)[:, None]
    scale = 2.0 * math.pi / period
    angle_hi = jnp.mod(hi * shifts, period).astype(jnp.float32) * scale
    angle_lo = jnp.mod(lo * shifts, period).astype(jnp.float32) * scale
    cos_hi, sin_hi = jnp.cos(angle_hi)[:, None, :], jnp.sin(angle_hi)[:, None, :]
    cos_lo, sin_lo = jnp.cos(angle_lo)[None, :, :], jnp.sin(angle_lo)[None, :, :]
    cos_t = (cos_hi * cos_lo - sin_hi * sin_lo).reshape(bins, lags)
    sin_t = (sin_hi * cos_lo + cos_hi * sin_lo).reshape(bins, lags)
    return cos_t * factor, -sin_t * factor


def whiten(block, quality):
    values = block.astype(jnp.float32)
    bins = values.shape[-1] // 2
    energy = jnp.sum(values * values, axis=-1) / bins
    weights = quality.astype(jnp.float32)[None, :] / jnp.sqrt(energy + 1e-06)
    return (values * weights[:, :, None]).astype(jnp.bfloat16)


def cross_spectra(sources, receivers):
    bins = sources.shape[-1] // 2
    sr = sources[:, None, :, :bins].astype(jnp.float32)
    si = sources[:, None, :, bins:].astype(jnp.float32)
    rr = receivers[:, :, None, :bins].astype(jnp.float32)
    ri = receivers[:, :, None, bins:].astype(jnp.float32)
    real_part = jnp.sum(sr * rr + si * ri, axis=0)
    imag_part = jnp.sum(sr * ri - si * rr, axis=0)
    return real_part, imag_part


def greet(axis, n, me):
    barrier = pltpu.get_barrier_semaphore()
    for k in range(1, n):
        pl.semaphore_signal(barrier, inc=1, device_id={axis: (me + k) % n},
                            device_id_type=pl.DeviceIdType.MESH)
    pl.semaphore_wait(barrier, n - 1)


def all_to_all(axis, n, me, rows_of, landing, send_sem, recv_sem):
    copies = []
    for k in range(1, n):
        peer = (me + k) % n
        copy = pltpu.make_async_remote_copy(
            src_ref=rows_of(peer), dst_ref=landing.at[me], send_sem=send_sem.at[k],
            recv_sem=recv_sem.at[me], device_id={axis: peer},
            device_id_type=pl.DeviceIdType.MESH)
        copy.start()
        copies.append(copy)
    for copy in copies:
        copy.wait_send()
    for k in range(1, n):
        source = (me + n - k) % n
        pltpu.make_async_remote_copy(
            src_ref=landing.at[source], dst_ref=landing.at[source], send_sem=send_sem.at[k],
            recv_sem=recv_sem.at[source], device_id={axis: source},
            device_id_type=pl.DeviceIdType.MESH).wait_recv()


def broadcast_kernel(axis, n, x_ref, o_ref, parts, mine, gathered, sems):
    me = lax.axis_index(axis)
    width = x_ref.shape[1] // n

    def columns(peer):
        return x_ref.at[:, pl.ds(pl.multiple_of(peer * width, width), width)]

    parts[me] = columns(me)[...]
    greet(axis, n, me)
    all_to_all(axis, n, me, columns, parts, sems.at[0], sems.at[1])
    mine[...] = jnp.sum(parts[...].astype(jnp.float32), axis=0).astype(mine.dtype)
    gathered[me] = mine[...]
    all_to_all(axis, n, me, lambda peer: mine, gathered, sems.at[2], sems.at[3])
    for peer in range(n):
        o_ref[:, peer * width:(peer + 1) * width] = gathered[peer]


def reduce_kernel(axis, n, x_ref, o_ref, parts, sems):
    me = lax.axis_index(axis)
    height = x_ref.shape[0] // n

    def rows(peer):
        return x_ref.at[pl.ds(pl.multiple_of(peer * height, height), height)]

    parts[me] = rows(me)[...]
    greet(axis, n, me)
    all_to_all(axis, n, me, rows, parts, sems.at[0], sems.at[1])
    total = jnp.sum(parts[...], axis=0).reshape(o_ref.shape)
    o_ref[...] = total.astype(o_ref.dtype)


def broadcast_sum(value, axis):
    n = lax.axis_size(axis)
    chunk = (value.shape[0], value.shape[1] // n)
    return pl.pallas_call(
        functools.partial(broadcast_kernel, axis, n),
        out_shape=jax.ShapeDtypeStruct(value.shape, value.dtype),
        in_specs=[pl.BlockSpec(memory_space=pltpu.VMEM)],
        out_specs=pl.BlockSpec(memory_space=pltpu.VMEM),
        scratch_shapes=[pltpu.VMEM((n,) + chunk, value.dtype), pltpu.VMEM(chunk, value.dtype),
                        pltpu.VMEM((n,) + chunk, value.dtype), pltpu.SemaphoreType.DMA((4, n))],
        compiler_params=pltpu.CompilerParams(collective_id=0, has_side_effects=True),
    )(value)


def start_all_to_all(axis, n, rows_of, landing, send_sem, recv_sem):
    me = lax.axis_index(axis)
    copies = []
    for k in range(1, n):
        peer = (me + k) % n
        copy = pltpu.make_async_remote_copy(
            src_ref=rows_of(peer), dst_ref=landing.at[me], send_sem=send_sem.at[k],
            recv_sem=recv_sem.at[me], device_id={axis: peer},
            device_id_type=pl.DeviceIdType.MESH)
        copy.start()
        copies.append(copy)

    def wait():
        for copy in copies:
            copy.wait_send()
        for k in range(1, n):
            source = (me + n - k) % n
            pltpu.make_async_remote_copy(
                src_ref=landing.at[source], dst_ref=landing.at[source], send_sem=send_sem.at[k],
                recv_sem=recv_sem.at[source], device_id={axis: source},
                device_id_type=pl.DeviceIdType.MESH).wait_recv()

    return wait


def columns_of(ref, n):
    width = ref.shape[1] // n
    return lambda peer: ref.at[:, pl.ds(pl.multiple_of(peer * width, width), width)]


def whiten_broadcast_kernel(axis, n, per_group, spec_ref, q_ref, sb_ref, o_ref, w_ref,
                            send, parts, mine, gathered, sems):
    me = lax.axis_index(axis)
    windows, channels, width = spec_ref.shape
    bins = width // 2
    steps = sb_ref.shape[0]

    channel = lax.broadcasted_iota(jnp.int32, (channels, 1), 0)
    quality = jnp.zeros((channels, 1), jnp.float32)
    for c in range(channels):
        quality = jnp.where(channel == c, q_ref[c].astype(jnp.float32), quality)

    def weighted(w):
        values = spec_ref[w].astype(jnp.float32)
        energy = jnp.sum(values * values, axis=-1, keepdims=True) / bins
        return values * (quality / jnp.sqrt(energy + 1e-06))

    for w in range(windows):
        block = weighted(w)
        for k in range(steps):
            kept = jnp.zeros((SRC, width), jnp.float32)
            for b in range(per_group):
                hit = me * per_group + b == sb_ref[k]
                kept = kept + jnp.where(hit, block[b * SRC:(b + 1) * SRC], 0.0)
            row = (k * windows + w) * SRC
            send[row:row + SRC, :] = kept.astype(send.dtype)
    greet(axis, n, me)
    columns = columns_of(send, n)
    parts[me] = columns(me)[...]
    wait = start_all_to_all(axis, n, columns, parts, sems.at[0], sems.at[1])
    for w in range(windows):
        w_ref[w] = weighted(w).astype(w_ref.dtype)
    wait()
    mine[...] = jnp.sum(parts[...].astype(jnp.float32), axis=0).astype(mine.dtype)
    gathered[me] = mine[...]
    wait = start_all_to_all(axis, n, lambda peer: mine, gathered, sems.at[2], sems.at[3])
    wait()
    piece = mine.shape[1]
    for peer in range(n):
        o_ref[:, peer * piece:(peer + 1) * piece] = gathered[peer]


def whiten_broadcast(spectra, quality, source_block, axis):
    n = lax.axis_size(axis)
    windows, channels, width = spectra.shape
    rows = source_block.shape[0] * windows * SRC
    chunk = (rows, width // n)
    vmem = pl.BlockSpec(memory_space=pltpu.VMEM)
    return pl.pallas_call(
        functools.partial(whiten_broadcast_kernel, axis, n, channels // SRC),
        out_shape=(jax.ShapeDtypeStruct((rows, width), jnp.bfloat16),
                   jax.ShapeDtypeStruct(spectra.shape, jnp.bfloat16)),
        in_specs=[vmem, pl.BlockSpec(memory_space=pltpu.SMEM), pl.BlockSpec(memory_space=pltpu.SMEM)],
        out_specs=(vmem, vmem),
        scratch_shapes=[pltpu.VMEM((rows, width), jnp.bfloat16),
                        pltpu.VMEM((n,) + chunk, jnp.bfloat16), pltpu.VMEM(chunk, jnp.bfloat16),
                        pltpu.VMEM((n,) + chunk, jnp.bfloat16), pltpu.SemaphoreType.DMA((4, n))],
        compiler_params=pltpu.CompilerParams(collective_id=0, has_side_effects=True),
    )(spectra, quality, source_block)


def scatter_sum(rows, axis, shape, dtype):
    n = lax.axis_size(axis)
    chunk = (rows.shape[0] // n, rows.shape[1])
    return pl.pallas_call(
        functools.partial(reduce_kernel, axis, n),
        out_shape=jax.ShapeDtypeStruct(shape, dtype),
        in_specs=[pl.BlockSpec(memory_space=pltpu.VMEM)],
        out_specs=pl.BlockSpec(memory_space=pltpu.VMEM),
        scratch_shapes=[pltpu.VMEM((n,) + chunk, rows.dtype), pltpu.SemaphoreType.DMA((2, n))],
        compiler_params=pltpu.CompilerParams(collective_id=1, has_side_effects=True),
    )(rows)


def body(spectra, quality, source_block):
    window_count, channel_count, row_width = spectra.shape
    bins = row_width // 2
    total_windows = window_count * lax.axis_size("win")
    cos_t, sin_t = lag_table(bins, L, 1.0 / math.sqrt(row_width * total_windows))
    sources, whitened = whiten_broadcast(spectra, quality, source_block, "chan")
    sources = sources.reshape(STEPS, window_count, SRC, row_width)
    win_size = lax.axis_size("win")
    per_dest = channel_count // win_size
    reals, imags = [], []
    for step in range(STEPS):
        real_part, imag_part = cross_spectra(sources[step], whitened)
        reals.append(real_part.reshape(win_size, per_dest, SRC, bins))
        imags.append(imag_part.reshape(win_size, per_dest, SRC, bins))
    rows = channel_count * SRC * STEPS
    real_rows = jnp.stack(reals, axis=1).reshape(rows, bins)
    imag_rows = jnp.stack(imags, axis=1).reshape(rows, bins)
    out = jnp.dot(
        real_rows, cos_t, precision=lax.Precision.HIGH, preferred_element_type=jnp.float32
    )
    out = out + jnp.dot(
        imag_rows, sin_t, precision=lax.Precision.HIGH, preferred_element_type=jnp.float32
    )
    return scatter_sum(out, "win", (STEPS, per_dest, SRC, L), jnp.bfloat16)


def solution(mesh):
    return jax.shard_map(
        body,
        mesh=mesh,
        in_specs=(P("win", "chan", None), P("chan"), P()),
        out_specs=P(None, ("chan", "win"), None, None),
        check_vma=False,
    )
```

```python
import functools
import math

import jax
import jax.numpy as jnp
from jax import lax
from jax.experimental import pallas as pl
from jax.experimental.pallas import tpu as pltpu
from jax.sharding import PartitionSpec as P

L = 512
SRC = 8
STEPS = 2


def from_root(value, axis, source):
    kept = jnp.where(lax.axis_index(axis) == source, value, 0).astype(value.dtype)
    return lax.psum(kept, axis)


def lag_table(bins, lags, factor):
    inner = 64
    period = 2 * bins
    shifts = lax.iota(jnp.int32, lags)[None, :] - lags // 2
    hi = lax.iota(jnp.int32, bins // inner)[:, None] * inner
    lo = lax.iota(jnp.int32, inner)[:, None]
    scale = 2.0 * math.pi / period
    angle_hi = jnp.mod(hi * shifts, period).astype(jnp.float32) * scale
    angle_lo = jnp.mod(lo * shifts, period).astype(jnp.float32) * scale
    cos_hi, sin_hi = jnp.cos(angle_hi)[:, None, :], jnp.sin(angle_hi)[:, None, :]
    cos_lo, sin_lo = jnp.cos(angle_lo)[None, :, :], jnp.sin(angle_lo)[None, :, :]
    cos_t = (cos_hi * cos_lo - sin_hi * sin_lo).reshape(bins, lags)
    sin_t = (sin_hi * cos_lo + cos_hi * sin_lo).reshape(bins, lags)
    return cos_t * factor, -sin_t * factor


def whiten(block, quality):
    values = block.astype(jnp.float32)
    bins = values.shape[-1] // 2
    energy = jnp.sum(values * values, axis=-1) / bins
    weights = quality.astype(jnp.float32)[None, :] / jnp.sqrt(energy + 1e-06)
    return (values * weights[:, :, None]).astype(jnp.bfloat16)


def cross_spectra(sources, receivers):
    bins = sources.shape[-1] // 2
    sr = sources[:, None, :, :bins].astype(jnp.float32)
    si = sources[:, None, :, bins:].astype(jnp.float32)
    rr = receivers[:, :, None, :bins].astype(jnp.float32)
    ri = receivers[:, :, None, bins:].astype(jnp.float32)
    real_part = jnp.sum(sr * rr + si * ri, axis=0)
    imag_part = jnp.sum(sr * ri - si * rr, axis=0)
    return real_part, imag_part


def greet(axis, n, me):
    barrier = pltpu.get_barrier_semaphore()
    for k in range(1, n):
        pl.semaphore_signal(barrier, inc=1, device_id={axis: (me + k) % n},
                            device_id_type=pl.DeviceIdType.MESH)
    pl.semaphore_wait(barrier, n - 1)


def all_to_all(axis, n, me, rows_of, landing, send_sem, recv_sem):
    copies = []
    for k in range(1, n):
        peer = (me + k) % n
        copy = pltpu.make_async_remote_copy(
            src_ref=rows_of(peer), dst_ref=landing.at[me], send_sem=send_sem.at[k],
            recv_sem=recv_sem.at[me], device_id={axis: peer},
            device_id_type=pl.DeviceIdType.MESH)
        copy.start()
        copies.append(copy)
    for copy in copies:
        copy.wait_send()
    for k in range(1, n):
        source = (me + n - k) % n
        pltpu.make_async_remote_copy(
            src_ref=landing.at[source], dst_ref=landing.at[source], send_sem=send_sem.at[k],
            recv_sem=recv_sem.at[source], device_id={axis: source},
            device_id_type=pl.DeviceIdType.MESH).wait_recv()


def broadcast_kernel(axis, n, x_ref, o_ref, parts, mine, gathered, sems):
    me = lax.axis_index(axis)
    width = x_ref.shape[1] // n

    def columns(peer):
        return x_ref.at[:, pl.ds(pl.multiple_of(peer * width, width), width)]

    parts[me] = columns(me)[...]
    greet(axis, n, me)
    all_to_all(axis, n, me, columns, parts, sems.at[0], sems.at[1])
    mine[...] = jnp.sum(parts[...].astype(jnp.float32), axis=0).astype(mine.dtype)
    gathered[me] = mine[...]
    all_to_all(axis, n, me, lambda peer: mine, gathered, sems.at[2], sems.at[3])
    for peer in range(n):
        o_ref[:, peer * width:(peer + 1) * width] = gathered[peer]


def reduce_kernel(axis, n, x_ref, o_ref, parts, sems):
    me = lax.axis_index(axis)
    height = x_ref.shape[0] // n

    def rows(peer):
        return x_ref.at[pl.ds(pl.multiple_of(peer * height, height), height)]

    parts[me] = rows(me)[...]
    greet(axis, n, me)
    all_to_all(axis, n, me, rows, parts, sems.at[0], sems.at[1])
    total = jnp.sum(parts[...], axis=0).reshape(o_ref.shape)
    o_ref[...] = total.astype(o_ref.dtype)


def broadcast_sum(value, axis):
    n = lax.axis_size(axis)
    chunk = (value.shape[0], value.shape[1] // n)
    return pl.pallas_call(
        functools.partial(broadcast_kernel, axis, n),
        out_shape=jax.ShapeDtypeStruct(value.shape, value.dtype),
        in_specs=[pl.BlockSpec(memory_space=pltpu.VMEM)],
        out_specs=pl.BlockSpec(memory_space=pltpu.VMEM),
        scratch_shapes=[pltpu.VMEM((n,) + chunk, value.dtype), pltpu.VMEM(chunk, value.dtype),
                        pltpu.VMEM((n,) + chunk, value.dtype), pltpu.SemaphoreType.DMA((4, n))],
        compiler_params=pltpu.CompilerParams(collective_id=0, has_side_effects=True),
    )(value)


def start_all_to_all(axis, n, rows_of, landing, send_sem, recv_sem):
    me = lax.axis_index(axis)
    copies = []
    for k in range(1, n):
        peer = (me + k) % n
        copy = pltpu.make_async_remote_copy(
            src_ref=rows_of(peer), dst_ref=landing.at[me], send_sem=send_sem.at[k],
            recv_sem=recv_sem.at[me], device_id={axis: peer},
            device_id_type=pl.DeviceIdType.MESH)
        copy.start()
        copies.append(copy)

    def wait():
        for copy in copies:
            copy.wait_send()
        for k in range(1, n):
            source = (me + n - k) % n
            pltpu.make_async_remote_copy(
                src_ref=landing.at[source], dst_ref=landing.at[source], send_sem=send_sem.at[k],
                recv_sem=recv_sem.at[source], device_id={axis: source},
                device_id_type=pl.DeviceIdType.MESH).wait_recv()

    return wait


def columns_of(ref, n):
    width = ref.shape[1] // n
    return lambda peer: ref.at[:, pl.ds(pl.multiple_of(peer * width, width), width)]


def whiten_broadcast_kernel(axis, n, per_group, factor, spec_ref, q_ref, sb_ref, o_ref, w_ref,
                            cos_ref, sin_ref, send, parts, mine, gathered, sems):
    me = lax.axis_index(axis)
    windows, channels, width = spec_ref.shape
    bins = width // 2
    steps = sb_ref.shape[0]

    channel = lax.broadcasted_iota(jnp.int32, (channels, 1), 0)
    quality = jnp.zeros((channels, 1), jnp.float32)
    for c in range(channels):
        quality = jnp.where(channel == c, q_ref[c].astype(jnp.float32), quality)

    def weighted(w):
        values = spec_ref[w].astype(jnp.float32)
        energy = jnp.sum(values * values, axis=-1, keepdims=True) / bins
        return values * (quality / jnp.sqrt(energy + 1e-06))

    for w in range(windows):
        block = weighted(w)
        for k in range(steps):
            kept = jnp.zeros((SRC, width), jnp.float32)
            for b in range(per_group):
                hit = me * per_group + b == sb_ref[k]
                kept = kept + jnp.where(hit, block[b * SRC:(b + 1) * SRC], 0.0)
            row = (k * windows + w) * SRC
            send[row:row + SRC, :] = kept.astype(send.dtype)
    greet(axis, n, me)
    columns = columns_of(send, n)
    parts[me] = columns(me)[...]
    wait = start_all_to_all(axis, n, columns, parts, sems.at[0], sems.at[1])
    for w in range(windows):
        w_ref[w] = weighted(w).astype(w_ref.dtype)
    wait()
    mine[...] = jnp.sum(parts[...].astype(jnp.float32), axis=0).astype(mine.dtype)
    gathered[me] = mine[...]
    wait = start_all_to_all(axis, n, lambda peer: mine, gathered, sems.at[2], sems.at[3])
    cos_t, sin_t = lag_table(bins, L, factor)
    cos_ref[...] = cos_t
    sin_ref[...] = sin_t
    wait()
    piece = mine.shape[1]
    for peer in range(n):
        o_ref[:, peer * piece:(peer + 1) * piece] = gathered[peer]


def whiten_broadcast(spectra, quality, source_block, axis, factor):
    n = lax.axis_size(axis)
    windows, channels, width = spectra.shape
    rows = source_block.shape[0] * windows * SRC
    chunk = (rows, width // n)
    vmem = pl.BlockSpec(memory_space=pltpu.VMEM)
    return pl.pallas_call(
        functools.partial(whiten_broadcast_kernel, axis, n, channels // SRC, factor),
        out_shape=(jax.ShapeDtypeStruct((rows, width), jnp.bfloat16),
                   jax.ShapeDtypeStruct(spectra.shape, jnp.bfloat16))
        + (jax.ShapeDtypeStruct((width // 2, L), jnp.float32),) * 2,
        in_specs=[vmem, pl.BlockSpec(memory_space=pltpu.SMEM), pl.BlockSpec(memory_space=pltpu.SMEM)],
        out_specs=(vmem,) * 4,
        scratch_shapes=[pltpu.VMEM((rows, width), jnp.bfloat16),
                        pltpu.VMEM((n,) + chunk, jnp.bfloat16), pltpu.VMEM(chunk, jnp.bfloat16),
                        pltpu.VMEM((n,) + chunk, jnp.bfloat16), pltpu.SemaphoreType.DMA((4, n))],
        compiler_params=pltpu.CompilerParams(collective_id=0, has_side_effects=True),
    )(spectra, quality, source_block)


def scatter_sum(rows, axis, shape, dtype):
    n = lax.axis_size(axis)
    chunk = (rows.shape[0] // n, rows.shape[1])
    return pl.pallas_call(
        functools.partial(reduce_kernel, axis, n),
        out_shape=jax.ShapeDtypeStruct(shape, dtype),
        in_specs=[pl.BlockSpec(memory_space=pltpu.VMEM)],
        out_specs=pl.BlockSpec(memory_space=pltpu.VMEM),
        scratch_shapes=[pltpu.VMEM((n,) + chunk, rows.dtype), pltpu.SemaphoreType.DMA((2, n))],
        compiler_params=pltpu.CompilerParams(collective_id=1, has_side_effects=True),
    )(rows)


def body(spectra, quality, source_block):
    window_count, channel_count, row_width = spectra.shape
    bins = row_width // 2
    total_windows = window_count * lax.axis_size("win")
    sources, whitened, cos_t, sin_t = whiten_broadcast(
        spectra, quality, source_block, "chan", 1.0 / math.sqrt(row_width * total_windows))
    sources = sources.reshape(STEPS, window_count, SRC, row_width)
    win_size = lax.axis_size("win")
    per_dest = channel_count // win_size
    reals, imags = [], []
    for step in range(STEPS):
        real_part, imag_part = cross_spectra(sources[step], whitened)
        reals.append(real_part.reshape(win_size, per_dest, SRC, bins))
        imags.append(imag_part.reshape(win_size, per_dest, SRC, bins))
    rows = channel_count * SRC * STEPS
    real_rows = jnp.stack(reals, axis=1).reshape(rows, bins)
    imag_rows = jnp.stack(imags, axis=1).reshape(rows, bins)
    out = jnp.dot(
        real_rows, cos_t, precision=lax.Precision.HIGH, preferred_element_type=jnp.float32
    )
    out = out + jnp.dot(
        imag_rows, sin_t, precision=lax.Precision.HIGH, preferred_element_type=jnp.float32
    )
    return scatter_sum(out, "win", (STEPS, per_dest, SRC, L), jnp.bfloat16)


def solution(mesh):
    return jax.shard_map(
        body,
        mesh=mesh,
        in_specs=(P("win", "chan", None), P("chan"), P()),
        out_specs=P(None, ("chan", "win"), None, None),
        check_vma=False,
    )
```

```python
import functools
import math

import jax
import jax.numpy as jnp
from jax import lax
from jax.experimental import pallas as pl
from jax.experimental.pallas import tpu as pltpu
from jax.sharding import PartitionSpec as P

L = 512
SRC = 8
STEPS = 2


def from_root(value, axis, source):
    kept = jnp.where(lax.axis_index(axis) == source, value, 0).astype(value.dtype)
    return lax.psum(kept, axis)


def lag_table(bins, lags, factor):
    inner = 64
    period = 2 * bins
    shifts = lax.iota(jnp.int32, lags)[None, :] - lags // 2
    hi = lax.iota(jnp.int32, bins // inner)[:, None] * inner
    lo = lax.iota(jnp.int32, inner)[:, None]
    scale = 2.0 * math.pi / period
    angle_hi = jnp.mod(hi * shifts, period).astype(jnp.float32) * scale
    angle_lo = jnp.mod(lo * shifts, period).astype(jnp.float32) * scale
    cos_hi, sin_hi = jnp.cos(angle_hi)[:, None, :], jnp.sin(angle_hi)[:, None, :]
    cos_lo, sin_lo = jnp.cos(angle_lo)[None, :, :], jnp.sin(angle_lo)[None, :, :]
    cos_t = (cos_hi * cos_lo - sin_hi * sin_lo).reshape(bins, lags)
    sin_t = (sin_hi * cos_lo + cos_hi * sin_lo).reshape(bins, lags)
    return cos_t * factor, -sin_t * factor


def whiten(block, quality):
    values = block.astype(jnp.float32)
    bins = values.shape[-1] // 2
    energy = jnp.sum(values * values, axis=-1) / bins
    weights = quality.astype(jnp.float32)[None, :] / jnp.sqrt(energy + 1e-06)
    return (values * weights[:, :, None]).astype(jnp.bfloat16)


def cross_spectra(sources, receivers):
    bins = sources.shape[-1] // 2
    sr = sources[:, None, :, :bins].astype(jnp.float32)
    si = sources[:, None, :, bins:].astype(jnp.float32)
    rr = receivers[:, :, None, :bins].astype(jnp.float32)
    ri = receivers[:, :, None, bins:].astype(jnp.float32)
    real_part = jnp.sum(sr * rr + si * ri, axis=0)
    imag_part = jnp.sum(sr * ri - si * rr, axis=0)
    return real_part, imag_part


def greet(axis, n, me):
    barrier = pltpu.get_barrier_semaphore()
    for k in range(1, n):
        pl.semaphore_signal(barrier, inc=1, device_id={axis: (me + k) % n},
                            device_id_type=pl.DeviceIdType.MESH)
    pl.semaphore_wait(barrier, n - 1)


def all_to_all(axis, n, me, rows_of, landing, send_sem, recv_sem):
    copies = []
    for k in range(1, n):
        peer = (me + k) % n
        copy = pltpu.make_async_remote_copy(
            src_ref=rows_of(peer), dst_ref=landing.at[me], send_sem=send_sem.at[k],
            recv_sem=recv_sem.at[me], device_id={axis: peer},
            device_id_type=pl.DeviceIdType.MESH)
        copy.start()
        copies.append(copy)
    for copy in copies:
        copy.wait_send()
    for k in range(1, n):
        source = (me + n - k) % n
        pltpu.make_async_remote_copy(
            src_ref=landing.at[source], dst_ref=landing.at[source], send_sem=send_sem.at[k],
            recv_sem=recv_sem.at[source], device_id={axis: source},
            device_id_type=pl.DeviceIdType.MESH).wait_recv()


def broadcast_kernel(axis, n, x_ref, o_ref, parts, mine, gathered, sems):
    me = lax.axis_index(axis)
    width = x_ref.shape[1] // n

    def columns(peer):
        return x_ref.at[:, pl.ds(pl.multiple_of(peer * width, width), width)]

    parts[me] = columns(me)[...]
    greet(axis, n, me)
    all_to_all(axis, n, me, columns, parts, sems.at[0], sems.at[1])
    mine[...] = jnp.sum(parts[...].astype(jnp.float32), axis=0).astype(mine.dtype)
    gathered[me] = mine[...]
    all_to_all(axis, n, me, lambda peer: mine, gathered, sems.at[2], sems.at[3])
    for peer in range(n):
        o_ref[:, peer * width:(peer + 1) * width] = gathered[peer]


def reduce_kernel(axis, n, x_ref, o_ref, parts, sems, own_sem):
    me = lax.axis_index(axis)
    height = x_ref.shape[0] // n

    def rows(peer):
        return x_ref.at[pl.ds(pl.multiple_of(peer * height, height), height)]

    own = pltpu.make_async_copy(rows(me), parts.at[me], own_sem.at[0])
    own.start()
    greet(axis, n, me)
    all_to_all(axis, n, me, rows, parts, sems.at[0], sems.at[1])
    own.wait()
    total = jnp.sum(parts[...], axis=0).reshape(o_ref.shape)
    o_ref[...] = total.astype(o_ref.dtype)


def broadcast_sum(value, axis):
    n = lax.axis_size(axis)
    chunk = (value.shape[0], value.shape[1] // n)
    return pl.pallas_call(
        functools.partial(broadcast_kernel, axis, n),
        out_shape=jax.ShapeDtypeStruct(value.shape, value.dtype),
        in_specs=[pl.BlockSpec(memory_space=pltpu.VMEM)],
        out_specs=pl.BlockSpec(memory_space=pltpu.VMEM),
        scratch_shapes=[pltpu.VMEM((n,) + chunk, value.dtype), pltpu.VMEM(chunk, value.dtype),
                        pltpu.VMEM((n,) + chunk, value.dtype), pltpu.SemaphoreType.DMA((4, n))],
        compiler_params=pltpu.CompilerParams(collective_id=0, has_side_effects=True),
    )(value)


def start_all_to_all(axis, n, rows_of, landing, send_sem, recv_sem):
    me = lax.axis_index(axis)
    copies = []
    for k in range(1, n):
        peer = (me + k) % n
        copy = pltpu.make_async_remote_copy(
            src_ref=rows_of(peer), dst_ref=landing.at[me], send_sem=send_sem.at[k],
            recv_sem=recv_sem.at[me], device_id={axis: peer},
            device_id_type=pl.DeviceIdType.MESH)
        copy.start()
        copies.append(copy)

    def wait():
        for copy in copies:
            copy.wait_send()
        for k in range(1, n):
            source = (me + n - k) % n
            pltpu.make_async_remote_copy(
                src_ref=landing.at[source], dst_ref=landing.at[source], send_sem=send_sem.at[k],
                recv_sem=recv_sem.at[source], device_id={axis: source},
                device_id_type=pl.DeviceIdType.MESH).wait_recv()

    return wait


def columns_of(ref, n):
    width = ref.shape[1] // n
    return lambda peer: ref.at[:, pl.ds(pl.multiple_of(peer * width, width), width)]


def whiten_broadcast_kernel(axis, n, per_group, spec_ref, q_ref, sb_ref, o_ref, w_ref,
                            send, parts, mine, gathered, sems):
    me = lax.axis_index(axis)
    windows, channels, width = spec_ref.shape
    bins = width // 2
    steps = sb_ref.shape[0]

    channel = lax.broadcasted_iota(jnp.int32, (channels, 1), 0)
    quality = jnp.zeros((channels, 1), jnp.float32)
    for c in range(channels):
        quality = jnp.where(channel == c, q_ref[c].astype(jnp.float32), quality)

    def weighted(w):
        values = spec_ref[w].astype(jnp.float32)
        energy = jnp.sum(values * values, axis=-1, keepdims=True) / bins
        return values * (quality / jnp.sqrt(energy + 1e-06))

    for w in range(windows):
        block = weighted(w)
        for k in range(steps):
            kept = jnp.zeros((SRC, width), jnp.float32)
            for b in range(per_group):
                hit = me * per_group + b == sb_ref[k]
                kept = kept + jnp.where(hit, block[b * SRC:(b + 1) * SRC], 0.0)
            row = (k * windows + w) * SRC
            send[row:row + SRC, :] = kept.astype(send.dtype)
    greet(axis, n, me)
    columns = columns_of(send, n)
    parts[me] = columns(me)[...]
    wait = start_all_to_all(axis, n, columns, parts, sems.at[0], sems.at[1])
    for w in range(windows):
        w_ref[w] = weighted(w).astype(w_ref.dtype)
    wait()
    mine[...] = jnp.sum(parts[...].astype(jnp.float32), axis=0).astype(mine.dtype)
    gathered[me] = mine[...]
    wait = start_all_to_all(axis, n, lambda peer: mine, gathered, sems.at[2], sems.at[3])
    wait()
    piece = mine.shape[1]
    for peer in range(n):
        o_ref[:, peer * piece:(peer + 1) * piece] = gathered[peer]


def whiten_broadcast(spectra, quality, source_block, axis):
    n = lax.axis_size(axis)
    windows, channels, width = spectra.shape
    rows = source_block.shape[0] * windows * SRC
    chunk = (rows, width // n)
    vmem = pl.BlockSpec(memory_space=pltpu.VMEM)
    return pl.pallas_call(
        functools.partial(whiten_broadcast_kernel, axis, n, channels // SRC),
        out_shape=(jax.ShapeDtypeStruct((rows, width), jnp.bfloat16),
                   jax.ShapeDtypeStruct(spectra.shape, jnp.bfloat16)),
        in_specs=[vmem, pl.BlockSpec(memory_space=pltpu.SMEM), pl.BlockSpec(memory_space=pltpu.SMEM)],
        out_specs=(vmem, vmem),
        scratch_shapes=[pltpu.VMEM((rows, width), jnp.bfloat16),
                        pltpu.VMEM((n,) + chunk, jnp.bfloat16), pltpu.VMEM(chunk, jnp.bfloat16),
                        pltpu.VMEM((n,) + chunk, jnp.bfloat16), pltpu.SemaphoreType.DMA((4, n))],
        compiler_params=pltpu.CompilerParams(collective_id=0, has_side_effects=True),
    )(spectra, quality, source_block)


def scatter_sum(rows, axis, shape, dtype):
    n = lax.axis_size(axis)
    chunk = (rows.shape[0] // n, rows.shape[1])
    return pl.pallas_call(
        functools.partial(reduce_kernel, axis, n),
        out_shape=jax.ShapeDtypeStruct(shape, dtype),
        in_specs=[pl.BlockSpec(memory_space=pl.ANY)],
        out_specs=pl.BlockSpec(memory_space=pltpu.VMEM),
        scratch_shapes=[pltpu.VMEM((n,) + chunk, rows.dtype), pltpu.SemaphoreType.DMA((2, n)),
                        pltpu.SemaphoreType.DMA((1,))],
        compiler_params=pltpu.CompilerParams(collective_id=1, has_side_effects=True),
    )(rows)


def body(spectra, quality, source_block):
    window_count, channel_count, row_width = spectra.shape
    bins = row_width // 2
    total_windows = window_count * lax.axis_size("win")
    cos_t, sin_t = lag_table(bins, L, 1.0 / math.sqrt(row_width * total_windows))
    sources, whitened = whiten_broadcast(spectra, quality, source_block, "chan")
    sources = sources.reshape(STEPS, window_count, SRC, row_width)
    win_size = lax.axis_size("win")
    per_dest = channel_count // win_size
    reals, imags = [], []
    for step in range(STEPS):
        real_part, imag_part = cross_spectra(sources[step], whitened)
        reals.append(real_part.reshape(win_size, per_dest, SRC, bins))
        imags.append(imag_part.reshape(win_size, per_dest, SRC, bins))
    rows = channel_count * SRC * STEPS
    real_rows = jnp.stack(reals, axis=1).reshape(rows, bins)
    imag_rows = jnp.stack(imags, axis=1).reshape(rows, bins)
    out = jnp.dot(
        real_rows, cos_t, precision=lax.Precision.HIGH, preferred_element_type=jnp.float32
    )
    out = out + jnp.dot(
        imag_rows, sin_t, precision=lax.Precision.HIGH, preferred_element_type=jnp.float32
    )
    return scatter_sum(out, "win", (STEPS, per_dest, SRC, L), jnp.bfloat16)


def solution(mesh):
    return jax.shard_map(
        body,
        mesh=mesh,
        in_specs=(P("win", "chan", None), P("chan"), P()),
        out_specs=P(None, ("chan", "win"), None, None),
        check_vma=False,
    )
```

```python
import functools
import math

import jax
import jax.numpy as jnp
from jax import lax
from jax.experimental import pallas as pl
from jax.experimental.pallas import tpu as pltpu
from jax.sharding import PartitionSpec as P

L = 512
SRC = 8
STEPS = 2


def from_root(value, axis, source):
    kept = jnp.where(lax.axis_index(axis) == source, value, 0).astype(value.dtype)
    return lax.psum(kept, axis)


def lag_table(bins, lags, factor):
    inner = 64
    period = 2 * bins
    shifts = lax.iota(jnp.int32, lags)[None, :] - lags // 2
    hi = lax.iota(jnp.int32, bins // inner)[:, None] * inner
    lo = lax.iota(jnp.int32, inner)[:, None]
    scale = 2.0 * math.pi / period
    angle_hi = jnp.mod(hi * shifts, period).astype(jnp.float32) * scale
    angle_lo = jnp.mod(lo * shifts, period).astype(jnp.float32) * scale
    cos_hi, sin_hi = jnp.cos(angle_hi)[:, None, :], jnp.sin(angle_hi)[:, None, :]
    cos_lo, sin_lo = jnp.cos(angle_lo)[None, :, :], jnp.sin(angle_lo)[None, :, :]
    cos_t = (cos_hi * cos_lo - sin_hi * sin_lo).reshape(bins, lags)
    sin_t = (sin_hi * cos_lo + cos_hi * sin_lo).reshape(bins, lags)
    return cos_t * factor, -sin_t * factor


def whiten(block, quality):
    values = block.astype(jnp.float32)
    bins = values.shape[-1] // 2
    energy = jnp.sum(values * values, axis=-1) / bins
    weights = quality.astype(jnp.float32)[None, :] / jnp.sqrt(energy + 1e-06)
    return (values * weights[:, :, None]).astype(jnp.bfloat16)


def cross_spectra(sources, receivers):
    bins = sources.shape[-1] // 2
    sr = sources[:, None, :, :bins].astype(jnp.float32)
    si = sources[:, None, :, bins:].astype(jnp.float32)
    rr = receivers[:, :, None, :bins].astype(jnp.float32)
    ri = receivers[:, :, None, bins:].astype(jnp.float32)
    real_part = jnp.sum(sr * rr + si * ri, axis=0)
    imag_part = jnp.sum(sr * ri - si * rr, axis=0)
    return real_part, imag_part


def shifts(n):
    order = []
    for k in range(1, n // 2 + 1):
        order += [k] if k == n - k else [k, n - k]
    return order


def greet(axis, n, me):
    barrier = pltpu.get_barrier_semaphore()
    for k in range(1, n):
        pl.semaphore_signal(barrier, inc=1, device_id={axis: (me + k) % n},
                            device_id_type=pl.DeviceIdType.MESH)
    pl.semaphore_wait(barrier, n - 1)


def all_to_all(axis, n, me, rows_of, landing, send_sem, recv_sem):
    copies = []
    for k in shifts(n):
        peer = (me + k) % n
        copy = pltpu.make_async_remote_copy(
            src_ref=rows_of(peer), dst_ref=landing.at[me], send_sem=send_sem.at[k],
            recv_sem=recv_sem.at[me], device_id={axis: peer},
            device_id_type=pl.DeviceIdType.MESH)
        copy.start()
        copies.append(copy)
    for copy in copies:
        copy.wait_send()
    for k in range(1, n):
        source = (me + n - k) % n
        pltpu.make_async_remote_copy(
            src_ref=landing.at[source], dst_ref=landing.at[source], send_sem=send_sem.at[k],
            recv_sem=recv_sem.at[source], device_id={axis: source},
            device_id_type=pl.DeviceIdType.MESH).wait_recv()


def broadcast_kernel(axis, n, x_ref, o_ref, parts, mine, gathered, sems):
    me = lax.axis_index(axis)
    width = x_ref.shape[1] // n

    def columns(peer):
        return x_ref.at[:, pl.ds(pl.multiple_of(peer * width, width), width)]

    parts[me] = columns(me)[...]
    greet(axis, n, me)
    all_to_all(axis, n, me, columns, parts, sems.at[0], sems.at[1])
    mine[...] = jnp.sum(parts[...].astype(jnp.float32), axis=0).astype(mine.dtype)
    gathered[me] = mine[...]
    all_to_all(axis, n, me, lambda peer: mine, gathered, sems.at[2], sems.at[3])
    for peer in range(n):
        o_ref[:, peer * width:(peer + 1) * width] = gathered[peer]


def reduce_kernel(axis, n, x_ref, o_ref, parts, sems, own_sem):
    me = lax.axis_index(axis)
    height = x_ref.shape[0] // n

    def rows(peer):
        return x_ref.at[pl.ds(pl.multiple_of(peer * height, height), height)]

    own = pltpu.make_async_copy(rows(me), parts.at[me], own_sem.at[0])
    own.start()
    greet(axis, n, me)
    all_to_all(axis, n, me, rows, parts, sems.at[0], sems.at[1])
    own.wait()
    total = jnp.sum(parts[...], axis=0).reshape(o_ref.shape)
    o_ref[...] = total.astype(o_ref.dtype)


def broadcast_sum(value, axis):
    n = lax.axis_size(axis)
    chunk = (value.shape[0], value.shape[1] // n)
    return pl.pallas_call(
        functools.partial(broadcast_kernel, axis, n),
        out_shape=jax.ShapeDtypeStruct(value.shape, value.dtype),
        in_specs=[pl.BlockSpec(memory_space=pltpu.VMEM)],
        out_specs=pl.BlockSpec(memory_space=pltpu.VMEM),
        scratch_shapes=[pltpu.VMEM((n,) + chunk, value.dtype), pltpu.VMEM(chunk, value.dtype),
                        pltpu.VMEM((n,) + chunk, value.dtype), pltpu.SemaphoreType.DMA((4, n))],
        compiler_params=pltpu.CompilerParams(collective_id=0, has_side_effects=True),
    )(value)


def start_all_to_all(axis, n, rows_of, landing, send_sem, recv_sem):
    me = lax.axis_index(axis)
    copies = []
    for k in shifts(n):
        peer = (me + k) % n
        copy = pltpu.make_async_remote_copy(
            src_ref=rows_of(peer), dst_ref=landing.at[me], send_sem=send_sem.at[k],
            recv_sem=recv_sem.at[me], device_id={axis: peer},
            device_id_type=pl.DeviceIdType.MESH)
        copy.start()
        copies.append(copy)

    def wait():
        for copy in copies:
            copy.wait_send()
        for k in range(1, n):
            source = (me + n - k) % n
            pltpu.make_async_remote_copy(
                src_ref=landing.at[source], dst_ref=landing.at[source], send_sem=send_sem.at[k],
                recv_sem=recv_sem.at[source], device_id={axis: source},
                device_id_type=pl.DeviceIdType.MESH).wait_recv()

    return wait


def columns_of(ref, n):
    width = ref.shape[1] // n
    return lambda peer: ref.at[:, pl.ds(pl.multiple_of(peer * width, width), width)]


def whiten_broadcast_kernel(axis, n, per_group, spec_ref, q_ref, sb_ref, o_ref, w_ref,
                            send, parts, mine, gathered, sems):
    me = lax.axis_index(axis)
    windows, channels, width = spec_ref.shape
    bins = width // 2
    steps = sb_ref.shape[0]

    channel = lax.broadcasted_iota(jnp.int32, (channels, 1), 0)
    quality = jnp.zeros((channels, 1), jnp.float32)
    for c in range(channels):
        quality = jnp.where(channel == c, q_ref[c].astype(jnp.float32), quality)

    def weighted(w):
        values = spec_ref[w].astype(jnp.float32)
        energy = jnp.sum(values * values, axis=-1, keepdims=True) / bins
        return values * (quality / jnp.sqrt(energy + 1e-06))

    for w in range(windows):
        block = weighted(w)
        for k in range(steps):
            kept = jnp.zeros((SRC, width), jnp.float32)
            for b in range(per_group):
                hit = me * per_group + b == sb_ref[k]
                kept = kept + jnp.where(hit, block[b * SRC:(b + 1) * SRC], 0.0)
            row = (k * windows + w) * SRC
            send[row:row + SRC, :] = kept.astype(send.dtype)
    greet(axis, n, me)
    columns = columns_of(send, n)
    parts[me] = columns(me)[...]
    wait = start_all_to_all(axis, n, columns, parts, sems.at[0], sems.at[1])
    for w in range(windows):
        w_ref[w] = weighted(w).astype(w_ref.dtype)
    wait()
    mine[...] = jnp.sum(parts[...].astype(jnp.float32), axis=0).astype(mine.dtype)
    gathered[me] = mine[...]
    wait = start_all_to_all(axis, n, lambda peer: mine, gathered, sems.at[2], sems.at[3])
    wait()
    piece = mine.shape[1]
    for peer in range(n):
        o_ref[:, peer * piece:(peer + 1) * piece] = gathered[peer]


def whiten_broadcast(spectra, quality, source_block, axis):
    n = lax.axis_size(axis)
    windows, channels, width = spectra.shape
    rows = source_block.shape[0] * windows * SRC
    chunk = (rows, width // n)
    vmem = pl.BlockSpec(memory_space=pltpu.VMEM)
    return pl.pallas_call(
        functools.partial(whiten_broadcast_kernel, axis, n, channels // SRC),
        out_shape=(jax.ShapeDtypeStruct((rows, width), jnp.bfloat16),
                   jax.ShapeDtypeStruct(spectra.shape, jnp.bfloat16)),
        in_specs=[vmem, pl.BlockSpec(memory_space=pltpu.SMEM), pl.BlockSpec(memory_space=pltpu.SMEM)],
        out_specs=(vmem, vmem),
        scratch_shapes=[pltpu.VMEM((rows, width), jnp.bfloat16),
                        pltpu.VMEM((n,) + chunk, jnp.bfloat16), pltpu.VMEM(chunk, jnp.bfloat16),
                        pltpu.VMEM((n,) + chunk, jnp.bfloat16), pltpu.SemaphoreType.DMA((4, n))],
        compiler_params=pltpu.CompilerParams(collective_id=0, has_side_effects=True),
    )(spectra, quality, source_block)


def scatter_sum(rows, axis, shape, dtype):
    n = lax.axis_size(axis)
    chunk = (rows.shape[0] // n, rows.shape[1])
    return pl.pallas_call(
        functools.partial(reduce_kernel, axis, n),
        out_shape=jax.ShapeDtypeStruct(shape, dtype),
        in_specs=[pl.BlockSpec(memory_space=pl.ANY)],
        out_specs=pl.BlockSpec(memory_space=pltpu.VMEM),
        scratch_shapes=[pltpu.VMEM((n,) + chunk, rows.dtype), pltpu.SemaphoreType.DMA((2, n)),
                        pltpu.SemaphoreType.DMA((1,))],
        compiler_params=pltpu.CompilerParams(collective_id=1, has_side_effects=True),
    )(rows)


def body(spectra, quality, source_block):
    window_count, channel_count, row_width = spectra.shape
    bins = row_width // 2
    total_windows = window_count * lax.axis_size("win")
    cos_t, sin_t = lag_table(bins, L, 1.0 / math.sqrt(row_width * total_windows))
    sources, whitened = whiten_broadcast(spectra, quality, source_block, "chan")
    sources = sources.reshape(STEPS, window_count, SRC, row_width)
    win_size = lax.axis_size("win")
    per_dest = channel_count // win_size
    reals, imags = [], []
    for step in range(STEPS):
        real_part, imag_part = cross_spectra(sources[step], whitened)
        reals.append(real_part.reshape(win_size, per_dest, SRC, bins))
        imags.append(imag_part.reshape(win_size, per_dest, SRC, bins))
    rows = channel_count * SRC * STEPS
    real_rows = jnp.stack(reals, axis=1).reshape(rows, bins)
    imag_rows = jnp.stack(imags, axis=1).reshape(rows, bins)
    out = jnp.dot(
        real_rows, cos_t, precision=lax.Precision.HIGH, preferred_element_type=jnp.float32
    )
    out = out + jnp.dot(
        imag_rows, sin_t, precision=lax.Precision.HIGH, preferred_element_type=jnp.float32
    )
    return scatter_sum(out, "win", (STEPS, per_dest, SRC, L), jnp.bfloat16)


def solution(mesh):
    return jax.shard_map(
        body,
        mesh=mesh,
        in_specs=(P("win", "chan", None), P("chan"), P()),
        out_specs=P(None, ("chan", "win"), None, None),
        check_vma=False,
    )
```

```python
import functools
import math

import jax
import jax.numpy as jnp
from jax import lax
from jax.experimental import pallas as pl
from jax.experimental.pallas import tpu as pltpu
from jax.sharding import PartitionSpec as P

L = 512
SRC = 8
STEPS = 2


def from_root(value, axis, source):
    kept = jnp.where(lax.axis_index(axis) == source, value, 0).astype(value.dtype)
    return lax.psum(kept, axis)


def lag_table(bins, lags, factor):
    inner = 64
    period = 2 * bins
    shifts = lax.iota(jnp.int32, lags)[None, :] - lags // 2
    hi = lax.iota(jnp.int32, bins // inner)[:, None] * inner
    lo = lax.iota(jnp.int32, inner)[:, None]
    scale = 2.0 * math.pi / period
    angle_hi = jnp.mod(hi * shifts, period).astype(jnp.float32) * scale
    angle_lo = jnp.mod(lo * shifts, period).astype(jnp.float32) * scale
    cos_hi, sin_hi = jnp.cos(angle_hi)[:, None, :], jnp.sin(angle_hi)[:, None, :]
    cos_lo, sin_lo = jnp.cos(angle_lo)[None, :, :], jnp.sin(angle_lo)[None, :, :]
    cos_t = (cos_hi * cos_lo - sin_hi * sin_lo).reshape(bins, lags)
    sin_t = (sin_hi * cos_lo + cos_hi * sin_lo).reshape(bins, lags)
    return cos_t * factor, -sin_t * factor


def whiten(block, quality):
    values = block.astype(jnp.float32)
    bins = values.shape[-1] // 2
    energy = jnp.sum(values * values, axis=-1) / bins
    weights = quality.astype(jnp.float32)[None, :] / jnp.sqrt(energy + 1e-06)
    return (values * weights[:, :, None]).astype(jnp.bfloat16)


def cross_spectra(sources, receivers):
    bins = sources.shape[-1] // 2
    sr = sources[:, None, :, :bins].astype(jnp.float32)
    si = sources[:, None, :, bins:].astype(jnp.float32)
    rr = receivers[:, :, None, :bins].astype(jnp.float32)
    ri = receivers[:, :, None, bins:].astype(jnp.float32)
    real_part = jnp.sum(sr * rr + si * ri, axis=0)
    imag_part = jnp.sum(sr * ri - si * rr, axis=0)
    return real_part, imag_part


def greet(axis, n, me):
    barrier = pltpu.get_barrier_semaphore()
    for k in range(1, n):
        pl.semaphore_signal(barrier, inc=1, device_id={axis: (me + k) % n},
                            device_id_type=pl.DeviceIdType.MESH)
    pl.semaphore_wait(barrier, n - 1)


def all_to_all(axis, n, me, rows_of, landing, send_sem, recv_sem):
    copies = []
    for k in range(1, n):
        peer = (me + k) % n
        copy = pltpu.make_async_remote_copy(
            src_ref=rows_of(peer), dst_ref=landing.at[me], send_sem=send_sem.at[k],
            recv_sem=recv_sem.at[me], device_id={axis: peer},
            device_id_type=pl.DeviceIdType.MESH)
        copy.start()
        copies.append(copy)
    for copy in copies:
        copy.wait_send()
    for k in range(1, n):
        source = (me + n - k) % n
        pltpu.make_async_remote_copy(
            src_ref=landing.at[source], dst_ref=landing.at[source], send_sem=send_sem.at[k],
            recv_sem=recv_sem.at[source], device_id={axis: source},
            device_id_type=pl.DeviceIdType.MESH).wait_recv()


def broadcast_kernel(axis, n, x_ref, o_ref, parts, mine, gathered, sems):
    me = lax.axis_index(axis)
    width = x_ref.shape[1] // n

    def columns(peer):
        return x_ref.at[:, pl.ds(pl.multiple_of(peer * width, width), width)]

    parts[me] = columns(me)[...]
    greet(axis, n, me)
    all_to_all(axis, n, me, columns, parts, sems.at[0], sems.at[1])
    mine[...] = jnp.sum(parts[...].astype(jnp.float32), axis=0).astype(mine.dtype)
    gathered[me] = mine[...]
    all_to_all(axis, n, me, lambda peer: mine, gathered, sems.at[2], sems.at[3])
    for peer in range(n):
        o_ref[:, peer * width:(peer + 1) * width] = gathered[peer]


def reduce_kernel(axis, n, x_ref, o_ref, parts, sems, own_sem):
    me = lax.axis_index(axis)
    height = x_ref.shape[0] // n

    def rows(peer):
        return x_ref.at[pl.ds(pl.multiple_of(peer * height, height), height)]

    own = pltpu.make_async_copy(rows(me), parts.at[me], own_sem.at[0])
    own.start()
    greet(axis, n, me)
    all_to_all(axis, n, me, rows, parts, sems.at[0], sems.at[1])
    own.wait()
    total = jnp.sum(parts[...], axis=0).reshape(o_ref.shape)
    o_ref[...] = total.astype(o_ref.dtype)


def pair_ring_kernel(axis, ring, x_ref, o_ref, mine, land_a, send_b, land_b, sems_a, sems_b,
                     own_sems):
    me = lax.axis_index(axis)
    z0, xl = me // 2, me % 2
    height = x_ref.shape[0] // (2 * ring)

    def rows(dest):
        return x_ref.at[pl.ds(pl.multiple_of(dest * height, height), height)]

    own = []
    for z in range(ring):
        copy = pltpu.make_async_copy(rows(2 * z + xl), mine.at[z], own_sems.at[z])
        copy.start()
        own.append(copy)
    barrier = pltpu.get_barrier_semaphore()
    peers = [2 * z0 + 1 - xl] + [2 * ((z0 + k) % ring) + xl for k in range(1, ring)]
    for peer in peers:
        pl.semaphore_signal(barrier, inc=1, device_id={axis: peer},
                            device_id_type=pl.DeviceIdType.MESH)
    pl.semaphore_wait(barrier, len(peers))
    copies = []
    for z in range(ring):
        copy = pltpu.make_async_remote_copy(
            src_ref=rows(2 * z + 1 - xl), dst_ref=land_a.at[z], send_sem=sems_a.at[0, z],
            recv_sem=sems_a.at[1, z], device_id={axis: peers[0]},
            device_id_type=pl.DeviceIdType.MESH)
        copy.start()
        copies.append(copy)
    for copy in copies:
        copy.wait_send()
    for copy in copies:
        copy.wait_recv()
    for copy in own:
        copy.wait()
    send_b[...] = mine[...] + land_a[...]
    copies = []
    for k in range(1, ring):
        zp = (z0 + k) % ring
        copy = pltpu.make_async_remote_copy(
            src_ref=send_b.at[zp], dst_ref=land_b.at[z0], send_sem=sems_b.at[0, k],
            recv_sem=sems_b.at[1, z0], device_id={axis: 2 * zp + xl},
            device_id_type=pl.DeviceIdType.MESH)
        copy.start()
        copies.append(copy)
    for copy in copies:
        copy.wait_send()
    for k in range(1, ring):
        zs = (z0 + ring - k) % ring
        pltpu.make_async_remote_copy(
            src_ref=land_b.at[zs], dst_ref=land_b.at[zs], send_sem=sems_b.at[0, k],
            recv_sem=sems_b.at[1, zs], device_id={axis: 2 * zs + xl},
            device_id_type=pl.DeviceIdType.MESH).wait_recv()
    land_b[z0] = send_b[z0]
    total = jnp.sum(land_b[...], axis=0).reshape(o_ref.shape)
    o_ref[...] = total.astype(o_ref.dtype)


def pair_ring_sum(rows, axis, shape, dtype):
    n = lax.axis_size(axis)
    ring = n // 2
    chunk = (ring, rows.shape[0] // n, rows.shape[1])
    return pl.pallas_call(
        functools.partial(pair_ring_kernel, axis, ring),
        out_shape=jax.ShapeDtypeStruct(shape, dtype),
        in_specs=[pl.BlockSpec(memory_space=pl.ANY)],
        out_specs=pl.BlockSpec(memory_space=pltpu.VMEM),
        scratch_shapes=[pltpu.VMEM(chunk, rows.dtype)] * 4
        + [pltpu.SemaphoreType.DMA((2, ring)), pltpu.SemaphoreType.DMA((2, ring)),
           pltpu.SemaphoreType.DMA((ring,))],
        compiler_params=pltpu.CompilerParams(collective_id=1, has_side_effects=True),
    )(rows)


def broadcast_sum(value, axis):
    n = lax.axis_size(axis)
    chunk = (value.shape[0], value.shape[1] // n)
    return pl.pallas_call(
        functools.partial(broadcast_kernel, axis, n),
        out_shape=jax.ShapeDtypeStruct(value.shape, value.dtype),
        in_specs=[pl.BlockSpec(memory_space=pltpu.VMEM)],
        out_specs=pl.BlockSpec(memory_space=pltpu.VMEM),
        scratch_shapes=[pltpu.VMEM((n,) + chunk, value.dtype), pltpu.VMEM(chunk, value.dtype),
                        pltpu.VMEM((n,) + chunk, value.dtype), pltpu.SemaphoreType.DMA((4, n))],
        compiler_params=pltpu.CompilerParams(collective_id=0, has_side_effects=True),
    )(value)


def start_all_to_all(axis, n, rows_of, landing, send_sem, recv_sem):
    me = lax.axis_index(axis)
    copies = []
    for k in range(1, n):
        peer = (me + k) % n
        copy = pltpu.make_async_remote_copy(
            src_ref=rows_of(peer), dst_ref=landing.at[me], send_sem=send_sem.at[k],
            recv_sem=recv_sem.at[me], device_id={axis: peer},
            device_id_type=pl.DeviceIdType.MESH)
        copy.start()
        copies.append(copy)

    def wait():
        for copy in copies:
            copy.wait_send()
        for k in range(1, n):
            source = (me + n - k) % n
            pltpu.make_async_remote_copy(
                src_ref=landing.at[source], dst_ref=landing.at[source], send_sem=send_sem.at[k],
                recv_sem=recv_sem.at[source], device_id={axis: source},
                device_id_type=pl.DeviceIdType.MESH).wait_recv()

    return wait


def columns_of(ref, n):
    width = ref.shape[1] // n
    return lambda peer: ref.at[:, pl.ds(pl.multiple_of(peer * width, width), width)]


def whiten_broadcast_kernel(axis, n, per_group, spec_ref, q_ref, sb_ref, o_ref, w_ref,
                            send, parts, mine, gathered, sems):
    me = lax.axis_index(axis)
    windows, channels, width = spec_ref.shape
    bins = width // 2
    steps = sb_ref.shape[0]

    channel = lax.broadcasted_iota(jnp.int32, (channels, 1), 0)
    quality = jnp.zeros((channels, 1), jnp.float32)
    for c in range(channels):
        quality = jnp.where(channel == c, q_ref[c].astype(jnp.float32), quality)

    def weighted(w):
        values = spec_ref[w].astype(jnp.float32)
        energy = jnp.sum(values * values, axis=-1, keepdims=True) / bins
        return values * (quality / jnp.sqrt(energy + 1e-06))

    for w in range(windows):
        block = weighted(w)
        for k in range(steps):
            kept = jnp.zeros((SRC, width), jnp.float32)
            for b in range(per_group):
                hit = me * per_group + b == sb_ref[k]
                kept = kept + jnp.where(hit, block[b * SRC:(b + 1) * SRC], 0.0)
            row = (k * windows + w) * SRC
            send[row:row + SRC, :] = kept.astype(send.dtype)
    greet(axis, n, me)
    columns = columns_of(send, n)
    parts[me] = columns(me)[...]
    wait = start_all_to_all(axis, n, columns, parts, sems.at[0], sems.at[1])
    for w in range(windows):
        w_ref[w] = weighted(w).astype(w_ref.dtype)
    wait()
    mine[...] = jnp.sum(parts[...].astype(jnp.float32), axis=0).astype(mine.dtype)
    gathered[me] = mine[...]
    wait = start_all_to_all(axis, n, lambda peer: mine, gathered, sems.at[2], sems.at[3])
    wait()
    piece = mine.shape[1]
    for peer in range(n):
        o_ref[:, peer * piece:(peer + 1) * piece] = gathered[peer]


def whiten_broadcast(spectra, quality, source_block, axis):
    n = lax.axis_size(axis)
    windows, channels, width = spectra.shape
    rows = source_block.shape[0] * windows * SRC
    chunk = (rows, width // n)
    vmem = pl.BlockSpec(memory_space=pltpu.VMEM)
    return pl.pallas_call(
        functools.partial(whiten_broadcast_kernel, axis, n, channels // SRC),
        out_shape=(jax.ShapeDtypeStruct((rows, width), jnp.bfloat16),
                   jax.ShapeDtypeStruct(spectra.shape, jnp.bfloat16)),
        in_specs=[vmem, pl.BlockSpec(memory_space=pltpu.SMEM), pl.BlockSpec(memory_space=pltpu.SMEM)],
        out_specs=(vmem, vmem),
        scratch_shapes=[pltpu.VMEM((rows, width), jnp.bfloat16),
                        pltpu.VMEM((n,) + chunk, jnp.bfloat16), pltpu.VMEM(chunk, jnp.bfloat16),
                        pltpu.VMEM((n,) + chunk, jnp.bfloat16), pltpu.SemaphoreType.DMA((4, n))],
        compiler_params=pltpu.CompilerParams(collective_id=0, has_side_effects=True),
    )(spectra, quality, source_block)


def scatter_sum(rows, axis, shape, dtype):
    n = lax.axis_size(axis)
    chunk = (rows.shape[0] // n, rows.shape[1])
    return pl.pallas_call(
        functools.partial(reduce_kernel, axis, n),
        out_shape=jax.ShapeDtypeStruct(shape, dtype),
        in_specs=[pl.BlockSpec(memory_space=pl.ANY)],
        out_specs=pl.BlockSpec(memory_space=pltpu.VMEM),
        scratch_shapes=[pltpu.VMEM((n,) + chunk, rows.dtype), pltpu.SemaphoreType.DMA((2, n)),
                        pltpu.SemaphoreType.DMA((1,))],
        compiler_params=pltpu.CompilerParams(collective_id=1, has_side_effects=True),
    )(rows)


def body(spectra, quality, source_block):
    window_count, channel_count, row_width = spectra.shape
    bins = row_width // 2
    total_windows = window_count * lax.axis_size("win")
    cos_t, sin_t = lag_table(bins, L, 1.0 / math.sqrt(row_width * total_windows))
    sources, whitened = whiten_broadcast(spectra, quality, source_block, "chan")
    sources = sources.reshape(STEPS, window_count, SRC, row_width)
    win_size = lax.axis_size("win")
    per_dest = channel_count // win_size
    reals, imags = [], []
    for step in range(STEPS):
        real_part, imag_part = cross_spectra(sources[step], whitened)
        reals.append(real_part.reshape(win_size, per_dest, SRC, bins))
        imags.append(imag_part.reshape(win_size, per_dest, SRC, bins))
    rows = channel_count * SRC * STEPS
    real_rows = jnp.stack(reals, axis=1).reshape(rows, bins)
    imag_rows = jnp.stack(imags, axis=1).reshape(rows, bins)
    out = jnp.dot(
        real_rows, cos_t, precision=lax.Precision.HIGH, preferred_element_type=jnp.float32
    )
    out = out + jnp.dot(
        imag_rows, sin_t, precision=lax.Precision.HIGH, preferred_element_type=jnp.float32
    )
    return pair_ring_sum(out, "win", (STEPS, per_dest, SRC, L), jnp.bfloat16)


def solution(mesh):
    return jax.shard_map(
        body,
        mesh=mesh,
        in_specs=(P("win", "chan", None), P("chan"), P()),
        out_specs=P(None, ("chan", "win"), None, None),
        check_vma=False,
    )
```

```python
import functools
import math

import jax
import jax.numpy as jnp
from jax import lax
from jax.experimental import pallas as pl
from jax.experimental.pallas import tpu as pltpu
from jax.sharding import PartitionSpec as P

L = 512
SRC = 8
STEPS = 2


def from_root(value, axis, source):
    kept = jnp.where(lax.axis_index(axis) == source, value, 0).astype(value.dtype)
    return lax.psum(kept, axis)


def lag_table(bins, lags, factor):
    inner = 64
    period = 2 * bins
    shifts = lax.iota(jnp.int32, lags)[None, :] - lags // 2
    hi = lax.iota(jnp.int32, bins // inner)[:, None] * inner
    lo = lax.iota(jnp.int32, inner)[:, None]
    scale = 2.0 * math.pi / period
    angle_hi = jnp.mod(hi * shifts, period).astype(jnp.float32) * scale
    angle_lo = jnp.mod(lo * shifts, period).astype(jnp.float32) * scale
    cos_hi, sin_hi = jnp.cos(angle_hi)[:, None, :], jnp.sin(angle_hi)[:, None, :]
    cos_lo, sin_lo = jnp.cos(angle_lo)[None, :, :], jnp.sin(angle_lo)[None, :, :]
    cos_t = (cos_hi * cos_lo - sin_hi * sin_lo).reshape(bins, lags)
    sin_t = (sin_hi * cos_lo + cos_hi * sin_lo).reshape(bins, lags)
    return cos_t * factor, -sin_t * factor


def whiten(block, quality):
    values = block.astype(jnp.float32)
    bins = values.shape[-1] // 2
    energy = jnp.sum(values * values, axis=-1) / bins
    weights = quality.astype(jnp.float32)[None, :] / jnp.sqrt(energy + 1e-06)
    return (values * weights[:, :, None]).astype(jnp.bfloat16)


def cross_spectra(sources, receivers):
    bins = sources.shape[-1] // 2
    sr = sources[:, None, :, :bins].astype(jnp.float32)
    si = sources[:, None, :, bins:].astype(jnp.float32)
    rr = receivers[:, :, None, :bins].astype(jnp.float32)
    ri = receivers[:, :, None, bins:].astype(jnp.float32)
    real_part = jnp.sum(sr * rr + si * ri, axis=0)
    imag_part = jnp.sum(sr * ri - si * rr, axis=0)
    return real_part, imag_part


def greet(axis, n, me):
    barrier = pltpu.get_barrier_semaphore()
    for k in range(1, n):
        pl.semaphore_signal(barrier, inc=1, device_id={axis: (me + k) % n},
                            device_id_type=pl.DeviceIdType.MESH)
    pl.semaphore_wait(barrier, n - 1)


def all_to_all(axis, n, me, rows_of, landing, send_sem, recv_sem):
    copies = []
    for k in range(1, n):
        peer = (me + k) % n
        copy = pltpu.make_async_remote_copy(
            src_ref=rows_of(peer), dst_ref=landing.at[me], send_sem=send_sem.at[k],
            recv_sem=recv_sem.at[me], device_id={axis: peer},
            device_id_type=pl.DeviceIdType.MESH)
        copy.start()
        copies.append(copy)
    for copy in copies:
        copy.wait_send()
    for k in range(1, n):
        source = (me + n - k) % n
        pltpu.make_async_remote_copy(
            src_ref=landing.at[source], dst_ref=landing.at[source], send_sem=send_sem.at[k],
            recv_sem=recv_sem.at[source], device_id={axis: source},
            device_id_type=pl.DeviceIdType.MESH).wait_recv()


def broadcast_kernel(axis, n, x_ref, o_ref, parts, mine, gathered, sems):
    me = lax.axis_index(axis)
    width = x_ref.shape[1] // n

    def columns(peer):
        return x_ref.at[:, pl.ds(pl.multiple_of(peer * width, width), width)]

    parts[me] = columns(me)[...]
    greet(axis, n, me)
    all_to_all(axis, n, me, columns, parts, sems.at[0], sems.at[1])
    mine[...] = jnp.sum(parts[...].astype(jnp.float32), axis=0).astype(mine.dtype)
    gathered[me] = mine[...]
    all_to_all(axis, n, me, lambda peer: mine, gathered, sems.at[2], sems.at[3])
    for peer in range(n):
        o_ref[:, peer * width:(peer + 1) * width] = gathered[peer]


def reduce_kernel(axis, n, x_ref, o_ref, parts, sems, own_sem):
    me = lax.axis_index(axis)
    height = x_ref.shape[0] // n

    def rows(peer):
        return x_ref.at[pl.ds(pl.multiple_of(peer * height, height), height)]

    own = pltpu.make_async_copy(rows(me), parts.at[me], own_sem.at[0])
    own.start()
    greet(axis, n, me)
    half = height // 2
    copies = []
    for k in range(1, n):
        peer = (me + k) % n
        for h in range(2):
            copy = pltpu.make_async_remote_copy(
                src_ref=rows(peer).at[pl.ds(h * half, half)],
                dst_ref=parts.at[me, pl.ds(h * half, half)], send_sem=sems.at[0, k, h],
                recv_sem=sems.at[1, me, h], device_id={axis: peer},
                device_id_type=pl.DeviceIdType.MESH)
            copy.start()
            copies.append(copy)
    for copy in copies:
        copy.wait_send()
    for k in range(1, n):
        source = (me + n - k) % n
        for h in range(2):
            pltpu.make_async_remote_copy(
                src_ref=parts.at[source, pl.ds(h * half, half)],
                dst_ref=parts.at[source, pl.ds(h * half, half)], send_sem=sems.at[0, k, h],
                recv_sem=sems.at[1, source, h], device_id={axis: source},
                device_id_type=pl.DeviceIdType.MESH).wait_recv()
    own.wait()
    total = jnp.sum(parts[...], axis=0).reshape(o_ref.shape)
    o_ref[...] = total.astype(o_ref.dtype)


def broadcast_sum(value, axis):
    n = lax.axis_size(axis)
    chunk = (value.shape[0], value.shape[1] // n)
    return pl.pallas_call(
        functools.partial(broadcast_kernel, axis, n),
        out_shape=jax.ShapeDtypeStruct(value.shape, value.dtype),
        in_specs=[pl.BlockSpec(memory_space=pltpu.VMEM)],
        out_specs=pl.BlockSpec(memory_space=pltpu.VMEM),
        scratch_shapes=[pltpu.VMEM((n,) + chunk, value.dtype), pltpu.VMEM(chunk, value.dtype),
                        pltpu.VMEM((n,) + chunk, value.dtype), pltpu.SemaphoreType.DMA((4, n))],
        compiler_params=pltpu.CompilerParams(collective_id=0, has_side_effects=True),
    )(value)


def start_all_to_all(axis, n, rows_of, landing, send_sem, recv_sem):
    me = lax.axis_index(axis)
    copies = []
    for k in range(1, n):
        peer = (me + k) % n
        copy = pltpu.make_async_remote_copy(
            src_ref=rows_of(peer), dst_ref=landing.at[me], send_sem=send_sem.at[k],
            recv_sem=recv_sem.at[me], device_id={axis: peer},
            device_id_type=pl.DeviceIdType.MESH)
        copy.start()
        copies.append(copy)

    def wait():
        for copy in copies:
            copy.wait_send()
        for k in range(1, n):
            source = (me + n - k) % n
            pltpu.make_async_remote_copy(
                src_ref=landing.at[source], dst_ref=landing.at[source], send_sem=send_sem.at[k],
                recv_sem=recv_sem.at[source], device_id={axis: source},
                device_id_type=pl.DeviceIdType.MESH).wait_recv()

    return wait


def columns_of(ref, n):
    width = ref.shape[1] // n
    return lambda peer: ref.at[:, pl.ds(pl.multiple_of(peer * width, width), width)]


def whiten_broadcast_kernel(axis, n, per_group, spec_ref, q_ref, sb_ref, o_ref, w_ref,
                            send, parts, mine, gathered, sems):
    me = lax.axis_index(axis)
    windows, channels, width = spec_ref.shape
    bins = width // 2
    steps = sb_ref.shape[0]

    channel = lax.broadcasted_iota(jnp.int32, (channels, 1), 0)
    quality = jnp.zeros((channels, 1), jnp.float32)
    for c in range(channels):
        quality = jnp.where(channel == c, q_ref[c].astype(jnp.float32), quality)

    def weighted(w):
        values = spec_ref[w].astype(jnp.float32)
        energy = jnp.sum(values * values, axis=-1, keepdims=True) / bins
        return values * (quality / jnp.sqrt(energy + 1e-06))

    for w in range(windows):
        block = weighted(w)
        for k in range(steps):
            kept = jnp.zeros((SRC, width), jnp.float32)
            for b in range(per_group):
                hit = me * per_group + b == sb_ref[k]
                kept = kept + jnp.where(hit, block[b * SRC:(b + 1) * SRC], 0.0)
            row = (k * windows + w) * SRC
            send[row:row + SRC, :] = kept.astype(send.dtype)
    greet(axis, n, me)
    columns = columns_of(send, n)
    parts[me] = columns(me)[...]
    wait = start_all_to_all(axis, n, columns, parts, sems.at[0], sems.at[1])
    for w in range(windows):
        w_ref[w] = weighted(w).astype(w_ref.dtype)
    wait()
    mine[...] = jnp.sum(parts[...].astype(jnp.float32), axis=0).astype(mine.dtype)
    gathered[me] = mine[...]
    wait = start_all_to_all(axis, n, lambda peer: mine, gathered, sems.at[2], sems.at[3])
    wait()
    piece = mine.shape[1]
    for peer in range(n):
        o_ref[:, peer * piece:(peer + 1) * piece] = gathered[peer]


def whiten_broadcast(spectra, quality, source_block, axis):
    n = lax.axis_size(axis)
    windows, channels, width = spectra.shape
    rows = source_block.shape[0] * windows * SRC
    chunk = (rows, width // n)
    vmem = pl.BlockSpec(memory_space=pltpu.VMEM)
    return pl.pallas_call(
        functools.partial(whiten_broadcast_kernel, axis, n, channels // SRC),
        out_shape=(jax.ShapeDtypeStruct((rows, width), jnp.bfloat16),
                   jax.ShapeDtypeStruct(spectra.shape, jnp.bfloat16)),
        in_specs=[vmem, pl.BlockSpec(memory_space=pltpu.SMEM), pl.BlockSpec(memory_space=pltpu.SMEM)],
        out_specs=(vmem, vmem),
        scratch_shapes=[pltpu.VMEM((rows, width), jnp.bfloat16),
                        pltpu.VMEM((n,) + chunk, jnp.bfloat16), pltpu.VMEM(chunk, jnp.bfloat16),
                        pltpu.VMEM((n,) + chunk, jnp.bfloat16), pltpu.SemaphoreType.DMA((4, n))],
        compiler_params=pltpu.CompilerParams(collective_id=0, has_side_effects=True),
    )(spectra, quality, source_block)


def scatter_sum(rows, axis, shape, dtype):
    n = lax.axis_size(axis)
    chunk = (rows.shape[0] // n, rows.shape[1])
    return pl.pallas_call(
        functools.partial(reduce_kernel, axis, n),
        out_shape=jax.ShapeDtypeStruct(shape, dtype),
        in_specs=[pl.BlockSpec(memory_space=pl.ANY)],
        out_specs=pl.BlockSpec(memory_space=pltpu.VMEM),
        scratch_shapes=[pltpu.VMEM((n,) + chunk, rows.dtype), pltpu.SemaphoreType.DMA((2, n, 2)),
                        pltpu.SemaphoreType.DMA((1,))],
        compiler_params=pltpu.CompilerParams(collective_id=1, has_side_effects=True),
    )(rows)


def body(spectra, quality, source_block):
    window_count, channel_count, row_width = spectra.shape
    bins = row_width // 2
    total_windows = window_count * lax.axis_size("win")
    cos_t, sin_t = lag_table(bins, L, 1.0 / math.sqrt(row_width * total_windows))
    sources, whitened = whiten_broadcast(spectra, quality, source_block, "chan")
    sources = sources.reshape(STEPS, window_count, SRC, row_width)
    win_size = lax.axis_size("win")
    per_dest = channel_count // win_size
    reals, imags = [], []
    for step in range(STEPS):
        real_part, imag_part = cross_spectra(sources[step], whitened)
        reals.append(real_part.reshape(win_size, per_dest, SRC, bins))
        imags.append(imag_part.reshape(win_size, per_dest, SRC, bins))
    rows = channel_count * SRC * STEPS
    real_rows = jnp.stack(reals, axis=1).reshape(rows, bins)
    imag_rows = jnp.stack(imags, axis=1).reshape(rows, bins)
    out = jnp.dot(
        real_rows, cos_t, precision=lax.Precision.HIGH, preferred_element_type=jnp.float32
    )
    out = out + jnp.dot(
        imag_rows, sin_t, precision=lax.Precision.HIGH, preferred_element_type=jnp.float32
    )
    return scatter_sum(out, "win", (STEPS, per_dest, SRC, L), jnp.bfloat16)


def solution(mesh):
    return jax.shard_map(
        body,
        mesh=mesh,
        in_specs=(P("win", "chan", None), P("chan"), P()),
        out_specs=P(None, ("chan", "win"), None, None),
        check_vma=False,
    )
```

```python
import functools
import math

import jax
import jax.numpy as jnp
from jax import lax
from jax.experimental import pallas as pl
from jax.experimental.pallas import tpu as pltpu
from jax.sharding import PartitionSpec as P

L = 512
SRC = 8
STEPS = 2


def from_root(value, axis, source):
    kept = jnp.where(lax.axis_index(axis) == source, value, 0).astype(value.dtype)
    return lax.psum(kept, axis)


def lag_table(bins, lags, factor):
    inner = 64
    period = 2 * bins
    shifts = lax.iota(jnp.int32, lags)[None, :] - lags // 2
    hi = lax.iota(jnp.int32, bins // inner)[:, None] * inner
    lo = lax.iota(jnp.int32, inner)[:, None]
    scale = 2.0 * math.pi / period
    angle_hi = jnp.mod(hi * shifts, period).astype(jnp.float32) * scale
    angle_lo = jnp.mod(lo * shifts, period).astype(jnp.float32) * scale
    cos_hi, sin_hi = jnp.cos(angle_hi)[:, None, :], jnp.sin(angle_hi)[:, None, :]
    cos_lo, sin_lo = jnp.cos(angle_lo)[None, :, :], jnp.sin(angle_lo)[None, :, :]
    cos_t = (cos_hi * cos_lo - sin_hi * sin_lo).reshape(bins, lags)
    sin_t = (sin_hi * cos_lo + cos_hi * sin_lo).reshape(bins, lags)
    return cos_t * factor, -sin_t * factor


def whiten(block, quality):
    values = block.astype(jnp.float32)
    bins = values.shape[-1] // 2
    energy = jnp.sum(values * values, axis=-1) / bins
    weights = quality.astype(jnp.float32)[None, :] / jnp.sqrt(energy + 1e-06)
    return (values * weights[:, :, None]).astype(jnp.bfloat16)


def cross_spectra(sources, receivers):
    bins = sources.shape[-1] // 2
    sr = sources[:, None, :, :bins].astype(jnp.float32)
    si = sources[:, None, :, bins:].astype(jnp.float32)
    rr = receivers[:, :, None, :bins].astype(jnp.float32)
    ri = receivers[:, :, None, bins:].astype(jnp.float32)
    real_part = jnp.sum(sr * rr + si * ri, axis=0)
    imag_part = jnp.sum(sr * ri - si * rr, axis=0)
    return real_part, imag_part


def greet(axis, n, me):
    barrier = pltpu.get_barrier_semaphore()
    for k in range(1, n):
        pl.semaphore_signal(barrier, inc=1, device_id={axis: (me + k) % n},
                            device_id_type=pl.DeviceIdType.MESH)
    pl.semaphore_wait(barrier, n - 1)


def all_to_all(axis, n, me, rows_of, landing, send_sem, recv_sem):
    copies = []
    for k in range(1, n):
        peer = (me + k) % n
        copy = pltpu.make_async_remote_copy(
            src_ref=rows_of(peer), dst_ref=landing.at[me], send_sem=send_sem.at[k],
            recv_sem=recv_sem.at[me], device_id={axis: peer},
            device_id_type=pl.DeviceIdType.MESH)
        copy.start()
        copies.append(copy)
    for copy in copies:
        copy.wait_send()
    for k in range(1, n):
        source = (me + n - k) % n
        pltpu.make_async_remote_copy(
            src_ref=landing.at[source], dst_ref=landing.at[source], send_sem=send_sem.at[k],
            recv_sem=recv_sem.at[source], device_id={axis: source},
            device_id_type=pl.DeviceIdType.MESH).wait_recv()


def broadcast_kernel(axis, n, x_ref, o_ref, parts, mine, gathered, sems):
    me = lax.axis_index(axis)
    width = x_ref.shape[1] // n

    def columns(peer):
        return x_ref.at[:, pl.ds(pl.multiple_of(peer * width, width), width)]

    parts[me] = columns(me)[...]
    greet(axis, n, me)
    all_to_all(axis, n, me, columns, parts, sems.at[0], sems.at[1])
    mine[...] = jnp.sum(parts[...].astype(jnp.float32), axis=0).astype(mine.dtype)
    gathered[me] = mine[...]
    all_to_all(axis, n, me, lambda peer: mine, gathered, sems.at[2], sems.at[3])
    for peer in range(n):
        o_ref[:, peer * width:(peer + 1) * width] = gathered[peer]


def reduce_kernel(axis, n, x_ref, o_ref, parts, sems, own_sem):
    me = lax.axis_index(axis)
    height = x_ref.shape[0] // n

    def rows(peer):
        return x_ref.at[pl.ds(pl.multiple_of(peer * height, height), height)]

    own = pltpu.make_async_copy(rows(me), parts.at[me], own_sem.at[0])
    own.start()
    greet(axis, n, me)
    all_to_all(axis, n, me, rows, parts, sems.at[0], sems.at[1])
    own.wait()
    total = jnp.sum(parts[...], axis=0).reshape(o_ref.shape)
    o_ref[...] = total.astype(o_ref.dtype)


def broadcast_sum(value, axis):
    n = lax.axis_size(axis)
    chunk = (value.shape[0], value.shape[1] // n)
    return pl.pallas_call(
        functools.partial(broadcast_kernel, axis, n),
        out_shape=jax.ShapeDtypeStruct(value.shape, value.dtype),
        in_specs=[pl.BlockSpec(memory_space=pltpu.VMEM)],
        out_specs=pl.BlockSpec(memory_space=pltpu.VMEM),
        scratch_shapes=[pltpu.VMEM((n,) + chunk, value.dtype), pltpu.VMEM(chunk, value.dtype),
                        pltpu.VMEM((n,) + chunk, value.dtype), pltpu.SemaphoreType.DMA((4, n))],
        compiler_params=pltpu.CompilerParams(collective_id=0, has_side_effects=True),
    )(value)


def start_all_to_all(axis, n, rows_of, landing, send_sem, recv_sem):
    me = lax.axis_index(axis)
    copies = []
    for k in range(1, n):
        peer = (me + k) % n
        copy = pltpu.make_async_remote_copy(
            src_ref=rows_of(peer), dst_ref=landing.at[me], send_sem=send_sem.at[k],
            recv_sem=recv_sem.at[me], device_id={axis: peer},
            device_id_type=pl.DeviceIdType.MESH)
        copy.start()
        copies.append(copy)

    def wait():
        for copy in copies:
            copy.wait_send()
        for k in range(1, n):
            source = (me + n - k) % n
            pltpu.make_async_remote_copy(
                src_ref=landing.at[source], dst_ref=landing.at[source], send_sem=send_sem.at[k],
                recv_sem=recv_sem.at[source], device_id={axis: source},
                device_id_type=pl.DeviceIdType.MESH).wait_recv()

    return wait


def columns_of(ref, n):
    width = ref.shape[1] // n
    return lambda peer: ref.at[:, pl.ds(pl.multiple_of(peer * width, width), width)]


def whiten_broadcast_kernel(axis, n, per_group, spec_ref, q_ref, sb_ref, o_ref, w_ref,
                            send, parts, mine, gathered, sems):
    me = lax.axis_index(axis)
    windows, channels, width = spec_ref.shape
    bins = width // 2
    steps = sb_ref.shape[0]

    channel = lax.broadcasted_iota(jnp.int32, (channels, 1), 0)
    quality = jnp.zeros((channels, 1), jnp.float32)
    for c in range(channels):
        quality = jnp.where(channel == c, q_ref[c].astype(jnp.float32), quality)

    def weighted(w):
        values = spec_ref[w].astype(jnp.float32)
        energy = jnp.sum(values * values, axis=-1, keepdims=True) / bins
        return values * (quality / jnp.sqrt(energy + 1e-06))

    for w in range(windows):
        block = weighted(w)
        for k in range(steps):
            kept = jnp.zeros((SRC, width), jnp.float32)
            for b in range(per_group):
                hit = me * per_group + b == sb_ref[k]
                kept = kept + jnp.where(hit, block[b * SRC:(b + 1) * SRC], 0.0)
            row = (k * windows + w) * SRC
            send[row:row + SRC, :] = kept.astype(send.dtype)
    greet(axis, n, me)
    columns = columns_of(send, n)
    parts[me] = columns(me)[...]
    wait = start_all_to_all(axis, n, columns, parts, sems.at[0], sems.at[1])
    for w in range(windows):
        w_ref[w] = weighted(w).astype(w_ref.dtype)
    wait()
    mine[...] = jnp.sum(parts[...].astype(jnp.float32), axis=0).astype(mine.dtype)
    gathered[me] = mine[...]
    wait = start_all_to_all(axis, n, lambda peer: mine, gathered, sems.at[2], sems.at[3])
    wait()
    piece = mine.shape[1]
    for peer in range(n):
        o_ref[:, peer * piece:(peer + 1) * piece] = gathered[peer]


def whiten_broadcast(spectra, quality, source_block, axis):
    n = lax.axis_size(axis)
    windows, channels, width = spectra.shape
    rows = source_block.shape[0] * windows * SRC
    chunk = (rows, width // n)
    vmem = pl.BlockSpec(memory_space=pltpu.VMEM)
    return pl.pallas_call(
        functools.partial(whiten_broadcast_kernel, axis, n, channels // SRC),
        out_shape=(jax.ShapeDtypeStruct((rows, width), jnp.bfloat16),
                   jax.ShapeDtypeStruct(spectra.shape, jnp.bfloat16)),
        in_specs=[vmem, pl.BlockSpec(memory_space=pltpu.SMEM), pl.BlockSpec(memory_space=pltpu.SMEM)],
        out_specs=(vmem, vmem),
        scratch_shapes=[pltpu.VMEM((rows, width), jnp.bfloat16),
                        pltpu.VMEM((n,) + chunk, jnp.bfloat16), pltpu.VMEM(chunk, jnp.bfloat16),
                        pltpu.VMEM((n,) + chunk, jnp.bfloat16), pltpu.SemaphoreType.DMA((4, n))],
        compiler_params=pltpu.CompilerParams(collective_id=0, has_side_effects=True),
    )(spectra, quality, source_block)


def scatter_sum(rows, axis, shape, dtype):
    n = lax.axis_size(axis)
    chunk = (rows.shape[0] // n, rows.shape[1])
    return pl.pallas_call(
        functools.partial(reduce_kernel, axis, n),
        out_shape=jax.ShapeDtypeStruct(shape, dtype),
        in_specs=[pl.BlockSpec(memory_space=pl.ANY)],
        out_specs=pl.BlockSpec(memory_space=pltpu.VMEM),
        scratch_shapes=[pltpu.VMEM((n,) + chunk, rows.dtype), pltpu.SemaphoreType.DMA((2, n)),
                        pltpu.SemaphoreType.DMA((1,))],
        compiler_params=pltpu.CompilerParams(collective_id=1, has_side_effects=True),
    )(rows)


def body(spectra, quality, source_block):
    window_count, channel_count, row_width = spectra.shape
    bins = row_width // 2
    total_windows = window_count * lax.axis_size("win")
    cos_t, sin_t = lag_table(bins, L, 1.0 / math.sqrt(row_width * total_windows))
    sources, whitened = whiten_broadcast(spectra, quality, source_block, "chan")
    sources = sources.reshape(STEPS, window_count, SRC, row_width)
    win_size = lax.axis_size("win")
    per_dest = channel_count // win_size
    reals, imags = [], []
    for step in range(STEPS):
        real_part, imag_part = cross_spectra(sources[step], whitened)
        reals.append(real_part.reshape(win_size, per_dest, SRC, bins))
        imags.append(imag_part.reshape(win_size, per_dest, SRC, bins))
    rows = channel_count * SRC * STEPS
    real_rows = jnp.stack(reals, axis=1).reshape(rows, bins)
    imag_rows = jnp.stack(imags, axis=1).reshape(rows, bins)
    out = jnp.dot(
        real_rows, cos_t, precision=lax.Precision.HIGH, preferred_element_type=jnp.float32
    )
    out = out + jnp.dot(
        imag_rows, sin_t, precision=lax.Precision.HIGH, preferred_element_type=jnp.float32
    )
    summed = scatter_sum(out, "win", (STEPS, per_dest, SRC, L), jnp.float32)
    return summed.astype(jnp.bfloat16)


def solution(mesh):
    return jax.shard_map(
        body,
        mesh=mesh,
        in_specs=(P("win", "chan", None), P("chan"), P()),
        out_specs=P(None, ("chan", "win"), None, None),
        check_vma=False,
    )
```

```python
import functools
import math

import jax
import jax.numpy as jnp
from jax import lax
from jax.experimental import pallas as pl
from jax.experimental.pallas import tpu as pltpu
from jax.sharding import PartitionSpec as P

L = 512
SRC = 8
STEPS = 2


def from_root(value, axis, source):
    kept = jnp.where(lax.axis_index(axis) == source, value, 0).astype(value.dtype)
    return lax.psum(kept, axis)


def lag_table(bins, lags, factor):
    inner = 64
    period = 2 * bins
    shifts = lax.iota(jnp.int32, lags)[None, :] - lags // 2
    hi = lax.iota(jnp.int32, bins // inner)[:, None] * inner
    lo = lax.iota(jnp.int32, inner)[:, None]
    scale = 2.0 * math.pi / period
    angle_hi = jnp.mod(hi * shifts, period).astype(jnp.float32) * scale
    angle_lo = jnp.mod(lo * shifts, period).astype(jnp.float32) * scale
    cos_hi, sin_hi = jnp.cos(angle_hi)[:, None, :], jnp.sin(angle_hi)[:, None, :]
    cos_lo, sin_lo = jnp.cos(angle_lo)[None, :, :], jnp.sin(angle_lo)[None, :, :]
    cos_t = (cos_hi * cos_lo - sin_hi * sin_lo).reshape(bins, lags)
    sin_t = (sin_hi * cos_lo + cos_hi * sin_lo).reshape(bins, lags)
    return cos_t * factor, -sin_t * factor


def whiten(block, quality):
    values = block.astype(jnp.float32)
    bins = values.shape[-1] // 2
    energy = jnp.sum(values * values, axis=-1) / bins
    weights = quality.astype(jnp.float32)[None, :] / jnp.sqrt(energy + 1e-06)
    return (values * weights[:, :, None]).astype(jnp.bfloat16)


def cross_spectra(sources, receivers):
    bins = sources.shape[-1] // 2
    sr = sources[:, None, :, :bins].astype(jnp.float32)
    si = sources[:, None, :, bins:].astype(jnp.float32)
    rr = receivers[:, :, None, :bins].astype(jnp.float32)
    ri = receivers[:, :, None, bins:].astype(jnp.float32)
    real_part = jnp.sum(sr * rr + si * ri, axis=0)
    imag_part = jnp.sum(sr * ri - si * rr, axis=0)
    return real_part, imag_part


def greet(axis, n, me):
    barrier = pltpu.get_barrier_semaphore()
    for k in range(1, n):
        pl.semaphore_signal(barrier, inc=1, device_id={axis: (me + k) % n},
                            device_id_type=pl.DeviceIdType.MESH)
    pl.semaphore_wait(barrier, n - 1)


def all_to_all(axis, n, me, rows_of, landing, send_sem, recv_sem):
    copies = []
    for k in range(1, n):
        peer = (me + k) % n
        copy = pltpu.make_async_remote_copy(
            src_ref=rows_of(peer), dst_ref=landing.at[me], send_sem=send_sem.at[k],
            recv_sem=recv_sem.at[me], device_id={axis: peer},
            device_id_type=pl.DeviceIdType.MESH)
        copy.start()
        copies.append(copy)
    for copy in copies:
        copy.wait_send()
    for k in range(1, n):
        source = (me + n - k) % n
        pltpu.make_async_remote_copy(
            src_ref=landing.at[source], dst_ref=landing.at[source], send_sem=send_sem.at[k],
            recv_sem=recv_sem.at[source], device_id={axis: source},
            device_id_type=pl.DeviceIdType.MESH).wait_recv()


def broadcast_kernel(axis, n, x_ref, o_ref, parts, mine, gathered, sems):
    me = lax.axis_index(axis)
    width = x_ref.shape[1] // n

    def columns(peer):
        return x_ref.at[:, pl.ds(pl.multiple_of(peer * width, width), width)]

    parts[me] = columns(me)[...]
    greet(axis, n, me)
    all_to_all(axis, n, me, columns, parts, sems.at[0], sems.at[1])
    mine[...] = jnp.sum(parts[...].astype(jnp.float32), axis=0).astype(mine.dtype)
    gathered[me] = mine[...]
    all_to_all(axis, n, me, lambda peer: mine, gathered, sems.at[2], sems.at[3])
    for peer in range(n):
        o_ref[:, peer * width:(peer + 1) * width] = gathered[peer]


def reduce_kernel(axis, n, x_ref, o_ref, parts, sems, own_sem):
    me = lax.axis_index(axis)
    height = x_ref.shape[0] // n

    def rows(peer):
        return x_ref.at[pl.ds(pl.multiple_of(peer * height, height), height)]

    own = pltpu.make_async_copy(rows(me), parts.at[me], own_sem.at[0])
    own.start()
    greet(axis, n, me)
    all_to_all(axis, n, me, rows, parts, sems.at[0], sems.at[1])
    own.wait()
    total = jnp.sum(parts[...], axis=0).reshape(o_ref.shape)
    o_ref[...] = total.astype(o_ref.dtype)


def broadcast_sum(value, axis):
    n = lax.axis_size(axis)
    chunk = (value.shape[0], value.shape[1] // n)
    return pl.pallas_call(
        functools.partial(broadcast_kernel, axis, n),
        out_shape=jax.ShapeDtypeStruct(value.shape, value.dtype),
        in_specs=[pl.BlockSpec(memory_space=pltpu.VMEM)],
        out_specs=pl.BlockSpec(memory_space=pltpu.VMEM),
        scratch_shapes=[pltpu.VMEM((n,) + chunk, value.dtype), pltpu.VMEM(chunk, value.dtype),
                        pltpu.VMEM((n,) + chunk, value.dtype), pltpu.SemaphoreType.DMA((4, n))],
        compiler_params=pltpu.CompilerParams(collective_id=0, has_side_effects=True),
    )(value)


def start_all_to_all(axis, n, rows_of, landing, send_sem, recv_sem):
    me = lax.axis_index(axis)
    copies = []
    for k in range(1, n):
        peer = (me + k) % n
        copy = pltpu.make_async_remote_copy(
            src_ref=rows_of(peer), dst_ref=landing.at[me], send_sem=send_sem.at[k],
            recv_sem=recv_sem.at[me], device_id={axis: peer},
            device_id_type=pl.DeviceIdType.MESH)
        copy.start()
        copies.append(copy)

    def wait():
        for copy in copies:
            copy.wait_send()
        for k in range(1, n):
            source = (me + n - k) % n
            pltpu.make_async_remote_copy(
                src_ref=landing.at[source], dst_ref=landing.at[source], send_sem=send_sem.at[k],
                recv_sem=recv_sem.at[source], device_id={axis: source},
                device_id_type=pl.DeviceIdType.MESH).wait_recv()

    return wait


def columns_of(ref, n):
    width = ref.shape[1] // n
    return lambda peer: ref.at[:, pl.ds(pl.multiple_of(peer * width, width), width)]


def whiten_broadcast_kernel(axis, n, per_group, spec_ref, q_ref, sb_ref, o_ref, w_ref,
                            send, parts, mine, gathered, sems):
    me = lax.axis_index(axis)
    windows, channels, width = spec_ref.shape
    bins = width // 2
    steps = sb_ref.shape[0]

    channel = lax.broadcasted_iota(jnp.int32, (channels, 1), 0)
    quality = jnp.zeros((channels, 1), jnp.float32)
    for c in range(channels):
        quality = jnp.where(channel == c, q_ref[c].astype(jnp.float32), quality)

    def weighted(w):
        values = spec_ref[w].astype(jnp.float32)
        energy = jnp.sum(values * values, axis=-1, keepdims=True) / bins
        return values * (quality / jnp.sqrt(energy + 1e-06))

    for w in range(windows):
        raw = spec_ref[w].astype(jnp.float32)
        for k in range(steps):
            picked = jnp.zeros((SRC, width), jnp.float32)
            gain = jnp.zeros((SRC, 1), jnp.float32)
            for b in range(per_group):
                hit = me * per_group + b == sb_ref[k]
                picked = picked + jnp.where(hit, raw[b * SRC:(b + 1) * SRC], 0.0)
                gain = gain + jnp.where(hit, quality[b * SRC:(b + 1) * SRC], 0.0)
            energy = jnp.sum(picked * picked, axis=-1, keepdims=True) / bins
            kept = picked * (gain / jnp.sqrt(energy + 1e-06))
            row = (k * windows + w) * SRC
            send[row:row + SRC, :] = kept.astype(send.dtype)
    greet(axis, n, me)
    columns = columns_of(send, n)
    parts[me] = columns(me)[...]
    wait = start_all_to_all(axis, n, columns, parts, sems.at[0], sems.at[1])
    for w in range(windows):
        w_ref[w] = weighted(w).astype(w_ref.dtype)
    wait()
    mine[...] = jnp.sum(parts[...].astype(jnp.float32), axis=0).astype(mine.dtype)
    gathered[me] = mine[...]
    wait = start_all_to_all(axis, n, lambda peer: mine, gathered, sems.at[2], sems.at[3])
    wait()
    piece = mine.shape[1]
    for peer in range(n):
        o_ref[:, peer * piece:(peer + 1) * piece] = gathered[peer]


def whiten_broadcast(spectra, quality, source_block, axis):
    n = lax.axis_size(axis)
    windows, channels, width = spectra.shape
    rows = source_block.shape[0] * windows * SRC
    chunk = (rows, width // n)
    vmem = pl.BlockSpec(memory_space=pltpu.VMEM)
    return pl.pallas_call(
        functools.partial(whiten_broadcast_kernel, axis, n, channels // SRC),
        out_shape=(jax.ShapeDtypeStruct((rows, width), jnp.bfloat16),
                   jax.ShapeDtypeStruct(spectra.shape, jnp.bfloat16)),
        in_specs=[vmem, pl.BlockSpec(memory_space=pltpu.SMEM), pl.BlockSpec(memory_space=pltpu.SMEM)],
        out_specs=(vmem, vmem),
        scratch_shapes=[pltpu.VMEM((rows, width), jnp.bfloat16),
                        pltpu.VMEM((n,) + chunk, jnp.bfloat16), pltpu.VMEM(chunk, jnp.bfloat16),
                        pltpu.VMEM((n,) + chunk, jnp.bfloat16), pltpu.SemaphoreType.DMA((4, n))],
        compiler_params=pltpu.CompilerParams(collective_id=0, has_side_effects=True),
    )(spectra, quality, source_block)


def scatter_sum(rows, axis, shape, dtype):
    n = lax.axis_size(axis)
    chunk = (rows.shape[0] // n, rows.shape[1])
    return pl.pallas_call(
        functools.partial(reduce_kernel, axis, n),
        out_shape=jax.ShapeDtypeStruct(shape, dtype),
        in_specs=[pl.BlockSpec(memory_space=pl.ANY)],
        out_specs=pl.BlockSpec(memory_space=pltpu.VMEM),
        scratch_shapes=[pltpu.VMEM((n,) + chunk, rows.dtype), pltpu.SemaphoreType.DMA((2, n)),
                        pltpu.SemaphoreType.DMA((1,))],
        compiler_params=pltpu.CompilerParams(collective_id=1, has_side_effects=True),
    )(rows)


def body(spectra, quality, source_block):
    window_count, channel_count, row_width = spectra.shape
    bins = row_width // 2
    total_windows = window_count * lax.axis_size("win")
    cos_t, sin_t = lag_table(bins, L, 1.0 / math.sqrt(row_width * total_windows))
    sources, whitened = whiten_broadcast(spectra, quality, source_block, "chan")
    sources = sources.reshape(STEPS, window_count, SRC, row_width)
    win_size = lax.axis_size("win")
    per_dest = channel_count // win_size
    reals, imags = [], []
    for step in range(STEPS):
        real_part, imag_part = cross_spectra(sources[step], whitened)
        reals.append(real_part.reshape(win_size, per_dest, SRC, bins))
        imags.append(imag_part.reshape(win_size, per_dest, SRC, bins))
    rows = channel_count * SRC * STEPS
    real_rows = jnp.stack(reals, axis=1).reshape(rows, bins)
    imag_rows = jnp.stack(imags, axis=1).reshape(rows, bins)
    out = jnp.dot(
        real_rows, cos_t, precision=lax.Precision.HIGH, preferred_element_type=jnp.float32
    )
    out = out + jnp.dot(
        imag_rows, sin_t, precision=lax.Precision.HIGH, preferred_element_type=jnp.float32
    )
    return scatter_sum(out, "win", (STEPS, per_dest, SRC, L), jnp.bfloat16)


def solution(mesh):
    return jax.shard_map(
        body,
        mesh=mesh,
        in_specs=(P("win", "chan", None), P("chan"), P()),
        out_specs=P(None, ("chan", "win"), None, None),
        check_vma=False,
    )
```

```python
import functools
import math

import jax
import jax.numpy as jnp
from jax import lax
from jax.experimental import pallas as pl
from jax.experimental.pallas import tpu as pltpu
from jax.sharding import PartitionSpec as P

L = 512
SRC = 8
STEPS = 2


def from_root(value, axis, source):
    kept = jnp.where(lax.axis_index(axis) == source, value, 0).astype(value.dtype)
    return lax.psum(kept, axis)


def lag_table(bins, lags, factor):
    inner = 64
    period = 2 * bins
    shifts = lax.iota(jnp.int32, lags)[None, :] - lags // 2
    hi = lax.iota(jnp.int32, bins // inner)[:, None] * inner
    lo = lax.iota(jnp.int32, inner)[:, None]
    scale = 2.0 * math.pi / period
    angle_hi = jnp.mod(hi * shifts, period).astype(jnp.float32) * scale
    angle_lo = jnp.mod(lo * shifts, period).astype(jnp.float32) * scale
    cos_hi, sin_hi = jnp.cos(angle_hi)[:, None, :], jnp.sin(angle_hi)[:, None, :]
    cos_lo, sin_lo = jnp.cos(angle_lo)[None, :, :], jnp.sin(angle_lo)[None, :, :]
    cos_t = (cos_hi * cos_lo - sin_hi * sin_lo).reshape(bins, lags)
    sin_t = (sin_hi * cos_lo + cos_hi * sin_lo).reshape(bins, lags)
    return cos_t * factor, -sin_t * factor


def whiten(block, quality):
    values = block.astype(jnp.float32)
    bins = values.shape[-1] // 2
    energy = jnp.sum(values * values, axis=-1) / bins
    weights = quality.astype(jnp.float32)[None, :] / jnp.sqrt(energy + 1e-06)
    return (values * weights[:, :, None]).astype(jnp.bfloat16)


def cross_spectra(sources, receivers):
    bins = sources.shape[-1] // 2
    sr = sources[:, None, :, :bins].astype(jnp.float32)
    si = sources[:, None, :, bins:].astype(jnp.float32)
    rr = receivers[:, :, None, :bins].astype(jnp.float32)
    ri = receivers[:, :, None, bins:].astype(jnp.float32)
    real_part = jnp.sum(sr * rr + si * ri, axis=0)
    imag_part = jnp.sum(sr * ri - si * rr, axis=0)
    return real_part, imag_part


def greet(axis, n, me):
    barrier = pltpu.get_barrier_semaphore()
    for k in range(1, n):
        pl.semaphore_signal(barrier, inc=1, device_id={axis: (me + k) % n},
                            device_id_type=pl.DeviceIdType.MESH)
    pl.semaphore_wait(barrier, n - 1)


def all_to_all(axis, n, me, rows_of, landing, send_sem, recv_sem):
    copies = []
    for k in range(1, n):
        peer = (me + k) % n
        copy = pltpu.make_async_remote_copy(
            src_ref=rows_of(peer), dst_ref=landing.at[me], send_sem=send_sem.at[k],
            recv_sem=recv_sem.at[me], device_id={axis: peer},
            device_id_type=pl.DeviceIdType.MESH)
        copy.start()
        copies.append(copy)
    for copy in copies:
        copy.wait_send()
    for k in range(1, n):
        source = (me + n - k) % n
        pltpu.make_async_remote_copy(
            src_ref=landing.at[source], dst_ref=landing.at[source], send_sem=send_sem.at[k],
            recv_sem=recv_sem.at[source], device_id={axis: source},
            device_id_type=pl.DeviceIdType.MESH).wait_recv()


def broadcast_kernel(axis, n, x_ref, o_ref, parts, mine, gathered, sems):
    me = lax.axis_index(axis)
    width = x_ref.shape[1] // n

    def columns(peer):
        return x_ref.at[:, pl.ds(pl.multiple_of(peer * width, width), width)]

    parts[me] = columns(me)[...]
    greet(axis, n, me)
    all_to_all(axis, n, me, columns, parts, sems.at[0], sems.at[1])
    mine[...] = jnp.sum(parts[...].astype(jnp.float32), axis=0).astype(mine.dtype)
    gathered[me] = mine[...]
    all_to_all(axis, n, me, lambda peer: mine, gathered, sems.at[2], sems.at[3])
    for peer in range(n):
        o_ref[:, peer * width:(peer + 1) * width] = gathered[peer]


def reduce_kernel(axis, n, x_ref, o_ref, parts, sems, own_sem):
    me = lax.axis_index(axis)
    height = x_ref.shape[0] // n

    def rows(peer):
        return x_ref.at[pl.ds(pl.multiple_of(peer * height, height), height)]

    own = pltpu.make_async_copy(rows(me), parts.at[me], own_sem.at[0])
    own.start()
    greet(axis, n, me)
    all_to_all(axis, n, me, rows, parts, sems.at[0], sems.at[1])
    own.wait()
    total = jnp.sum(parts[...], axis=0).reshape(o_ref.shape)
    o_ref[...] = total.astype(o_ref.dtype)


def broadcast_sum(value, axis):
    n = lax.axis_size(axis)
    chunk = (value.shape[0], value.shape[1] // n)
    return pl.pallas_call(
        functools.partial(broadcast_kernel, axis, n),
        out_shape=jax.ShapeDtypeStruct(value.shape, value.dtype),
        in_specs=[pl.BlockSpec(memory_space=pltpu.VMEM)],
        out_specs=pl.BlockSpec(memory_space=pltpu.VMEM),
        scratch_shapes=[pltpu.VMEM((n,) + chunk, value.dtype), pltpu.VMEM(chunk, value.dtype),
                        pltpu.VMEM((n,) + chunk, value.dtype), pltpu.SemaphoreType.DMA((4, n))],
        compiler_params=pltpu.CompilerParams(collective_id=0, has_side_effects=True),
    )(value)


def start_all_to_all(axis, n, rows_of, landing, send_sem, recv_sem):
    me = lax.axis_index(axis)
    copies = []
    for k in range(1, n):
        peer = (me + k) % n
        copy = pltpu.make_async_remote_copy(
            src_ref=rows_of(peer), dst_ref=landing.at[me], send_sem=send_sem.at[k],
            recv_sem=recv_sem.at[me], device_id={axis: peer},
            device_id_type=pl.DeviceIdType.MESH)
        copy.start()
        copies.append(copy)

    def wait():
        for copy in copies:
            copy.wait_send()
        for k in range(1, n):
            source = (me + n - k) % n
            pltpu.make_async_remote_copy(
                src_ref=landing.at[source], dst_ref=landing.at[source], send_sem=send_sem.at[k],
                recv_sem=recv_sem.at[source], device_id={axis: source},
                device_id_type=pl.DeviceIdType.MESH).wait_recv()

    return wait


def columns_of(ref, n):
    width = ref.shape[1] // n
    return lambda peer: ref.at[:, pl.ds(pl.multiple_of(peer * width, width), width)]


def whiten_broadcast_kernel(axis, n, per_group, spec_ref, q_ref, sb_ref, o_ref, w_ref,
                            send, parts, mine, gathered, sems):
    me = lax.axis_index(axis)
    windows, channels, width = spec_ref.shape
    bins = width // 2
    steps = sb_ref.shape[0]

    channel = lax.broadcasted_iota(jnp.int32, (channels, 1), 0)
    quality = jnp.zeros((channels, 1), jnp.float32)
    for c in range(channels):
        quality = jnp.where(channel == c, q_ref[c].astype(jnp.float32), quality)

    def weighted(w):
        values = spec_ref[w].astype(jnp.float32)
        energy = jnp.sum(values * values, axis=-1, keepdims=True) / bins
        return values * (quality / jnp.sqrt(energy + 1e-06))

    barrier = pltpu.get_barrier_semaphore()
    for k in range(1, n):
        pl.semaphore_signal(barrier, inc=1, device_id={axis: (me + k) % n},
                            device_id_type=pl.DeviceIdType.MESH)
    for w in range(windows):
        block = weighted(w)
        for k in range(steps):
            kept = jnp.zeros((SRC, width), jnp.float32)
            for b in range(per_group):
                hit = me * per_group + b == sb_ref[k]
                kept = kept + jnp.where(hit, block[b * SRC:(b + 1) * SRC], 0.0)
            row = (k * windows + w) * SRC
            send[row:row + SRC, :] = kept.astype(send.dtype)
    pl.semaphore_wait(barrier, n - 1)
    columns = columns_of(send, n)
    parts[me] = columns(me)[...]
    wait = start_all_to_all(axis, n, columns, parts, sems.at[0], sems.at[1])
    for w in range(windows):
        w_ref[w] = weighted(w).astype(w_ref.dtype)
    wait()
    mine[...] = jnp.sum(parts[...].astype(jnp.float32), axis=0).astype(mine.dtype)
    gathered[me] = mine[...]
    wait = start_all_to_all(axis, n, lambda peer: mine, gathered, sems.at[2], sems.at[3])
    wait()
    piece = mine.shape[1]
    for peer in range(n):
        o_ref[:, peer * piece:(peer + 1) * piece] = gathered[peer]


def whiten_broadcast(spectra, quality, source_block, axis):
    n = lax.axis_size(axis)
    windows, channels, width = spectra.shape
    rows = source_block.shape[0] * windows * SRC
    chunk = (rows, width // n)
    vmem = pl.BlockSpec(memory_space=pltpu.VMEM)
    return pl.pallas_call(
        functools.partial(whiten_broadcast_kernel, axis, n, channels // SRC),
        out_shape=(jax.ShapeDtypeStruct((rows, width), jnp.bfloat16),
                   jax.ShapeDtypeStruct(spectra.shape, jnp.bfloat16)),
        in_specs=[vmem, pl.BlockSpec(memory_space=pltpu.SMEM), pl.BlockSpec(memory_space=pltpu.SMEM)],
        out_specs=(vmem, vmem),
        scratch_shapes=[pltpu.VMEM((rows, width), jnp.bfloat16),
                        pltpu.VMEM((n,) + chunk, jnp.bfloat16), pltpu.VMEM(chunk, jnp.bfloat16),
                        pltpu.VMEM((n,) + chunk, jnp.bfloat16), pltpu.SemaphoreType.DMA((4, n))],
        compiler_params=pltpu.CompilerParams(collective_id=0, has_side_effects=True),
    )(spectra, quality, source_block)


def scatter_sum(rows, axis, shape, dtype):
    n = lax.axis_size(axis)
    chunk = (rows.shape[0] // n, rows.shape[1])
    return pl.pallas_call(
        functools.partial(reduce_kernel, axis, n),
        out_shape=jax.ShapeDtypeStruct(shape, dtype),
        in_specs=[pl.BlockSpec(memory_space=pl.ANY)],
        out_specs=pl.BlockSpec(memory_space=pltpu.VMEM),
        scratch_shapes=[pltpu.VMEM((n,) + chunk, rows.dtype), pltpu.SemaphoreType.DMA((2, n)),
                        pltpu.SemaphoreType.DMA((1,))],
        compiler_params=pltpu.CompilerParams(collective_id=1, has_side_effects=True),
    )(rows)


def body(spectra, quality, source_block):
    window_count, channel_count, row_width = spectra.shape
    bins = row_width // 2
    total_windows = window_count * lax.axis_size("win")
    cos_t, sin_t = lag_table(bins, L, 1.0 / math.sqrt(row_width * total_windows))
    sources, whitened = whiten_broadcast(spectra, quality, source_block, "chan")
    sources = sources.reshape(STEPS, window_count, SRC, row_width)
    win_size = lax.axis_size("win")
    per_dest = channel_count // win_size
    reals, imags = [], []
    for step in range(STEPS):
        real_part, imag_part = cross_spectra(sources[step], whitened)
        reals.append(real_part.reshape(win_size, per_dest, SRC, bins))
        imags.append(imag_part.reshape(win_size, per_dest, SRC, bins))
    rows = channel_count * SRC * STEPS
    real_rows = jnp.stack(reals, axis=1).reshape(rows, bins)
    imag_rows = jnp.stack(imags, axis=1).reshape(rows, bins)
    out = jnp.dot(
        real_rows, cos_t, precision=lax.Precision.HIGH, preferred_element_type=jnp.float32
    )
    out = out + jnp.dot(
        imag_rows, sin_t, precision=lax.Precision.HIGH, preferred_element_type=jnp.float32
    )
    return scatter_sum(out, "win", (STEPS, per_dest, SRC, L), jnp.bfloat16)


def solution(mesh):
    return jax.shard_map(
        body,
        mesh=mesh,
        in_specs=(P("win", "chan", None), P("chan"), P()),
        out_specs=P(None, ("chan", "win"), None, None),
        check_vma=False,
    )
```
